32 devices in a mesh: dp: 4 (over y, x), expert: 8 (over z, core).
Axes of the slice: x: 2, y: 2, z: 4, core: 2. Of those that a mesh axis runs over, the one named last changes fastest.
Arguments:
- hidden_in: bfloat16 [4096, 2048], P(('dp', 'expert')), may hold values from -6 to 6
- out_grad: bfloat16 [4096, 2048], P(('dp', 'expert')), may hold values from -6 to 6
- lengths: int32 [4, 5], P('dp'), may hold values from 1 to 512, 1024 in all within a row
- routes: int32 [4096, 4], P(('dp', 'expert')), may hold values from 0 to 7, all different within a row; in each aligned block of 128 rows (0 to 127, 128 to 255, ...) at most 128 rows name the same one
- norm1_gain: bfloat16 [2048], P(('dp', 'expert')), may hold values from 0.5 to 1.5
- qkv_weight: bfloat16 [2048, 6144], P(('dp', 'expert')), may hold values from -0.125 to 0.125
- qkv_bias: bfloat16 [6144], P(('dp', 'expert')), may hold values from -0.625 to 0.625
- out_weight: bfloat16 [2048, 2048], P(('dp', 'expert')), may hold values from -1 to 1
- norm2_gain: bfloat16 [2048], P(('dp', 'expert')), may hold values from 0.5 to 1.5
- router_weight: bfloat16 [2048, 8], P(('dp', 'expert')), may hold values from -0.0625 to 0.0625
- shared_gate: bfloat16 [2048], P(('dp', 'expert')), may hold values from -0.125 to 0.125
- shared_in: bfloat16 [2048, 11264], P(('dp', 'expert')), may hold values from -0.125 to 0.125
- shared_out: bfloat16 [5632, 2048], P(('dp', 'expert')), may hold values from -0.15625 to 0.15625
- expert_in: bfloat16 [8, 2048, 2816], P('expert', 'dp'), may hold values from -0.125 to 0.125
- expert_out: bfloat16 [8, 1408, 2048], P('expert', 'dp'), may hold values from -0.5 to 0.5
Outputs:
- output: bfloat16 [4096, 2048], P(('dp', 'expert'))
- input_grad: bfloat16 [4096, 2048], P(('dp', 'expert'))
- grad_norm1: float32 [2048], P(('dp', 'expert'))
- grad_qkv: float32 [2048, 6144], P(('dp', 'expert'))
- grad_bias: float32 [6144], P(('dp', 'expert'))
- grad_out_weight: float32 [2048, 2048], P(('dp', 'expert'))
- grad_norm2: float32 [2048], P(('dp', 'expert'))
- grad_router: float32 [2048, 8], P(('dp', 'expert'))
- grad_shared_gate: float32 [2048], P(('dp', 'expert'))
- grad_shared_in: float32 [2048, 11264], P(('dp', 'expert'))
- grad_shared_out: float32 [5632, 2048], P(('dp', 'expert'))
- grad_expert_in: float32 [8, 2048, 2816], P('expert', 'dp')
- grad_expert_out: float32 [8, 1408, 2048], P('expert', 'dp')
The draws below stay inside these ranges and needn't reach their ends.
Inputs may be any that keep to these rules, and one draw needn't show every extreme that they name: `routes`: each row names 4 different experts. Among the 128 rows of one device, no expert is named more than 128 times, a bound that some block reaches. Row g belongs to data group g and sums to 1024: its first 4 entries are the group's sequence lengths in order, the last is the padding after them. Some entry equals 512.
All inputs are finite; a program needn't handle non-finite values.
Results may differ from the reference program's by a relative error of at most 0.015.
Values may be sent and summed in bfloat16 or wider, within the bound.
A program may use at most 448 MiB of HBM per device.

```python
import math
import jax
import jax.numpy as jnp
import numpy as np
from jax import lax

D = 2048
HD = 128
FFE = 1408
SH = 5632
TOP = 4
TOK_DEV = 128
SEQS = 4
EXPERTS = 8
GROUP_TOK = 1024
TOKENS = 4096
MAXLEN = 512
CAP = 128
N_DP = 4


def block_levels(own_key, dims, pieces, least, largest):
    def one(dim, blocks):
        draws = jax.random.uniform(jax.random.fold_in(jax.random.fold_in(own_key, 6), dim), (blocks,), jnp.float32, least / len(pieces), largest / len(pieces))
        return jnp.repeat(jnp.exp(draws), dims[dim] // blocks).reshape((-1,) + (1,) * (len(dims) - dim - 1))

    level = one(*pieces[0])
    for cut in pieces[1:]:
        level = level * one(*cut)
    return level


def length_profile(count, total, bound, slope):
    weights = [(1 << 20) // math.isqrt(grade ** slope) + 1 for grade in range(2, count + 1)]
    surplus, counts = total - bound - (count - 1), [1] * (count - 1)
    while surplus > 0:
        free = [i for i in range(count - 1) if counts[i] < bound]
        whole, left = sum([weights[i] for i in free]), surplus
        for i in free:
            addition = min(bound - counts[i], max(1, left * weights[i] // whole), surplus)
            counts[i] = counts[i] + addition
            surplus = surplus - addition
    return np.array([bound] + counts)


def ragged_sizes(rng, count, total, bound, skew):
    if count == 2:
        one = jax.random.randint(rng, (), max(1, total - bound), min(bound, total - 1) + 1)
        return jnp.stack([one, total - one])
    tallies = jnp.asarray(length_profile(count, total, bound, skew), jnp.int32)
    twos = (count - 1) // 2
    giver, taker = tallies[1:1 + 2 * twos:2], tallies[2:2 + 2 * twos:2]
    room = jnp.minimum(giver - 1, bound - taker)
    shifted = jax.random.randint(jax.random.fold_in(rng, 1), (twos,), 0, 1 << 20) % (room + 1)
    tallies = tallies.at[1:1 + 2 * twos:2].set(giver - shifted).at[2:2 + 2 * twos:2].set(taker + shifted)
    return tallies[jax.random.permutation(jax.random.fold_in(rng, 2), count)]


def routed_block(rng, own, number, rows, amount, top, reach, skew):
    sequence = jax.random.permutation(rng, amount)
    crowded, usual = load_shares(amount, rows * top, reach, skew, True), load_shares(amount, rows * top, reach, skew, False)
    places = jnp.arange(amount)

    def named(sizes, turn):
        used = int((sizes > 0).sum())
        fixed = max(1, used // 4)
        moved = fixed + (places - fixed + turn * (used - fixed)) % max(1, amount - fixed)
        return jnp.zeros((amount,), jnp.int32).at[sequence[jnp.where(places < fixed, places, moved)]].set(jnp.asarray(sizes, jnp.int32))

    sizes = jnp.where(number % 4 == 0, named(crowded, number // 4), named(usual, number - number // 4 - 1))
    mixed = jax.random.permutation(jax.random.fold_in(own, 3), amount)
    giver, receiver = mixed[0:amount // 2 * 2:2], mixed[1:amount // 2 * 2:2]
    slack = jnp.minimum(sizes[giver] - 1, reach - sizes[receiver]) // 2
    slack = jnp.where((giver == sequence[0]) | (receiver == sequence[0]) | (sizes[receiver] == 0), 0, jnp.maximum(slack, 0))
    moved = jax.random.randint(jax.random.fold_in(own, 4), (amount // 2,), 0, 1 << 20) % (slack + 1)
    sizes = sizes.at[giver].add(-moved).at[receiver].add(moved)
    items = jnp.searchsorted(jnp.cumsum(sizes), jnp.arange(rows * top), side="right").astype(jnp.int32)
    grid = items.reshape(top, rows).T
    grid = grid[jax.random.permutation(jax.random.fold_in(own, 1), rows)]
    turn = jax.random.randint(jax.random.fold_in(own, 2), (rows, 1), 0, top)
    return jnp.take_along_axis(grid, (jnp.arange(top)[None, :] + turn) % top, axis=1)


def load_shares(number_of, total, limit, skew, full):
    portions = [(1 << 20) // math.isqrt(rank ** skew) + 1 for rank in range(1, number_of + 1)]
    largest = limit if full else min(limit, max(-(-total // number_of), total * portions[0] // sum(portions)))
    least = 1 if total - largest >= number_of - 1 else 0
    holding, rest = [largest] + [least] * (number_of - 1), total - largest - least * (number_of - 1)
    while rest > 0:
        free = [i for i in range(1, number_of) if holding[i] < largest] or [i for i in range(1, number_of) if holding[i] < limit]
        whole, budget = sum([portions[i] for i in free]), rest
        for i in free:
            more = min(limit - holding[i], max(1, budget * portions[i] // whole), rest)
            holding[i] = holding[i] + more
            rest = rest - more
    return np.array(holding)


def centred(stream_key, dims, scale, limit, cuts=(), kind=jnp.bfloat16):
    entries = jax.random.normal(stream_key, dims, jnp.float32) * scale
    if len(cuts) > 0:
        entries = block_levels(stream_key, dims, cuts, -0.22, 0.18) * entries
    return jnp.clip(entries, min=-limit, max=limit).astype(kind)


def setup_inputs(seed: int = 0) -> dict:
    key_of = jax.random.split(jax.random.key(seed), 16)
    hidden_in = centred(key_of[0], (TOKENS, D), 1.0, 6.0, ((0, 32),))
    out_grad = centred(key_of[1], (TOKENS, D), 1.0, 6.0, ((0, 32),))
    lengths = jax.vmap(lambda own: ragged_sizes(own, SEQS + 1, GROUP_TOK, MAXLEN, 1))(jax.random.split(key_of[2], N_DP)).reshape((N_DP, SEQS + 1)).astype(jnp.int32)
    routes_keys = jax.random.split(jax.random.fold_in(key_of[3], 1), TOKENS // TOK_DEV)
    routes_turns = jax.random.permutation(jax.random.fold_in(key_of[3], 3), TOKENS // TOK_DEV)
    routes = jax.vmap(lambda own, number: routed_block(jax.random.fold_in(key_of[3], 2), own, number, TOK_DEV, EXPERTS, TOP, CAP, 1))(routes_keys, routes_turns).reshape((TOKENS, TOP))
    norm1_gain = jnp.clip(1.0 + 0.1 * jax.random.normal(key_of[4], (D,), jnp.float32), 0.5, 1.5).astype(jnp.bfloat16)
    qkv_weight = centred(key_of[5], (D, 3 * D), D ** -0.5, 0.125, ((0, 32),))
    qkv_bias = centred(key_of[6], (3 * D,), 0.1, 0.625, ((0, 32),))
    out_weight = centred(key_of[7], (D, D), (D // 64) ** -0.5, 1.0, ((0, 32),))
    norm2_gain = jnp.clip(1.0 + 0.1 * jax.random.normal(key_of[8], (D,), jnp.float32), 0.5, 1.5).astype(jnp.bfloat16)
    router_weight = centred(key_of[9], (D, EXPERTS), 0.011, 0.0625, ((0, 32),))
    shared_gate = centred(key_of[10], (D,), 0.022, 0.125, ((0, 32),))
    shared_in = centred(key_of[11], (D, 2 * SH), D ** -0.5, 0.125, ((0, 32),))
    shared_out = centred(key_of[12], (SH, D), (SH // 4) ** -0.5, 0.15625, ((0, 32),))
    expert_in = centred(key_of[13], (EXPERTS, D, 2 * FFE), D ** -0.5, 0.125, ((0, 8), (1, 4)))
    expert_out = centred(key_of[14], (EXPERTS, FFE, D), (max(1, FFE * TOP * TOP // (3 * EXPERTS * EXPERTS))) ** -0.5, 0.5, ((0, 8), (1, 4)))
    return {"hidden_in": hidden_in, "out_grad": out_grad, "lengths": lengths, "routes": routes, "norm1_gain": norm1_gain, "qkv_weight": qkv_weight, "qkv_bias": qkv_bias, "out_weight": out_weight, "norm2_gain": norm2_gain, "router_weight": router_weight, "shared_gate": shared_gate, "shared_in": shared_in, "shared_out": shared_out, "expert_in": expert_in, "expert_out": expert_out}


EPSILON = 1e-06
THETA = 1000000.0
NEG_FILL = -1e+30

@jax.custom_vjp
def low(v):
    return lax.optimization_barrier(v.astype(jnp.bfloat16)).astype(jnp.float32)

@jax.custom_vjp
def low_back(v):
    return v

def low_keep(v):
    return (low(v), None)

def low_pass(kept, grad):
    return (grad,)

def back_keep(v):
    return (v, None)

def back_low(kept, grad):
    return (low(grad),)
low.defvjp(low_keep, low_pass)
low_back.defvjp(back_keep, back_low)

def rms_scale(values):
    return lax.rsqrt(lax.optimization_barrier(jnp.mean(values * values, axis=-1, keepdims=True)) + EPSILON)

def rotary_tables(positions, head_size):
    half_size = head_size // 2
    steps_up = jnp.arange(half_size, dtype=jnp.float32) * (2.0 / head_size)
    inverse = THETA ** (-steps_up)
    angles = positions.astype(jnp.float32)[:, None] * inverse[None, :]
    angles = jnp.concatenate([angles, angles], axis=-1)
    return (jnp.cos(angles)[:, None, :], jnp.sin(angles)[:, None, :])

def rotate(values, cosine, sine):
    half_size = values.shape[-1] // 2
    turned = jnp.concatenate([-values[..., half_size:], values[..., :half_size]], axis=-1)
    return values * cosine + turned * sine

def swiglu(gate_up):
    half_size = gate_up.shape[-1] // 2
    return jax.nn.silu(gate_up[..., :half_size]) * gate_up[..., half_size:]

def segment_table(length_row, count):
    ends = jnp.cumsum(length_row, dtype=jnp.int32)
    starts = ends - length_row
    places = jnp.arange(count, dtype=jnp.int32)
    segment = lax.optimization_barrier(jnp.sum((places[:, None] >= ends[None, :-1]).astype(jnp.int32), axis=1, dtype=jnp.int32))
    owners = segment[:, None] == jnp.arange(length_row.shape[0], dtype=jnp.int32)[None, :]
    first = lax.optimization_barrier(jnp.sum(jnp.where(owners, starts[None, :], 0), axis=1, dtype=jnp.int32))
    return (segment, places - first)

def reference(hidden_in, out_grad, lengths, routes, norm1_gain, qkv_weight, qkv_bias, out_weight, norm2_gain, router_weight, shared_gate, shared_in, shared_out, expert_in, expert_out):
    highest = lax.Precision.HIGHEST
    token_count, model_width = hidden_in.shape
    head_count = model_width // HD
    group_count = token_count // GROUP_TOK
    block_count = token_count // TOK_DEV
    expert_count = router_weight.shape[1]
    top_count = routes.shape[1]
    score_scale = HD ** (-0.5)
    query_rows = min(512, GROUP_TOK)
    query_blocks = token_count // query_rows
    segment_parts = []
    position_parts = []
    for group_index in range(group_count):
        segment_part, position_part = segment_table(lengths[group_index], GROUP_TOK)
        segment_parts.append(segment_part)
        position_parts.append(position_part)
    segment_flat = jnp.concatenate(segment_parts)
    position_flat = jnp.concatenate(position_parts)
    valid_rows = (segment_flat < SEQS).astype(jnp.float32)[:, None]
    cosine, sine = rotary_tables(position_flat, HD)
    block_routes = routes.reshape(block_count, TOK_DEV * top_count)
    expert_ids = jnp.arange(expert_count, dtype=jnp.int32)
    chosen = (block_routes[:, :, None] == expert_ids[None, None, :]).astype(jnp.int32)
    earlier = jnp.cumsum(chosen, axis=1, dtype=jnp.int32) - chosen
    slot_rank = lax.optimization_barrier(jnp.sum(earlier * chosen, axis=2, dtype=jnp.int32))
    slot_of = block_routes * CAP + slot_rank
    owner_token = jnp.broadcast_to(jnp.arange(TOK_DEV * top_count, dtype=jnp.int32) // top_count, slot_of.shape)
    block_ids = jnp.broadcast_to(jnp.arange(block_count, dtype=jnp.int32)[:, None], slot_of.shape)
    slot_token = jnp.full((block_count, expert_count * CAP), TOK_DEV, jnp.int32).at[block_ids, slot_of].set(owner_token)

    def forward(inputs, gain_one, weight_qkv, bias_qkv, weight_out, gain_two, weight_router, weight_gate, weight_shared_in, weight_shared_out, weight_expert_in, weight_expert_out):
        normed_one = low(inputs * rms_scale(inputs) * gain_one)
        projected = low_back(jnp.dot(normed_one, weight_qkv, precision=highest) + bias_qkv)
        query_low = low(rotate(projected[:, :model_width].reshape(token_count, head_count, HD), cosine, sine))
        key_low = low(rotate(projected[:, model_width:2 * model_width].reshape(token_count, head_count, HD), cosine, sine))
        value_low = low(projected[:, 2 * model_width:].reshape(token_count, head_count, HD))

        def attend_block(packed):
            query_block, start = packed
            group_start = start // GROUP_TOK * GROUP_TOK
            key_group = lax.dynamic_slice_in_dim(key_low, group_start, GROUP_TOK, 0)
            value_group = lax.dynamic_slice_in_dim(value_low, group_start, GROUP_TOK, 0)
            segment_group = lax.dynamic_slice_in_dim(segment_flat, group_start, GROUP_TOK, 0)
            position_group = lax.dynamic_slice_in_dim(position_flat, group_start, GROUP_TOK, 0)
            segment_block = lax.dynamic_slice_in_dim(segment_flat, start, query_rows, 0)
            position_block = lax.dynamic_slice_in_dim(position_flat, start, query_rows, 0)
            raw = jnp.einsum('qhd,khd->hqk', query_block, key_group, precision=highest) * score_scale
            allowed = (segment_block[:, None] == segment_group[None, :]) & (position_block[:, None] >= position_group[None, :])
            scores = low_back(jnp.where(allowed[None], raw, NEG_FILL))
            peak = lax.optimization_barrier(jnp.max(scores, axis=-1, keepdims=True))
            log_total = peak + jnp.log(lax.optimization_barrier(jnp.sum(jnp.exp(scores - peak), axis=-1, keepdims=True)))
            weights_low = low(jnp.exp(scores - log_total))
            return jnp.einsum('hqk,khd->qhd', weights_low, value_group, precision=highest)
        block_starts = jnp.arange(query_blocks, dtype=jnp.int32) * query_rows
        attended = lax.map(jax.checkpoint(attend_block), (query_low.reshape(query_blocks, query_rows, head_count, HD), block_starts))
        attended = low(low_back(attended.reshape(token_count, model_width)))
        middle = inputs + low_back(jnp.dot(attended, weight_out, precision=highest))
        normed_two = low(middle * rms_scale(middle) * gain_two)
        logits = low_back(jnp.dot(normed_two, weight_router, precision=highest))
        gate_logit = low_back(jnp.dot(normed_two, weight_gate, precision=highest))
        peak_logit = lax.optimization_barrier(jnp.max(logits, axis=-1, keepdims=True))
        router_total = peak_logit + jnp.log(lax.optimization_barrier(jnp.sum(jnp.exp(logits - peak_logit), axis=-1, keepdims=True)))
        router_probs = jnp.exp(logits - router_total)
        gates = jnp.take_along_axis(router_probs, routes, axis=1)
        padded = jnp.concatenate([normed_two.reshape(block_count, TOK_DEV, model_width), jnp.zeros((block_count, 1, model_width), jnp.float32)], axis=1)
        gathered = jnp.take_along_axis(padded, slot_token[:, :, None], axis=1)
        per_expert = gathered.reshape(block_count, expert_count, CAP, model_width).transpose(1, 0, 2, 3).reshape(expert_count, block_count * CAP, model_width)

        def run_expert(packed):
            rows_in, weight_first, weight_second = packed
            gate_up = low_back(jnp.dot(rows_in, weight_first, precision=highest))
            return low(low_back(jnp.dot(low(swiglu(gate_up)), weight_second, precision=highest)))
        expert_rows = lax.map(jax.checkpoint(run_expert), (per_expert, weight_expert_in, weight_expert_out))
        returned = expert_rows.reshape(expert_count, block_count, CAP, model_width).transpose(1, 0, 2, 3).reshape(block_count, expert_count * CAP, model_width)
        picked = jnp.take_along_axis(returned, slot_of[:, :, None], axis=1).reshape(token_count, top_count, model_width)
        routed = lax.optimization_barrier(jnp.sum(gates[:, :, None] * picked, axis=1))
        shared_up = low_back(jnp.dot(normed_two, weight_shared_in, precision=highest))
        shared_rows = low_back(jnp.dot(low(swiglu(shared_up)), weight_shared_out, precision=highest))
        opener = jax.nn.sigmoid(gate_logit)[:, None]
        return valid_rows * (middle + routed + opener * shared_rows)
    primals = [weight.astype(jnp.float32) for weight in (hidden_in, norm1_gain, qkv_weight, qkv_bias, out_weight, norm2_gain, router_weight, shared_gate, shared_in, shared_out, expert_in, expert_out)]
    outcome, pullback = jax.vjp(forward, *primals)
    gradients = pullback(out_grad.astype(jnp.float32))
    return (outcome.astype(jnp.bfloat16), gradients[0].astype(jnp.bfloat16), gradients[1], gradients[2], gradients[3], gradients[4], gradients[5], gradients[6], gradients[7], gradients[8], gradients[9], gradients[10], gradients[11])
```

```python
import jax
import jax.numpy as jnp
from jax import lax
from jax.sharding import PartitionSpec as P

HD = 128


EPSILON = 1e-06
THETA = 1000000.0
NEG_FILL = -1e30


def rms_scale(values):
    return lax.rsqrt(jnp.mean(values * values, axis=-1, keepdims=True) + EPSILON)


def rotary_tables(positions, head_size):
    half_size = head_size // 2
    steps_up = jnp.arange(half_size, dtype=jnp.float32) * (2.0 / head_size)
    inverse = THETA ** (-steps_up)
    angles = positions.astype(jnp.float32)[:, None] * inverse[None, :]
    angles = jnp.concatenate([angles, angles], axis=-1)
    return (jnp.cos(angles)[:, None, :], jnp.sin(angles)[:, None, :])


def rotate(values, cosine, sine):
    half_size = values.shape[-1] // 2
    turned = jnp.concatenate([-values[..., half_size:], values[..., :half_size]], axis=-1)
    return values * cosine + turned * sine


def rotate_back(grad_values, cosine, sine):
    half_size = grad_values.shape[-1] // 2
    scaled = grad_values * sine
    turned = jnp.concatenate([scaled[..., half_size:], -scaled[..., :half_size]], axis=-1)
    return grad_values * cosine + turned


def swiglu(gate_up):
    half_size = gate_up.shape[-1] // 2
    return jax.nn.silu(gate_up[..., :half_size]) * gate_up[..., half_size:]


def swiglu_back(gate_up, grad_hidden):
    half_size = gate_up.shape[-1] // 2
    gate_part = gate_up[..., :half_size]
    up_part = gate_up[..., half_size:]
    sigmoid_gate = jax.nn.sigmoid(gate_part)
    grad_gate = grad_hidden * up_part * sigmoid_gate * (1.0 + gate_part * (1.0 - sigmoid_gate))
    grad_up = grad_hidden * gate_part * sigmoid_gate
    return jnp.concatenate([grad_gate, grad_up], axis=-1)


def norm_back(values, scale_rows, gain, grad_normed):
    weighted = grad_normed * gain
    inner = jnp.mean(weighted * values, axis=-1, keepdims=True)
    grad_values = scale_rows * weighted - values * scale_rows * scale_rows * scale_rows * inner
    grad_gain = jnp.sum(grad_normed * values * scale_rows, axis=0)
    return (grad_values, grad_gain)


def segment_table(length_row, count):
    ends = jnp.cumsum(length_row, dtype=jnp.int32)
    starts = ends - length_row
    places = jnp.arange(count, dtype=jnp.int32)
    segment = jnp.sum(
        (places[:, None] >= ends[None, :-1]).astype(jnp.int32), axis=1, dtype=jnp.int32
    )
    owners = segment[:, None] == jnp.arange(length_row.shape[0], dtype=jnp.int32)[None, :]
    first = jnp.sum(jnp.where(owners, starts[None, :], 0), axis=1, dtype=jnp.int32)
    return (segment, places - first)


def per_device(
    hidden_in,
    out_grad,
    lengths,
    routes,
    norm1_gain,
    qkv_weight,
    qkv_bias,
    out_weight,
    norm2_gain,
    router_weight,
    shared_gate,
    shared_in,
    shared_out,
    expert_in,
    expert_out,
):
    highest = lax.Precision.HIGHEST
    row_count, model_width = hidden_in.shape
    head_count = model_width // HD
    group_size = lax.axis_size("expert")
    group_rows = row_count * group_size
    top_count = routes.shape[1]
    expert_count = router_weight.shape[1]
    local_count = expert_in.shape[0]
    capacity = max(2, 2 * row_count * top_count // expert_count)
    slot_count = expert_count * capacity
    score_scale = HD ** (-0.5)
    dense = (
        lax.all_gather(norm1_gain, ("dp", "expert"), axis=0, tiled=True),
        lax.all_gather(qkv_weight, ("dp", "expert"), axis=0, tiled=True),
        lax.all_gather(qkv_bias, ("dp", "expert"), axis=0, tiled=True),
        lax.all_gather(out_weight, ("dp", "expert"), axis=0, tiled=True),
        lax.all_gather(norm2_gain, ("dp", "expert"), axis=0, tiled=True),
        lax.all_gather(router_weight, ("dp", "expert"), axis=0, tiled=True),
        lax.all_gather(shared_gate, ("dp", "expert"), axis=0, tiled=True),
        lax.all_gather(shared_in, ("dp", "expert"), axis=0, tiled=True),
        lax.all_gather(shared_out, ("dp", "expert"), axis=0, tiled=True),
    )
    (
        gain_first,
        weight_qkv,
        bias_first,
        weight_out,
        gain_second,
        weight_router,
        weight_gate,
        weight_shared_in,
        weight_shared_out,
    ) = dense
    weight_expert_in, weight_expert_out = (
        lax.all_gather(expert_in, "dp", axis=1, tiled=True),
        lax.all_gather(expert_out, "dp", axis=1, tiled=True),
    )
    segment_all, position_all = segment_table(lengths[0], group_rows)
    first_row = lax.axis_index("expert") * row_count
    segment_mine = lax.dynamic_slice_in_dim(segment_all, first_row, row_count, 0)
    position_mine = lax.dynamic_slice_in_dim(position_all, first_row, row_count, 0)
    valid_rows = (segment_mine < lengths.shape[1] - 1).astype(jnp.float32)[:, None]
    cosine, sine = rotary_tables(position_mine, HD)
    allowed = (
        (segment_mine[:, None] == segment_all[None, :])
        & (position_mine[:, None] >= position_all[None, :])
    )[None]
    inputs = hidden_in.astype(jnp.float32)
    scale_first = rms_scale(inputs)
    gain_one = gain_first.astype(jnp.float32)
    normed_one = (inputs * scale_first * gain_one).astype(jnp.bfloat16)
    projected = jnp.dot(
        normed_one, weight_qkv, preferred_element_type=jnp.float32
    ) + bias_first.astype(jnp.float32)
    query_low = rotate(
        projected[:, :model_width].reshape(row_count, head_count, HD), cosine, sine
    ).astype(jnp.bfloat16)
    key_low = rotate(
        projected[:, model_width : 2 * model_width].reshape(row_count, head_count, HD), cosine, sine
    ).astype(jnp.bfloat16)
    value_low = (
        projected[:, 2 * model_width :].reshape(row_count, head_count, HD).astype(jnp.bfloat16)
    )
    keys_all, values_all = (
        lax.all_gather(key_low, "expert", axis=0, tiled=True),
        lax.all_gather(value_low, "expert", axis=0, tiled=True),
    )

    def score_rows(queries):
        raw = (
            jnp.einsum("qhd,khd->hqk", queries, keys_all, preferred_element_type=jnp.float32)
            * score_scale
        )
        return jnp.where(allowed, raw, NEG_FILL)

    scores = score_rows(query_low)
    peak = jnp.max(scores, axis=-1, keepdims=True)
    log_total = peak + jnp.log(jnp.sum(jnp.exp(scores - peak), axis=-1, keepdims=True))
    weights_low = jnp.exp(scores - log_total).astype(jnp.bfloat16)
    attended = (
        jnp.einsum("hqk,khd->qhd", weights_low, values_all, preferred_element_type=jnp.float32)
        .reshape(row_count, model_width)
        .astype(jnp.bfloat16)
    )
    middle = inputs + jnp.dot(attended, weight_out, preferred_element_type=jnp.float32)
    scale_second = rms_scale(middle)
    gain_two = gain_second.astype(jnp.float32)
    normed_two = (middle * scale_second * gain_two).astype(jnp.bfloat16)
    logits = jnp.dot(normed_two, weight_router, preferred_element_type=jnp.float32)
    gate_logit = jnp.dot(normed_two, weight_gate, preferred_element_type=jnp.float32)
    peak_logit = jnp.max(logits, axis=-1, keepdims=True)
    router_total = peak_logit + jnp.log(
        jnp.sum(jnp.exp(logits - peak_logit), axis=-1, keepdims=True)
    )
    router_probs = jnp.exp(logits - router_total)
    expert_ids = jnp.arange(expert_count, dtype=jnp.int32)
    chosen = routes[:, :, None] == expert_ids[None, None, :]
    chosen_float = chosen.astype(jnp.float32)
    gates = jnp.sum(chosen_float * router_probs[:, None, :], axis=2)
    flat_hits = chosen.reshape(row_count * top_count, expert_count).astype(jnp.int32)
    earlier = jnp.cumsum(flat_hits, axis=0, dtype=jnp.int32) - flat_hits
    slot_rank = jnp.sum(earlier * flat_hits, axis=1, dtype=jnp.int32)
    slot_of = routes.reshape(-1) * capacity + slot_rank
    slot_hits = (
        (slot_of[:, None] == jnp.arange(slot_count, dtype=jnp.int32)[None, :])
        .reshape(row_count, top_count, slot_count)
        .astype(jnp.float32)
    )
    placement_map = jnp.sum(slot_hits, axis=1)
    weighted_map = jnp.sum(slot_hits * gates[:, :, None], axis=1)
    send_rows = (
        jnp.einsum(
            "ts,td->sd",
            placement_map.astype(jnp.bfloat16),
            normed_two,
            preferred_element_type=jnp.float32,
        )
        .astype(jnp.bfloat16)
        .reshape(expert_count, capacity, model_width)
    )
    arrived = lax.all_to_all(send_rows, "expert", split_axis=0, concat_axis=0, tiled=True)
    item_count = arrived.shape[1]
    grouped = arrived.reshape(group_size, local_count, item_count, model_width)
    gate_up = jnp.einsum(
        "gecd,edf->gecf", grouped, weight_expert_in, preferred_element_type=jnp.float32
    )
    hidden_low = swiglu(gate_up).astype(jnp.bfloat16)
    produced = jnp.einsum(
        "gecf,efd->gecd", hidden_low, weight_expert_out, preferred_element_type=jnp.float32
    ).astype(jnp.bfloat16)
    produced_rows = produced.reshape(group_size * local_count, item_count, model_width)
    expert_gate_up = gate_up.reshape(group_size * local_count, item_count, gate_up.shape[-1])
    back_rows = lax.all_to_all(produced_rows, "expert", split_axis=0, concat_axis=0, tiled=True)
    back_float = back_rows.reshape(slot_count, model_width).astype(jnp.float32)
    routed = jnp.dot(weighted_map, back_float, precision=highest)
    shared_up = jnp.dot(normed_two, weight_shared_in, preferred_element_type=jnp.float32)
    shared_hidden = swiglu(shared_up).astype(jnp.bfloat16)
    shared_rows = jnp.dot(shared_hidden, weight_shared_out, preferred_element_type=jnp.float32)
    opener = jax.nn.sigmoid(gate_logit)[:, None]
    output = (valid_rows * (middle + routed + opener * shared_rows)).astype(jnp.bfloat16)
    held = (
        lax.all_gather(norm1_gain, ("dp", "expert"), axis=0, tiled=True),
        lax.all_gather(qkv_weight, ("dp", "expert"), axis=0, tiled=True),
        lax.all_gather(qkv_bias, ("dp", "expert"), axis=0, tiled=True),
        lax.all_gather(out_weight, ("dp", "expert"), axis=0, tiled=True),
        lax.all_gather(norm2_gain, ("dp", "expert"), axis=0, tiled=True),
        lax.all_gather(router_weight, ("dp", "expert"), axis=0, tiled=True),
        lax.all_gather(shared_gate, ("dp", "expert"), axis=0, tiled=True),
        lax.all_gather(shared_in, ("dp", "expert"), axis=0, tiled=True),
        lax.all_gather(shared_out, ("dp", "expert"), axis=0, tiled=True),
    )
    (
        gain_first,
        weight_qkv,
        bias_first,
        weight_out,
        gain_second,
        weight_router,
        weight_gate,
        weight_shared_in,
        weight_shared_out,
    ) = held
    gain_one = gain_first.astype(jnp.float32)
    gain_two = gain_second.astype(jnp.float32)
    grad_rows = out_grad.astype(jnp.float32) * valid_rows
    grad_shared_rows = (grad_rows * opener).astype(jnp.bfloat16)
    grad_gate_logit = (
        jnp.sum(grad_rows * shared_rows, axis=-1) * opener[:, 0] * (1.0 - opener[:, 0])
    ).astype(jnp.bfloat16)
    grad_shared_hidden = jnp.einsum(
        "td,fd->tf", grad_shared_rows, weight_shared_out, preferred_element_type=jnp.float32
    )
    grad_shared_up = swiglu_back(shared_up, grad_shared_hidden).astype(jnp.bfloat16)
    term_shared_out = jnp.einsum(
        "tf,td->fd", shared_hidden, grad_shared_rows, preferred_element_type=jnp.float32
    )
    term_shared_in = jnp.einsum(
        "td,tf->df", normed_two, grad_shared_up, preferred_element_type=jnp.float32
    )
    slot_product = jnp.einsum("td,sd->ts", grad_rows, back_float, precision=highest)
    grad_gates = jnp.sum(slot_hits * slot_product[:, None, :], axis=2)
    grad_probs = jnp.sum(chosen_float * grad_gates[:, :, None], axis=1)
    grad_logits = (
        router_probs * (grad_probs - jnp.sum(router_probs * grad_probs, axis=-1, keepdims=True))
    ).astype(jnp.bfloat16)
    term_router = jnp.einsum(
        "td,te->de", normed_two, grad_logits, preferred_element_type=jnp.float32
    )
    term_gate = jnp.einsum(
        "td,t->d", normed_two, grad_gate_logit, preferred_element_type=jnp.float32
    )
    grad_result = (
        jnp.einsum("ts,td->sd", weighted_map, grad_rows, precision=highest)
        .astype(jnp.bfloat16)
        .reshape(expert_count, capacity, model_width)
    )
    grad_arrived = lax.all_to_all(grad_result, "expert", split_axis=0, concat_axis=0, tiled=True)
    grad_grouped = grad_arrived.reshape(group_size, local_count, capacity, model_width)
    gate_up_grouped = expert_gate_up.reshape(
        group_size, local_count, capacity, expert_gate_up.shape[-1]
    )
    hidden_again = swiglu(gate_up_grouped).astype(jnp.bfloat16)
    grad_hidden = jnp.einsum(
        "gecd,efd->gecf", grad_grouped, weight_expert_out, preferred_element_type=jnp.float32
    )
    grad_gate_up = swiglu_back(gate_up_grouped, grad_hidden).astype(jnp.bfloat16)
    arrived_grouped = arrived.reshape(group_size, local_count, capacity, model_width)
    term_expert_in = jnp.einsum(
        "gecd,gecf->edf", arrived_grouped, grad_gate_up, preferred_element_type=jnp.float32
    )
    term_expert_out = jnp.einsum(
        "gecf,gecd->efd", hidden_again, grad_grouped, preferred_element_type=jnp.float32
    )
    grad_sent = jnp.einsum(
        "gecf,edf->gecd", grad_gate_up, weight_expert_in, preferred_element_type=jnp.float32
    ).reshape(group_size * local_count, capacity, model_width)
    grad_slots = lax.all_to_all(
        grad_sent.astype(jnp.bfloat16), "expert", split_axis=0, concat_axis=0, tiled=True
    ).astype(grad_sent.dtype)
    grad_expert_in, grad_expert_out = (
        lax.psum_scatter(
            term_expert_in.astype(jnp.bfloat16), "dp", scatter_dimension=1, tiled=True
        ).astype(jnp.float32),
        lax.psum_scatter(
            term_expert_out.astype(jnp.bfloat16), "dp", scatter_dimension=1, tiled=True
        ).astype(jnp.float32),
    )
    grad_normed_two = jnp.einsum(
        "te,de->td", grad_logits, weight_router, preferred_element_type=jnp.float32
    )
    grad_normed_two = (
        grad_normed_two
        + grad_gate_logit.astype(jnp.float32)[:, None] * weight_gate.astype(jnp.float32)[None, :]
    )
    grad_normed_two = grad_normed_two + jnp.einsum(
        "tf,df->td", grad_shared_up, weight_shared_in, preferred_element_type=jnp.float32
    )
    grad_normed_two = grad_normed_two + jnp.dot(
        placement_map, grad_slots.reshape(slot_count, model_width), precision=highest
    )
    grad_middle_norm, term_norm_two = norm_back(middle, scale_second, gain_two, grad_normed_two)
    grad_middle = grad_rows + grad_middle_norm
    grad_norm2, grad_router, grad_shared_gate, grad_shared_in, grad_shared_out = (
        lax.psum_scatter(term_norm_two, ("dp", "expert"), scatter_dimension=0, tiled=True),
        lax.psum_scatter(term_router, ("dp", "expert"), scatter_dimension=0, tiled=True),
        lax.psum_scatter(term_gate, ("dp", "expert"), scatter_dimension=0, tiled=True),
        lax.psum_scatter(term_shared_in, ("dp", "expert"), scatter_dimension=0, tiled=True),
        lax.psum_scatter(term_shared_out, ("dp", "expert"), scatter_dimension=0, tiled=True),
    )
    grad_branch = grad_middle.astype(jnp.bfloat16)
    term_out_weight = jnp.einsum(
        "td,te->de", attended, grad_branch, preferred_element_type=jnp.float32
    )
    grad_attended = (
        jnp.einsum("te,de->td", grad_branch, weight_out, preferred_element_type=jnp.float32)
        .astype(jnp.bfloat16)
        .reshape(row_count, head_count, HD)
    )
    weights_again = jnp.exp(score_rows(query_low) - log_total)
    weights_again_low = weights_again.astype(jnp.bfloat16)
    grad_weights = jnp.einsum(
        "qhd,khd->hqk", grad_attended, values_all, preferred_element_type=jnp.float32
    )
    delta_rows = jnp.sum(weights_again * grad_weights, axis=-1, keepdims=True)
    grad_scores = (weights_again * (grad_weights - delta_rows)).astype(jnp.bfloat16)
    grad_query_turned = (
        jnp.einsum("hqk,khd->qhd", grad_scores, keys_all, preferred_element_type=jnp.float32)
        * score_scale
    )
    grad_keys_all = (
        jnp.einsum("hqk,qhd->khd", grad_scores, query_low, preferred_element_type=jnp.float32)
        * score_scale
    )
    grad_values_all = jnp.einsum(
        "hqk,qhd->khd", weights_again_low, grad_attended, preferred_element_type=jnp.float32
    )
    grad_key_turned, grad_values = (
        lax.psum_scatter(
            grad_keys_all.astype(jnp.bfloat16), "expert", scatter_dimension=0, tiled=True
        ).astype(jnp.float32),
        lax.psum_scatter(
            grad_values_all.astype(jnp.bfloat16), "expert", scatter_dimension=0, tiled=True
        ).astype(jnp.float32),
    )
    grad_projected = jnp.concatenate(
        [
            rotate_back(grad_query_turned, cosine, sine).reshape(row_count, model_width),
            rotate_back(grad_key_turned, cosine, sine).reshape(row_count, model_width),
            grad_values.reshape(row_count, model_width),
        ],
        axis=-1,
    ).astype(jnp.bfloat16)
    term_bias = jnp.sum(grad_projected.astype(jnp.float32), axis=0)
    term_qkv = jnp.einsum(
        "td,tf->df", normed_one, grad_projected, preferred_element_type=jnp.float32
    )
    grad_normed_one = jnp.einsum(
        "tf,df->td", grad_projected, weight_qkv, preferred_element_type=jnp.float32
    )
    grad_input_norm, term_norm_one = norm_back(inputs, scale_first, gain_one, grad_normed_one)
    input_grad = (grad_middle + grad_input_norm).astype(jnp.bfloat16)
    grad_norm1, grad_qkv, grad_bias, grad_out_weight = (
        lax.psum_scatter(term_norm_one, ("dp", "expert"), scatter_dimension=0, tiled=True),
        lax.psum_scatter(term_qkv, ("dp", "expert"), scatter_dimension=0, tiled=True),
        lax.psum_scatter(term_bias, ("dp", "expert"), scatter_dimension=0, tiled=True),
        lax.psum_scatter(term_out_weight, ("dp", "expert"), scatter_dimension=0, tiled=True),
    )
    return (
        output,
        input_grad,
        grad_norm1,
        grad_qkv,
        grad_bias,
        grad_out_weight,
        grad_norm2,
        grad_router,
        grad_shared_gate,
        grad_shared_in,
        grad_shared_out,
        grad_expert_in,
        grad_expert_out,
    )


def bf16(values):
    return values.astype(jnp.bfloat16)


def two_parts(values):
    high = lax.reduce_precision(values, exponent_bits=8, mantissa_bits=7)
    return (bf16(high), bf16(values - high))


def mm(left, right):
    return jnp.dot(left, right, preferred_element_type=jnp.float32)


def mm_nt(left, right):
    return lax.dot_general(
        left, right, (((1,), (1,)), ((), ())), preferred_element_type=jnp.float32
    )


def mm_tn(left, right):
    return lax.dot_general(
        left, right, (((0,), (0,)), ((), ())), preferred_element_type=jnp.float32
    )


def group_device(
    hidden_in,
    out_grad,
    lengths,
    routes,
    norm1_gain,
    qkv_weight,
    qkv_bias,
    out_weight,
    norm2_gain,
    router_weight,
    shared_gate,
    shared_in,
    shared_out,
    expert_in,
    expert_out,
):
    size = lax.axis_size("expert")
    parts = lax.axis_size("dp")
    me = lax.axis_index("expert")
    core = me % 2
    rows, width = hidden_in.shape
    group = rows * size
    heads = width // HD
    own_heads = heads // size
    half = parts // 2
    places = size // 2
    block = width // (parts * size)
    top = routes.shape[1]
    experts = router_weight.shape[1]
    score_scale = HD ** (-0.5)
    bias_cols = 3 * width // (parts * size) // block
    extra = 128
    shared_block = shared_out.shape[0]
    own_shared = parts * shared_block
    own_qkv = 3 * own_heads * HD

    def by_head(columns):
        count = columns.shape[0]
        cut = columns.reshape(count, 3, 2, half, places, HD)
        return cut.transpose(4, 2, 0, 1, 3, 5).reshape(size, count, own_qkv)

    def from_head(pieces):
        count = pieces.shape[1]
        cut = pieces.reshape(places, 2, count, 3, half, HD)
        return cut.transpose(2, 3, 1, 4, 0, 5).reshape(count, 3 * width)

    side = jnp.pad(bf16(routes), ((0, 0), (0, extra - top)))
    gathered = lax.all_gather(
        jnp.concatenate([hidden_in, side], axis=1), "expert", axis=0, tiled=True
    )
    hidden_all = gathered[:, :width].astype(jnp.float32)
    routes_all = gathered[:, width : width + top].astype(jnp.int32)

    small = jnp.concatenate(
        [
            norm1_gain[:, None],
            norm2_gain[:, None],
            shared_gate[:, None],
            router_weight,
            qkv_bias.reshape(block, bias_cols),
        ],
        axis=1,
    )
    small = jnp.pad(small, ((0, 0), (0, extra - small.shape[1])))
    sent = jnp.concatenate(
        [by_head(qkv_weight), jnp.broadcast_to(small[None], (size, block, extra))], axis=2
    )
    sent = lax.all_to_all(sent, "expert", split_axis=0, concat_axis=0, tiled=True)
    qkv_full = lax.all_gather(
        sent.reshape(size * block, own_qkv + extra), "dp", axis=0, tiled=True
    )
    weight_qkv = qkv_full[:, :own_qkv]
    small = qkv_full[:, own_qkv:]
    gain_one = small[:, 0].astype(jnp.float32)
    gain_two = small[:, 1].astype(jnp.float32)
    weight_router = small[:, 2 : 3 + experts]
    bias_all = by_head(small[:, 3 + experts : 3 + experts + bias_cols].reshape(1, 3 * width))
    bias_own = lax.dynamic_index_in_dim(bias_all, me, 0, keepdims=False).astype(jnp.float32)

    swap = [(i, i ^ 1) for i in range(size)]

    def own_half(values):
        return lax.dynamic_slice_in_dim(values, core * half, half, 0)

    def other_half(values):
        return lax.dynamic_slice_in_dim(values, (1 - core) * half, half, 0)

    out_blocks = lax.all_gather(out_weight[None], "dp", axis=0, tiled=True)
    kept = own_half(out_blocks)
    came = lax.ppermute(other_half(out_blocks), "expert", swap)
    weight_out = jnp.stack(
        [jnp.where(core == 0, kept, came), jnp.where(core == 0, came, kept)], axis=1
    ).reshape(own_heads * HD, width)

    cut = shared_in.reshape(block, 2, parts, size, shared_block)
    cut = cut.transpose(3, 0, 1, 2, 4).reshape(size, block, 2 * own_shared)
    cut = lax.all_to_all(cut, "expert", split_axis=0, concat_axis=0, tiled=True)

    segment, position = segment_table(lengths[0], group)
    valid_all = (segment < lengths.shape[1] - 1).astype(jnp.float32)[:, None]
    cosine, sine = rotary_tables(position, HD)
    allowed = (
        (segment[:, None] == segment[None, :]) & (position[:, None] >= position[None, :])
    )[None]
    scale_first_all = rms_scale(hidden_all)
    normed_one = bf16(hidden_all * scale_first_all * gain_one)
    projected = mm(normed_one, weight_qkv) + bias_own
    split = projected.reshape(group, 3, own_heads, HD)
    query_low = bf16(rotate(split[:, 0], cosine, sine))
    key_low = bf16(rotate(split[:, 1], cosine, sine))
    value_low = bf16(split[:, 2])

    def score_rows():
        raw = (
            jnp.einsum("qhd,khd->hqk", query_low, key_low, preferred_element_type=jnp.float32)
            * score_scale
        )
        return jnp.where(allowed, raw, NEG_FILL)

    scores = score_rows()
    peak = jnp.max(scores, axis=-1, keepdims=True)
    log_total = peak + jnp.log(jnp.sum(jnp.exp(scores - peak), axis=-1, keepdims=True))
    weights_low = bf16(jnp.exp(scores - log_total))
    attended = bf16(
        jnp.einsum(
            "hqk,khd->qhd", weights_low, value_low, preferred_element_type=jnp.float32
        ).reshape(group, own_heads * HD)
    )
    branch = lax.psum_scatter(
        bf16(mm(attended, weight_out)), "expert", scatter_dimension=0, tiled=True
    )
    inputs = hidden_in.astype(jnp.float32)
    middle = inputs + branch.astype(jnp.float32)
    scale_second = rms_scale(middle)
    normed_two = bf16(middle * scale_second * gain_two)
    normed_all = lax.all_gather(normed_two, "expert", axis=0, tiled=True)

    weight_expert_in = lax.all_gather(expert_in, "dp", axis=1, tiled=True)[0]
    weight_expert_out = lax.all_gather(expert_out, "dp", axis=1, tiled=True)[0]
    weight_shared_in = lax.all_gather(
        cut.reshape(size * block, 2 * own_shared), "dp", axis=0, tiled=True
    )
    weight_shared_out = lax.all_gather(shared_out, "dp", axis=0, tiled=True)
    grad_all = lax.all_gather(out_grad, "expert", axis=0, tiled=True)

    gate_logits = mm(normed_all, weight_router)
    logits = gate_logits[:, 1:]
    opener_all = jax.nn.sigmoid(gate_logits[:, :1])
    peak_logit = jnp.max(logits, axis=-1, keepdims=True)
    router_total = peak_logit + jnp.log(
        jnp.sum(jnp.exp(logits - peak_logit), axis=-1, keepdims=True)
    )
    probs_all = jnp.exp(logits - router_total)
    expert_ids = jnp.arange(experts, dtype=jnp.int32)
    named = jnp.sum((routes_all == me).astype(jnp.float32), axis=1, keepdims=True)
    own_prob = jnp.sum(
        jnp.where(expert_ids[None, :] == me, probs_all, 0.0), axis=1, keepdims=True
    )
    gate_own = named * own_prob

    expert_up = mm(normed_all, weight_expert_in)
    expert_hidden = bf16(swiglu(expert_up))
    expert_result = bf16(mm(expert_hidden, weight_expert_out)).astype(jnp.float32)
    shared_up = mm(normed_all, weight_shared_in)
    shared_hidden = bf16(swiglu(shared_up))
    shared_rows = mm(shared_hidden, weight_shared_out)
    grad_rows = grad_all.astype(jnp.float32) * valid_all
    dot_expert = named * jnp.sum(grad_rows * expert_result, axis=1, keepdims=True)
    dot_shared = jnp.sum(grad_rows * shared_rows, axis=1, keepdims=True)
    mine = expert_ids[None, :] == me
    expert_high, expert_low = two_parts(dot_expert)
    shared_high, shared_low = two_parts(dot_shared)
    zero = jnp.zeros((), jnp.bfloat16)
    riders = jnp.concatenate(
        [
            jnp.where(mine, column, zero)
            for column in (expert_high, expert_low, shared_high, shared_low)
        ],
        axis=1,
    )
    riders = jnp.pad(riders, ((0, 0), (0, extra - riders.shape[1])))
    combined = jnp.concatenate(
        [bf16(gate_own * expert_result + opener_all * shared_rows), riders], axis=1
    )
    summed = lax.psum_scatter(combined, "expert", scatter_dimension=0, tiled=True)

    def rows_of(values):
        return lax.dynamic_slice_in_dim(values, me * rows, rows, 0)

    valid_rows = rows_of(valid_all)
    output = bf16(valid_rows * (middle + summed[:, :width].astype(jnp.float32)))
    tail = summed[:, width : width + 4 * experts].astype(jnp.float32)
    grad_probs = tail[:, :experts] + tail[:, experts : 2 * experts]
    dot_gate = jnp.sum(tail[:, 2 * experts :], axis=1, keepdims=True)

    grad_shared_rows = bf16(grad_rows * opener_all)
    grad_shared_up = bf16(swiglu_back(shared_up, mm_nt(grad_shared_rows, weight_shared_out)))
    term_shared_out = mm_tn(shared_hidden, grad_shared_rows)
    term_shared_in = mm_tn(normed_all, grad_shared_up)
    grad_result = bf16(gate_own * grad_rows)
    grad_expert_up = bf16(swiglu_back(expert_up, mm_nt(grad_result, weight_expert_out)))
    term_expert_out = mm_tn(expert_hidden, grad_result)
    term_expert_in = mm_tn(normed_all, grad_expert_up)
    grad_normed_part = bf16(
        mm_nt(grad_shared_up, weight_shared_in) + mm_nt(grad_expert_up, weight_expert_in)
    )
    grad_normed_two = lax.psum_scatter(
        grad_normed_part, "expert", scatter_dimension=0, tiled=True
    ).astype(jnp.float32)
    grad_expert_in = lax.psum_scatter(
        bf16(term_expert_in)[None], "dp", scatter_dimension=1, tiled=True
    ).astype(jnp.float32)
    grad_expert_out = lax.psum_scatter(
        bf16(term_expert_out)[None], "dp", scatter_dimension=1, tiled=True
    ).astype(jnp.float32)
    grad_shared_out = lax.psum_scatter(
        bf16(term_shared_out), "dp", scatter_dimension=0, tiled=True
    ).astype(jnp.float32)
    cut = lax.psum_scatter(bf16(term_shared_in), "dp", scatter_dimension=0, tiled=True)
    cut = lax.all_to_all(
        cut.reshape(size, block, 2 * own_shared), "expert", split_axis=0, concat_axis=0, tiled=True
    )
    grad_shared_in = (
        cut.reshape(size, block, 2, parts, shared_block)
        .transpose(1, 2, 3, 0, 4)
        .reshape(block, 2 * parts * size * shared_block)
        .astype(jnp.float32)
    )

    opener = rows_of(opener_all)
    probs = rows_of(probs_all)
    grad_gate_logit = dot_gate * opener * (1.0 - opener)
    grad_logits = probs * (grad_probs - jnp.sum(probs * grad_probs, axis=-1, keepdims=True))
    grad_heads = bf16(jnp.concatenate([grad_gate_logit, grad_logits], axis=1))
    term_router = mm_tn(normed_two, grad_heads)
    grad_normed_two = grad_normed_two + mm_nt(grad_heads, weight_router)
    grad_middle_norm, term_norm_two = norm_back(middle, scale_second, gain_two, grad_normed_two)
    grad_middle = rows_of(grad_rows) + grad_middle_norm
    grad_branch = lax.all_gather(bf16(grad_middle), "expert", axis=0, tiled=True)

    term_out = bf16(mm_tn(attended, grad_branch)).reshape(half, 2, block, width)
    grad_attended = bf16(mm_nt(grad_branch, weight_out)).reshape(group, own_heads, HD)
    weights_again = jnp.exp(score_rows() - log_total)
    grad_weights = jnp.einsum(
        "qhd,khd->hqk", grad_attended, value_low, preferred_element_type=jnp.float32
    )
    delta_rows = jnp.sum(weights_again * grad_weights, axis=-1, keepdims=True)
    grad_scores = bf16(weights_again * (grad_weights - delta_rows))
    grad_query_turned = (
        jnp.einsum("hqk,khd->qhd", grad_scores, key_low, preferred_element_type=jnp.float32)
        * score_scale
    )
    grad_key_turned = (
        jnp.einsum("hqk,qhd->khd", grad_scores, query_low, preferred_element_type=jnp.float32)
        * score_scale
    )
    grad_values = jnp.einsum(
        "hqk,qhd->khd", bf16(weights_again), grad_attended, preferred_element_type=jnp.float32
    )
    grad_projected = bf16(
        jnp.stack(
            [
                rotate_back(grad_query_turned, cosine, sine),
                rotate_back(grad_key_turned, cosine, sine),
                grad_values,
            ],
            axis=1,
        ).reshape(group, own_qkv)
    )
    grad_normed_part = bf16(mm_nt(grad_projected, weight_qkv))
    grad_normed_one = lax.psum_scatter(
        grad_normed_part, "expert", scatter_dimension=0, tiled=True
    ).astype(jnp.float32)
    scale_first = rms_scale(inputs)
    grad_input_norm, term_norm_one = norm_back(inputs, scale_first, gain_one, grad_normed_one)
    input_grad = bf16(grad_middle + grad_input_norm)

    kept = jnp.where(core == 0, term_out[:, 0], term_out[:, 1])
    given = jnp.where(core == 0, term_out[:, 1], term_out[:, 0])
    came = lax.ppermute(given, "expert", swap)
    out_blocks = jnp.concatenate(
        [jnp.where(core == 0, kept, came), jnp.where(core == 0, came, kept)], axis=0
    )
    grad_out_weight = lax.psum_scatter(
        out_blocks, "dp", scatter_dimension=0, tiled=True
    ).astype(jnp.float32)[0]

    term_qkv = mm_tn(normed_one, grad_projected)
    term_bias = jnp.sum(grad_projected.astype(jnp.float32), axis=0)
    bias_slots = jnp.where(jnp.arange(size)[:, None] == me, term_bias[None, :], 0.0)
    bias_rows = from_head(bias_slots[:, None, :]).reshape(width, bias_cols)
    small_terms = jnp.concatenate(
        [term_norm_one[:, None], term_norm_two[:, None], term_router, bias_rows], axis=1
    )
    count = small_terms.shape[1]
    small_high, small_low = two_parts(small_terms)
    small_terms = jnp.concatenate([small_high, small_low], axis=1)
    small_terms = jnp.pad(small_terms, ((0, 0), (0, extra - 2 * count)))
    back = lax.psum_scatter(
        jnp.concatenate([bf16(term_qkv), small_terms], axis=1), "dp", scatter_dimension=0, tiled=True
    )
    back = lax.all_to_all(
        back.reshape(size, block, own_qkv + extra), "expert", split_axis=0, concat_axis=0, tiled=True
    ).astype(jnp.float32)
    grad_qkv = from_head(back[:, :, :own_qkv])
    small_sum = jnp.sum(back[:, :, own_qkv:], axis=0)
    small_sum = small_sum[:, :count] + small_sum[:, count : 2 * count]
    grad_norm1 = small_sum[:, 0]
    grad_norm2 = small_sum[:, 1]
    grad_shared_gate = small_sum[:, 2]
    grad_router = small_sum[:, 3 : 3 + experts]
    grad_bias = small_sum[:, 3 + experts :].reshape(block * bias_cols)
    return (
        output,
        input_grad,
        grad_norm1,
        grad_qkv,
        grad_bias,
        grad_out_weight,
        grad_norm2,
        grad_router,
        grad_shared_gate,
        grad_shared_in,
        grad_shared_out,
        grad_expert_in,
        grad_expert_out,
    )


def solution(mesh):
    size, parts = mesh.shape["expert"], mesh.shape["dp"]

    def device(*arrays):
        block = arrays[5].shape[0]
        whole_heads = 2 * block == HD and parts % 2 == 0 and size % 2 == 0
        one_expert = arrays[13].shape[0] == 1
        if whole_heads and one_expert and arrays[5].shape[1] % (3 * size * HD) == 0:
            return group_device(*arrays)
        return per_device(*arrays)

    return jax.shard_map(
        device,
        mesh=mesh,
        in_specs=(
            P(("dp", "expert"), None),
            P(("dp", "expert"), None),
            P("dp", None),
            P(("dp", "expert"), None),
            P(("dp", "expert")),
            P(("dp", "expert"), None),
            P(("dp", "expert")),
            P(("dp", "expert"), None),
            P(("dp", "expert")),
            P(("dp", "expert"), None),
            P(("dp", "expert")),
            P(("dp", "expert"), None),
            P(("dp", "expert"), None),
            P("expert", "dp", None),
            P("expert", "dp", None),
        ),
        out_specs=(
            P(("dp", "expert"), None),
            P(("dp", "expert"), None),
            P(("dp", "expert")),
            P(("dp", "expert"), None),
            P(("dp", "expert")),
            P(("dp", "expert"), None),
            P(("dp", "expert")),
            P(("dp", "expert"), None),
            P(("dp", "expert")),
            P(("dp", "expert"), None),
            P(("dp", "expert"), None),
            P("expert", "dp", None),
            P("expert", "dp", None),
        ),
        check_vma=False,
    )
```

```python
import functools

import jax
import jax.numpy as jnp
from jax import lax
from jax.experimental import pallas as pl
from jax.experimental.pallas import tpu as pltpu
from jax.sharding import PartitionSpec as P

HD = 128


EPSILON = 1e-06
THETA = 1000000.0
NEG_FILL = -1e30


def rms_scale(values):
    return lax.rsqrt(jnp.mean(values * values, axis=-1, keepdims=True) + EPSILON)


def rotary_tables(positions, head_size):
    half_size = head_size // 2
    steps_up = jnp.arange(half_size, dtype=jnp.float32) * (2.0 / head_size)
    inverse = THETA ** (-steps_up)
    angles = positions.astype(jnp.float32)[:, None] * inverse[None, :]
    angles = jnp.concatenate([angles, angles], axis=-1)
    return (jnp.cos(angles)[:, None, :], jnp.sin(angles)[:, None, :])


def rotate(values, cosine, sine):
    half_size = values.shape[-1] // 2
    turned = jnp.concatenate([-values[..., half_size:], values[..., :half_size]], axis=-1)
    return values * cosine + turned * sine


def rotate_back(grad_values, cosine, sine):
    half_size = grad_values.shape[-1] // 2
    scaled = grad_values * sine
    turned = jnp.concatenate([scaled[..., half_size:], -scaled[..., :half_size]], axis=-1)
    return grad_values * cosine + turned


def swiglu(gate_up):
    half_size = gate_up.shape[-1] // 2
    return jax.nn.silu(gate_up[..., :half_size]) * gate_up[..., half_size:]


def swiglu_back(gate_up, grad_hidden):
    half_size = gate_up.shape[-1] // 2
    gate_part = gate_up[..., :half_size]
    up_part = gate_up[..., half_size:]
    sigmoid_gate = jax.nn.sigmoid(gate_part)
    grad_gate = grad_hidden * up_part * sigmoid_gate * (1.0 + gate_part * (1.0 - sigmoid_gate))
    grad_up = grad_hidden * gate_part * sigmoid_gate
    return jnp.concatenate([grad_gate, grad_up], axis=-1)


def norm_back(values, scale_rows, gain, grad_normed):
    weighted = grad_normed * gain
    inner = jnp.mean(weighted * values, axis=-1, keepdims=True)
    grad_values = scale_rows * weighted - values * scale_rows * scale_rows * scale_rows * inner
    grad_gain = jnp.sum(grad_normed * values * scale_rows, axis=0)
    return (grad_values, grad_gain)


def segment_table(length_row, count):
    ends = jnp.cumsum(length_row, dtype=jnp.int32)
    starts = ends - length_row
    places = jnp.arange(count, dtype=jnp.int32)
    segment = jnp.sum(
        (places[:, None] >= ends[None, :-1]).astype(jnp.int32), axis=1, dtype=jnp.int32
    )
    owners = segment[:, None] == jnp.arange(length_row.shape[0], dtype=jnp.int32)[None, :]
    first = jnp.sum(jnp.where(owners, starts[None, :], 0), axis=1, dtype=jnp.int32)
    return (segment, places - first)


def per_device(
    hidden_in,
    out_grad,
    lengths,
    routes,
    norm1_gain,
    qkv_weight,
    qkv_bias,
    out_weight,
    norm2_gain,
    router_weight,
    shared_gate,
    shared_in,
    shared_out,
    expert_in,
    expert_out,
):
    highest = lax.Precision.HIGHEST
    row_count, model_width = hidden_in.shape
    head_count = model_width // HD
    group_size = lax.axis_size("expert")
    group_rows = row_count * group_size
    top_count = routes.shape[1]
    expert_count = router_weight.shape[1]
    local_count = expert_in.shape[0]
    capacity = max(2, 2 * row_count * top_count // expert_count)
    slot_count = expert_count * capacity
    score_scale = HD ** (-0.5)
    dense = (
        lax.all_gather(norm1_gain, ("dp", "expert"), axis=0, tiled=True),
        lax.all_gather(qkv_weight, ("dp", "expert"), axis=0, tiled=True),
        lax.all_gather(qkv_bias, ("dp", "expert"), axis=0, tiled=True),
        lax.all_gather(out_weight, ("dp", "expert"), axis=0, tiled=True),
        lax.all_gather(norm2_gain, ("dp", "expert"), axis=0, tiled=True),
        lax.all_gather(router_weight, ("dp", "expert"), axis=0, tiled=True),
        lax.all_gather(shared_gate, ("dp", "expert"), axis=0, tiled=True),
        lax.all_gather(shared_in, ("dp", "expert"), axis=0, tiled=True),
        lax.all_gather(shared_out, ("dp", "expert"), axis=0, tiled=True),
    )
    (
        gain_first,
        weight_qkv,
        bias_first,
        weight_out,
        gain_second,
        weight_router,
        weight_gate,
        weight_shared_in,
        weight_shared_out,
    ) = dense
    weight_expert_in, weight_expert_out = (
        lax.all_gather(expert_in, "dp", axis=1, tiled=True),
        lax.all_gather(expert_out, "dp", axis=1, tiled=True),
    )
    segment_all, position_all = segment_table(lengths[0], group_rows)
    first_row = lax.axis_index("expert") * row_count
    segment_mine = lax.dynamic_slice_in_dim(segment_all, first_row, row_count, 0)
    position_mine = lax.dynamic_slice_in_dim(position_all, first_row, row_count, 0)
    valid_rows = (segment_mine < lengths.shape[1] - 1).astype(jnp.float32)[:, None]
    cosine, sine = rotary_tables(position_mine, HD)
    allowed = (
        (segment_mine[:, None] == segment_all[None, :])
        & (position_mine[:, None] >= position_all[None, :])
    )[None]
    inputs = hidden_in.astype(jnp.float32)
    scale_first = rms_scale(inputs)
    gain_one = gain_first.astype(jnp.float32)
    normed_one = (inputs * scale_first * gain_one).astype(jnp.bfloat16)
    projected = jnp.dot(
        normed_one, weight_qkv, preferred_element_type=jnp.float32
    ) + bias_first.astype(jnp.float32)
    query_low = rotate(
        projected[:, :model_width].reshape(row_count, head_count, HD), cosine, sine
    ).astype(jnp.bfloat16)
    key_low = rotate(
        projected[:, model_width : 2 * model_width].reshape(row_count, head_count, HD), cosine, sine
    ).astype(jnp.bfloat16)
    value_low = (
        projected[:, 2 * model_width :].reshape(row_count, head_count, HD).astype(jnp.bfloat16)
    )
    keys_all, values_all = (
        lax.all_gather(key_low, "expert", axis=0, tiled=True),
        lax.all_gather(value_low, "expert", axis=0, tiled=True),
    )

    def score_rows(queries):
        raw = (
            jnp.einsum("qhd,khd->hqk", queries, keys_all, preferred_element_type=jnp.float32)
            * score_scale
        )
        return jnp.where(allowed, raw, NEG_FILL)

    scores = score_rows(query_low)
    peak = jnp.max(scores, axis=-1, keepdims=True)
    log_total = peak + jnp.log(jnp.sum(jnp.exp(scores - peak), axis=-1, keepdims=True))
    weights_low = jnp.exp(scores - log_total).astype(jnp.bfloat16)
    attended = (
        jnp.einsum("hqk,khd->qhd", weights_low, values_all, preferred_element_type=jnp.float32)
        .reshape(row_count, model_width)
        .astype(jnp.bfloat16)
    )
    middle = inputs + jnp.dot(attended, weight_out, preferred_element_type=jnp.float32)
    scale_second = rms_scale(middle)
    gain_two = gain_second.astype(jnp.float32)
    normed_two = (middle * scale_second * gain_two).astype(jnp.bfloat16)
    logits = jnp.dot(normed_two, weight_router, preferred_element_type=jnp.float32)
    gate_logit = jnp.dot(normed_two, weight_gate, preferred_element_type=jnp.float32)
    peak_logit = jnp.max(logits, axis=-1, keepdims=True)
    router_total = peak_logit + jnp.log(
        jnp.sum(jnp.exp(logits - peak_logit), axis=-1, keepdims=True)
    )
    router_probs = jnp.exp(logits - router_total)
    expert_ids = jnp.arange(expert_count, dtype=jnp.int32)
    chosen = routes[:, :, None] == expert_ids[None, None, :]
    chosen_float = chosen.astype(jnp.float32)
    gates = jnp.sum(chosen_float * router_probs[:, None, :], axis=2)
    flat_hits = chosen.reshape(row_count * top_count, expert_count).astype(jnp.int32)
    earlier = jnp.cumsum(flat_hits, axis=0, dtype=jnp.int32) - flat_hits
    slot_rank = jnp.sum(earlier * flat_hits, axis=1, dtype=jnp.int32)
    slot_of = routes.reshape(-1) * capacity + slot_rank
    slot_hits = (
        (slot_of[:, None] == jnp.arange(slot_count, dtype=jnp.int32)[None, :])
        .reshape(row_count, top_count, slot_count)
        .astype(jnp.float32)
    )
    placement_map = jnp.sum(slot_hits, axis=1)
    weighted_map = jnp.sum(slot_hits * gates[:, :, None], axis=1)
    send_rows = (
        jnp.einsum(
            "ts,td->sd",
            placement_map.astype(jnp.bfloat16),
            normed_two,
            preferred_element_type=jnp.float32,
        )
        .astype(jnp.bfloat16)
        .reshape(expert_count, capacity, model_width)
    )
    arrived = lax.all_to_all(send_rows, "expert", split_axis=0, concat_axis=0, tiled=True)
    item_count = arrived.shape[1]
    grouped = arrived.reshape(group_size, local_count, item_count, model_width)
    gate_up = jnp.einsum(
        "gecd,edf->gecf", grouped, weight_expert_in, preferred_element_type=jnp.float32
    )
    hidden_low = swiglu(gate_up).astype(jnp.bfloat16)
    produced = jnp.einsum(
        "gecf,efd->gecd", hidden_low, weight_expert_out, preferred_element_type=jnp.float32
    ).astype(jnp.bfloat16)
    produced_rows = produced.reshape(group_size * local_count, item_count, model_width)
    expert_gate_up = gate_up.reshape(group_size * local_count, item_count, gate_up.shape[-1])
    back_rows = lax.all_to_all(produced_rows, "expert", split_axis=0, concat_axis=0, tiled=True)
    back_float = back_rows.reshape(slot_count, model_width).astype(jnp.float32)
    routed = jnp.dot(weighted_map, back_float, precision=highest)
    shared_up = jnp.dot(normed_two, weight_shared_in, preferred_element_type=jnp.float32)
    shared_hidden = swiglu(shared_up).astype(jnp.bfloat16)
    shared_rows = jnp.dot(shared_hidden, weight_shared_out, preferred_element_type=jnp.float32)
    opener = jax.nn.sigmoid(gate_logit)[:, None]
    output = (valid_rows * (middle + routed + opener * shared_rows)).astype(jnp.bfloat16)
    held = (
        lax.all_gather(norm1_gain, ("dp", "expert"), axis=0, tiled=True),
        lax.all_gather(qkv_weight, ("dp", "expert"), axis=0, tiled=True),
        lax.all_gather(qkv_bias, ("dp", "expert"), axis=0, tiled=True),
        lax.all_gather(out_weight, ("dp", "expert"), axis=0, tiled=True),
        lax.all_gather(norm2_gain, ("dp", "expert"), axis=0, tiled=True),
        lax.all_gather(router_weight, ("dp", "expert"), axis=0, tiled=True),
        lax.all_gather(shared_gate, ("dp", "expert"), axis=0, tiled=True),
        lax.all_gather(shared_in, ("dp", "expert"), axis=0, tiled=True),
        lax.all_gather(shared_out, ("dp", "expert"), axis=0, tiled=True),
    )
    (
        gain_first,
        weight_qkv,
        bias_first,
        weight_out,
        gain_second,
        weight_router,
        weight_gate,
        weight_shared_in,
        weight_shared_out,
    ) = held
    gain_one = gain_first.astype(jnp.float32)
    gain_two = gain_second.astype(jnp.float32)
    grad_rows = out_grad.astype(jnp.float32) * valid_rows
    grad_shared_rows = (grad_rows * opener).astype(jnp.bfloat16)
    grad_gate_logit = (
        jnp.sum(grad_rows * shared_rows, axis=-1) * opener[:, 0] * (1.0 - opener[:, 0])
    ).astype(jnp.bfloat16)
    grad_shared_hidden = jnp.einsum(
        "td,fd->tf", grad_shared_rows, weight_shared_out, preferred_element_type=jnp.float32
    )
    grad_shared_up = swiglu_back(shared_up, grad_shared_hidden).astype(jnp.bfloat16)
    term_shared_out = jnp.einsum(
        "tf,td->fd", shared_hidden, grad_shared_rows, preferred_element_type=jnp.float32
    )
    term_shared_in = jnp.einsum(
        "td,tf->df", normed_two, grad_shared_up, preferred_element_type=jnp.float32
    )
    slot_product = jnp.einsum("td,sd->ts", grad_rows, back_float, precision=highest)
    grad_gates = jnp.sum(slot_hits * slot_product[:, None, :], axis=2)
    grad_probs = jnp.sum(chosen_float * grad_gates[:, :, None], axis=1)
    grad_logits = (
        router_probs * (grad_probs - jnp.sum(router_probs * grad_probs, axis=-1, keepdims=True))
    ).astype(jnp.bfloat16)
    term_router = jnp.einsum(
        "td,te->de", normed_two, grad_logits, preferred_element_type=jnp.float32
    )
    term_gate = jnp.einsum(
        "td,t->d", normed_two, grad_gate_logit, preferred_element_type=jnp.float32
    )
    grad_result = (
        jnp.einsum("ts,td->sd", weighted_map, grad_rows, precision=highest)
        .astype(jnp.bfloat16)
        .reshape(expert_count, capacity, model_width)
    )
    grad_arrived = lax.all_to_all(grad_result, "expert", split_axis=0, concat_axis=0, tiled=True)
    grad_grouped = grad_arrived.reshape(group_size, local_count, capacity, model_width)
    gate_up_grouped = expert_gate_up.reshape(
        group_size, local_count, capacity, expert_gate_up.shape[-1]
    )
    hidden_again = swiglu(gate_up_grouped).astype(jnp.bfloat16)
    grad_hidden = jnp.einsum(
        "gecd,efd->gecf", grad_grouped, weight_expert_out, preferred_element_type=jnp.float32
    )
    grad_gate_up = swiglu_back(gate_up_grouped, grad_hidden).astype(jnp.bfloat16)
    arrived_grouped = arrived.reshape(group_size, local_count, capacity, model_width)
    term_expert_in = jnp.einsum(
        "gecd,gecf->edf", arrived_grouped, grad_gate_up, preferred_element_type=jnp.float32
    )
    term_expert_out = jnp.einsum(
        "gecf,gecd->efd", hidden_again, grad_grouped, preferred_element_type=jnp.float32
    )
    grad_sent = jnp.einsum(
        "gecf,edf->gecd", grad_gate_up, weight_expert_in, preferred_element_type=jnp.float32
    ).reshape(group_size * local_count, capacity, model_width)
    grad_slots = lax.all_to_all(
        grad_sent.astype(jnp.bfloat16), "expert", split_axis=0, concat_axis=0, tiled=True
    ).astype(grad_sent.dtype)
    grad_expert_in, grad_expert_out = (
        lax.psum_scatter(
            term_expert_in.astype(jnp.bfloat16), "dp", scatter_dimension=1, tiled=True
        ).astype(jnp.float32),
        lax.psum_scatter(
            term_expert_out.astype(jnp.bfloat16), "dp", scatter_dimension=1, tiled=True
        ).astype(jnp.float32),
    )
    grad_normed_two = jnp.einsum(
        "te,de->td", grad_logits, weight_router, preferred_element_type=jnp.float32
    )
    grad_normed_two = (
        grad_normed_two
        + grad_gate_logit.astype(jnp.float32)[:, None] * weight_gate.astype(jnp.float32)[None, :]
    )
    grad_normed_two = grad_normed_two + jnp.einsum(
        "tf,df->td", grad_shared_up, weight_shared_in, preferred_element_type=jnp.float32
    )
    grad_normed_two = grad_normed_two + jnp.dot(
        placement_map, grad_slots.reshape(slot_count, model_width), precision=highest
    )
    grad_middle_norm, term_norm_two = norm_back(middle, scale_second, gain_two, grad_normed_two)
    grad_middle = grad_rows + grad_middle_norm
    grad_norm2, grad_router, grad_shared_gate, grad_shared_in, grad_shared_out = (
        lax.psum_scatter(term_norm_two, ("dp", "expert"), scatter_dimension=0, tiled=True),
        lax.psum_scatter(term_router, ("dp", "expert"), scatter_dimension=0, tiled=True),
        lax.psum_scatter(term_gate, ("dp", "expert"), scatter_dimension=0, tiled=True),
        lax.psum_scatter(term_shared_in, ("dp", "expert"), scatter_dimension=0, tiled=True),
        lax.psum_scatter(term_shared_out, ("dp", "expert"), scatter_dimension=0, tiled=True),
    )
    grad_branch = grad_middle.astype(jnp.bfloat16)
    term_out_weight = jnp.einsum(
        "td,te->de", attended, grad_branch, preferred_element_type=jnp.float32
    )
    grad_attended = (
        jnp.einsum("te,de->td", grad_branch, weight_out, preferred_element_type=jnp.float32)
        .astype(jnp.bfloat16)
        .reshape(row_count, head_count, HD)
    )
    weights_again = jnp.exp(score_rows(query_low) - log_total)
    weights_again_low = weights_again.astype(jnp.bfloat16)
    grad_weights = jnp.einsum(
        "qhd,khd->hqk", grad_attended, values_all, preferred_element_type=jnp.float32
    )
    delta_rows = jnp.sum(weights_again * grad_weights, axis=-1, keepdims=True)
    grad_scores = (weights_again * (grad_weights - delta_rows)).astype(jnp.bfloat16)
    grad_query_turned = (
        jnp.einsum("hqk,khd->qhd", grad_scores, keys_all, preferred_element_type=jnp.float32)
        * score_scale
    )
    grad_keys_all = (
        jnp.einsum("hqk,qhd->khd", grad_scores, query_low, preferred_element_type=jnp.float32)
        * score_scale
    )
    grad_values_all = jnp.einsum(
        "hqk,qhd->khd", weights_again_low, grad_attended, preferred_element_type=jnp.float32
    )
    grad_key_turned, grad_values = (
        lax.psum_scatter(
            grad_keys_all.astype(jnp.bfloat16), "expert", scatter_dimension=0, tiled=True
        ).astype(jnp.float32),
        lax.psum_scatter(
            grad_values_all.astype(jnp.bfloat16), "expert", scatter_dimension=0, tiled=True
        ).astype(jnp.float32),
    )
    grad_projected = jnp.concatenate(
        [
            rotate_back(grad_query_turned, cosine, sine).reshape(row_count, model_width),
            rotate_back(grad_key_turned, cosine, sine).reshape(row_count, model_width),
            grad_values.reshape(row_count, model_width),
        ],
        axis=-1,
    ).astype(jnp.bfloat16)
    term_bias = jnp.sum(grad_projected.astype(jnp.float32), axis=0)
    term_qkv = jnp.einsum(
        "td,tf->df", normed_one, grad_projected, preferred_element_type=jnp.float32
    )
    grad_normed_one = jnp.einsum(
        "tf,df->td", grad_projected, weight_qkv, preferred_element_type=jnp.float32
    )
    grad_input_norm, term_norm_one = norm_back(inputs, scale_first, gain_one, grad_normed_one)
    input_grad = (grad_middle + grad_input_norm).astype(jnp.bfloat16)
    grad_norm1, grad_qkv, grad_bias, grad_out_weight = (
        lax.psum_scatter(term_norm_one, ("dp", "expert"), scatter_dimension=0, tiled=True),
        lax.psum_scatter(term_qkv, ("dp", "expert"), scatter_dimension=0, tiled=True),
        lax.psum_scatter(term_bias, ("dp", "expert"), scatter_dimension=0, tiled=True),
        lax.psum_scatter(term_out_weight, ("dp", "expert"), scatter_dimension=0, tiled=True),
    )
    return (
        output,
        input_grad,
        grad_norm1,
        grad_qkv,
        grad_bias,
        grad_out_weight,
        grad_norm2,
        grad_router,
        grad_shared_gate,
        grad_shared_in,
        grad_shared_out,
        grad_expert_in,
        grad_expert_out,
    )


MESH_IDS = pl.DeviceIdType.MESH
STRIP = 16


class Line:
    def __init__(self, chips):
        me = lax.axis_index("expert")
        self.chips = chips
        self.z = me // 2
        self.core = lax.rem(me, 2)
        self.below = self.z > 0
        self.above = self.z < chips - 1

    def at(self, z, core):
        return {"expert": 2 * z + core}

    def meet(self):
        barrier = pltpu.get_barrier_semaphore()

        def hello(z, core):
            pl.semaphore_signal(
                barrier, inc=1, device_id=self.at(z, core), device_id_type=MESH_IDS
            )

        hello(self.z, 1 - self.core)
        pl.when(self.above)(lambda: hello(self.z + 1, self.core))
        pl.when(self.below)(lambda: hello(self.z - 1, self.core))
        peers = 1 + jnp.minimum(self.z, 1) + jnp.minimum(self.chips - 1 - self.z, 1)
        pl.semaphore_wait(barrier, peers)


def gather_scratch(chips):
    return [
        pltpu.SemaphoreType.DMA((2, chips - 1)),
        pltpu.SemaphoreType.DMA((2, chips - 1)),
        pltpu.SemaphoreType.DMA((2 * chips - 1,)),
        pltpu.SemaphoreType.DMA((2 * chips - 1,)),
        pltpu.SemaphoreType.DMA,
    ]


def gather_line(line, own, out, send, recv, pair_send, pair_recv, local):
    chips, z, core = line.chips, line.z, line.core
    rows = own.shape[0]

    def block(chip, which):
        return out.at[pl.ds((2 * chip + which) * rows, rows)]

    def hop(step, up):
        origin = z - step if up else z + step
        return pltpu.make_async_remote_copy(
            src_ref=own if step == 0 else block(origin, core),
            dst_ref=block(origin, core),
            send_sem=send.at[0 if up else 1, step],
            recv_sem=recv.at[0 if up else 1, step],
            device_id=line.at(z + 1 if up else z - 1, core),
            device_id_type=MESH_IDS,
        )

    def arrival(step, up):
        origin = z - 1 - step if up else z + 1 + step
        return pltpu.make_async_remote_copy(
            src_ref=own,
            dst_ref=block(origin, core),
            send_sem=send.at[0 if up else 1, step],
            recv_sem=recv.at[0 if up else 1, step],
            device_id=line.at(z - 1 if up else z + 1, core),
            device_id_type=MESH_IDS,
        )

    def across(index, origin, source, which):
        return pltpu.make_async_remote_copy(
            src_ref=source,
            dst_ref=block(origin, which),
            send_sem=pair_send.at[index],
            recv_sem=pair_recv.at[index],
            device_id=line.at(z, 1 - core),
            device_id_type=MESH_IDS,
        )

    def sends(step, up):
        return (z >= step) & line.above if up else (z + step <= chips - 1) & line.below

    def comes(step, up):
        return z - 1 - step >= 0 if up else z + 1 + step <= chips - 1

    def pair_of(step, up):
        return 1 + step + (0 if up else chips - 1)

    keep = pltpu.make_async_copy(own, block(z, core), local)
    keep.start()
    for step in range(chips - 1):
        for up in (True, False):
            pl.when(sends(step, up))(lambda step=step, up=up: hop(step, up).start())
        if step == 0:
            across(0, z, own, core).start()
        for up in (True, False):

            def take(step=step, up=up):
                arrival(step, up).wait_recv()
                origin = z - 1 - step if up else z + 1 + step
                across(pair_of(step, up), origin, block(origin, core), core).start()

            pl.when(comes(step, up))(take)
    across(0, z, own, core).wait_send()
    across(0, z, own, 1 - core).wait_recv()
    for step in range(chips - 1):
        for up in (True, False):
            pl.when(sends(step, up))(lambda step=step, up=up: hop(step, up).wait_send())

            def settle(step=step, up=up):
                origin = z - 1 - step if up else z + 1 + step
                across(pair_of(step, up), origin, block(origin, core), core).wait_send()
                across(pair_of(step, up), origin, block(origin, core), 1 - core).wait_recv()

            pl.when(comes(step, up))(settle)
    keep.wait()


def scatter_scratch(chips, rows, width):
    return [
        pltpu.VMEM((chips, rows, width), jnp.bfloat16),
        pltpu.VMEM((2, chips, rows, width), jnp.bfloat16),
        pltpu.SemaphoreType.DMA((chips,)),
        pltpu.SemaphoreType.DMA((chips,)),
        pltpu.SemaphoreType.DMA((2, chips)),
        pltpu.SemaphoreType.DMA((2, chips)),
    ]


def strips(rows, body):
    @pl.loop(0, rows // STRIP)
    def _(index):
        body(pl.ds(pl.multiple_of(index * STRIP, STRIP), STRIP))


def scatter_line(line, part, total, held, come, pair_send, pair_recv, send, recv):
    chips, z, core = line.chips, line.z, line.core
    rows = total.shape[0]

    def start_of(chip, which):
        return (2 * chip + which) * rows

    def across(chip):
        return pltpu.make_async_remote_copy(
            src_ref=part.at[pl.ds(start_of(chip, 1 - core), rows)],
            dst_ref=held.at[chip],
            send_sem=pair_send.at[chip],
            recv_sem=pair_recv.at[chip],
            device_id=line.at(z, 1 - core),
            device_id_type=MESH_IDS,
        )

    def hop(chip, up, target):
        way = 0 if up else 1
        return pltpu.make_async_remote_copy(
            src_ref=held.at[chip],
            dst_ref=come.at[way, chip],
            send_sem=send.at[way, chip],
            recv_sem=recv.at[way, chip],
            device_id=line.at(target, core),
            device_id_type=MESH_IDS,
        )

    def value(chip, strip, ways):
        first = start_of(chip, core)
        mine = part[pl.ds(pl.multiple_of(first + strip.start, STRIP), STRIP), :]
        summed = mine.astype(jnp.float32) + held[chip, strip, :].astype(jnp.float32)
        for way in ways:
            summed = summed + come[way, chip, strip, :].astype(jnp.float32)
        return summed

    def add(chip, ways):
        def body(strip):
            held[chip, strip, :] = value(chip, strip, ways).astype(jnp.bfloat16)

        strips(rows, body)

    order = []
    for near in range((chips + 1) // 2):
        for chip in (chips - 1 - near, near):
            if chip not in order:
                order.append(chip)
    for chip in order:
        across(chip).start()

    def forward(chip, up):
        across(chip).wait_recv()
        way = 0 if up else 1

        def with_arrival():
            hop(chip, up, z).wait_recv()
            add(chip, (way,))

        more = line.below if up else line.above
        pl.when(more)(with_arrival)
        pl.when(jnp.logical_not(more))(lambda: add(chip, ()))
        hop(chip, up, z + 1 if up else z - 1).start()

    def up_chip(step):
        return chips - 1 - step + z

    def down_chip(step):
        return step - (chips - 1 - z)

    def up_sends(step):
        return (z <= step) & line.above

    def down_sends(step):
        return (step >= chips - 1 - z) & line.below

    for step in range(chips - 1):
        pl.when(up_sends(step))(lambda step=step: forward(up_chip(step), True))
        pl.when(down_sends(step))(lambda step=step: forward(down_chip(step), False))

    across(z).wait_recv()
    pl.when(line.below)(lambda: hop(z, True, z).wait_recv())
    pl.when(line.above)(lambda: hop(z, False, z).wait_recv())

    def last(ways):
        def body(strip):
            total[strip, :] = value(z, strip, ways)

        strips(rows, body)

    inner = line.below & line.above
    pl.when(inner)(lambda: last((0, 1)))
    pl.when(jnp.logical_not(line.below))(lambda: last((1,)))
    pl.when(jnp.logical_not(line.above))(lambda: last((0,)))
    for chip in order:
        across(chip).wait_send()
    for step in range(chips - 1):
        pl.when(up_sends(step))(
            lambda step=step: hop(up_chip(step), True, z + 1).wait_send()
        )
        pl.when(down_sends(step))(
            lambda step=step: hop(down_chip(step), False, z - 1).wait_send()
        )


def gather_kernel(chips, own, out, *scratch):
    line = Line(chips)
    line.meet()
    gather_line(line, own, out, *scratch)


def middle_kernel(chips, part, hidden, gain, middle, normed_all, total, normed, *scratch):
    line = Line(chips)
    line.meet()
    scatter_line(line, part, total, *scratch[:6])

    def body(strip):
        rows = hidden[strip, :].astype(jnp.float32) + total[strip, :]
        middle[strip, :] = rows
        normed[strip, :] = (rows * rms_scale(rows) * gain[...]).astype(jnp.bfloat16)

    strips(hidden.shape[0], body)
    gather_line(line, normed, normed_all, *scratch[6:])


def branch_kernel(
    chips, part, middle, gain, out_grad, probs, collect, router,
    grad_middle, grad_all, heads, term, total, turned, *scratch
):
    line = Line(chips)
    line.meet()
    scatter_line(line, part, total, *scratch[:6])
    width = middle.shape[1]
    term[...] = jnp.zeros_like(term)

    def body(strip):
        tail = jnp.dot(
            total[strip, width:].astype(jnp.bfloat16), collect[...],
            preferred_element_type=jnp.float32,
        )
        prob = probs[strip, :]
        lane = lax.broadcasted_iota(jnp.int32, prob.shape, 1)
        inner = jnp.sum(jnp.where(lane > 0, prob * tail, 0.0), axis=1, keepdims=True)
        head = jnp.where(lane > 0, prob * (tail - inner), tail * prob * (1.0 - prob))
        head = head.astype(jnp.bfloat16)
        heads[strip, :] = head
        grad = total[strip, :width] + jnp.dot(
            head, router[...], preferred_element_type=jnp.float32
        )
        rows = middle[strip, :]
        scale = rms_scale(rows)
        weighted = grad * gain[...]
        mean = jnp.mean(weighted * rows, axis=-1, keepdims=True)
        term[...] += jnp.sum(grad * rows * scale, axis=0, keepdims=True)
        result = (
            out_grad[strip, :].astype(jnp.float32)
            + scale * weighted
            - rows * scale * scale * scale * mean
        )
        grad_middle[strip, :] = result
        turned[strip, :] = result.astype(jnp.bfloat16)

    strips(middle.shape[0], body)
    gather_line(line, turned, grad_all, *scratch[6:])


def input_kernel(chips, part, hidden, gain, grad_middle, input_grad, term, total, *scratch):
    line = Line(chips)
    line.meet()
    scatter_line(line, part, total, *scratch)
    term[...] = jnp.zeros_like(term)

    def body(strip):
        grad = total[strip, :]
        rows = hidden[strip, :].astype(jnp.float32)
        scale = rms_scale(rows)
        weighted = grad * gain[...]
        mean = jnp.mean(weighted * rows, axis=-1, keepdims=True)
        term[...] += jnp.sum(grad * rows * scale, axis=0, keepdims=True)
        result = (
            grad_middle[strip, :] + scale * weighted - rows * scale * scale * scale * mean
        )
        input_grad[strip, :] = result.astype(jnp.bfloat16)

    strips(hidden.shape[0], body)


def output_kernel(chips, part, middle, valid, output, total, *scratch):
    line = Line(chips)
    line.meet()
    scatter_line(line, part, total, *scratch)

    def body(strip):
        rows = valid[strip, :] * (middle[strip, :] + total[strip, :])
        output[strip, :] = rows.astype(jnp.bfloat16)

    strips(middle.shape[0], body)


def remote_call(kernel, chips, inputs, outputs, scratch, number, micros):
    moved = sum(a.size * a.dtype.itemsize for a in inputs)
    return pl.pallas_call(
        functools.partial(kernel, chips),
        out_shape=[jax.ShapeDtypeStruct(shape, kind) for shape, kind, _ in outputs],
        in_specs=[pl.BlockSpec(memory_space=pltpu.VMEM)] * len(inputs),
        out_specs=[
            pl.BlockSpec(memory_space=pl.ANY if far else pltpu.VMEM) for _, _, far in outputs
        ],
        scratch_shapes=scratch,
        compiler_params=pltpu.CompilerParams(collective_id=number, has_side_effects=True),
        cost_estimate=pl.CostEstimate(
            flops=int(micros * 1e9), bytes_accessed=moved, transcendentals=0
        ),
    )(*inputs)


def bf16(values):
    return values.astype(jnp.bfloat16)


def two_parts(values):
    high = lax.reduce_precision(values, exponent_bits=8, mantissa_bits=7)
    return (bf16(high), bf16(values - high))


def mm(left, right):
    return jnp.dot(left, right, preferred_element_type=jnp.float32)


def mm_nt(left, right):
    return lax.dot_general(
        left, right, (((1,), (1,)), ((), ())), preferred_element_type=jnp.float32
    )


def mm_tn(left, right):
    return lax.dot_general(
        left, right, (((0,), (0,)), ((), ())), preferred_element_type=jnp.float32
    )


def group_device(
    hidden_in,
    out_grad,
    lengths,
    routes,
    norm1_gain,
    qkv_weight,
    qkv_bias,
    out_weight,
    norm2_gain,
    router_weight,
    shared_gate,
    shared_in,
    shared_out,
    expert_in,
    expert_out,
):
    size = lax.axis_size("expert")
    parts = lax.axis_size("dp")
    me = lax.axis_index("expert")
    core = me % 2
    rows, width = hidden_in.shape
    group = rows * size
    heads = width // HD
    own_heads = heads // size
    half = parts // 2
    places = size // 2
    block = width // (parts * size)
    top = routes.shape[1]
    experts = router_weight.shape[1]
    score_scale = HD ** (-0.5)
    bias_cols = 3 * width // (parts * size) // block
    extra = 128
    shared_block = shared_out.shape[0]
    expert_block = expert_out.shape[1]
    pair_block = expert_block + shared_block
    hidden_units = parts * pair_block
    padded = -(-hidden_units // 128) * 128
    own_shared = parts * shared_block
    chips = places
    own_qkv = 3 * own_heads * HD

    def by_head(columns):
        count = columns.shape[0]
        cut = columns.reshape(count, 3, 2, half, places, HD)
        return cut.transpose(4, 2, 0, 1, 3, 5).reshape(size, count, own_qkv)

    def from_head(pieces):
        count = pieces.shape[1]
        cut = pieces.reshape(places, 2, count, 3, half, HD)
        return cut.transpose(2, 3, 1, 4, 0, 5).reshape(count, 3 * width)

    side = jnp.pad(bf16(routes), ((0, 0), (0, extra - top)))
    (gathered,) = remote_call(
        gather_kernel,
        chips,
        [jnp.concatenate([hidden_in, out_grad, side], axis=1)],
        [((group, 2 * width + extra), jnp.bfloat16, True)],
        gather_scratch(chips),
        0,
        70,
    )
    hidden_all = gathered[:, :width].astype(jnp.float32)
    routes_all = gathered[:, 2 * width : 2 * width + top].astype(jnp.int32)

    weight_down = lax.all_gather(
        jnp.concatenate([expert_out[0], shared_out], axis=0), "dp", axis=0, tiled=True
    )

    small = jnp.concatenate(
        [
            norm1_gain[:, None],
            norm2_gain[:, None],
            shared_gate[:, None],
            router_weight,
            qkv_bias.reshape(block, bias_cols),
        ],
        axis=1,
    )
    small = jnp.pad(small, ((0, 0), (0, extra - small.shape[1])))
    cut = shared_in.reshape(block, 2, parts, size, shared_block)
    cut = cut.transpose(3, 0, 1, 2, 4).reshape(size, block, 2 * own_shared)
    sent = jnp.concatenate(
        [by_head(qkv_weight), jnp.broadcast_to(small[None], (size, block, extra)), cut], axis=2
    )
    sent = lax.all_to_all(sent, "expert", split_axis=0, concat_axis=0, tiled=True)
    sent = sent.reshape(size * block, own_qkv + extra + 2 * own_shared)
    out_cols = width * block // (size * block)
    first = jnp.concatenate(
        [sent[:, : own_qkv + extra], out_weight.reshape(size * block, out_cols)], axis=1
    )
    first, weight_down = lax.optimization_barrier((first, weight_down))
    qkv_full = lax.all_gather(first, "dp", axis=0, tiled=True)
    weight_qkv = qkv_full[:, :own_qkv]
    small = qkv_full[:, own_qkv : own_qkv + extra]
    gain_one = small[:, 0].astype(jnp.float32)
    gain_two = small[:, 1].astype(jnp.float32)
    router_rows = jnp.pad(small[:, 2 : 3 + experts].T, ((0, 127 - experts), (0, 0)))
    bias_all = by_head(small[:, 3 + experts : 3 + experts + bias_cols].reshape(1, 3 * width))
    bias_own = lax.dynamic_index_in_dim(bias_all, me, 0, keepdims=False).astype(jnp.float32)

    cut = sent[:, own_qkv + extra :].reshape(size * block, 2, parts, shared_block)
    up = expert_in[0].reshape(size * block, 2, parts, expert_block)
    up = jnp.concatenate([up, cut], axis=3).reshape(size * block, 2, hidden_units)
    up = jnp.pad(up, ((0, 0), (0, 0), (0, padded - hidden_units)))
    up = up.reshape(size * block, 2 * padded)
    up, qkv_full = lax.optimization_barrier((up, qkv_full))
    weight_up = lax.all_gather(up, "dp", axis=0, tiled=True)

    swap = [(i, i ^ 1) for i in range(size)]

    def own_half(values):
        return lax.dynamic_slice_in_dim(values, core * half, half, 0)

    def other_half(values):
        return lax.dynamic_slice_in_dim(values, (1 - core) * half, half, 0)

    out_blocks = qkv_full[:, own_qkv + extra :].reshape(parts, block, width)
    kept = own_half(out_blocks)
    came = lax.ppermute(other_half(out_blocks), "expert", swap)
    weight_out = jnp.stack(
        [jnp.where(core == 0, kept, came), jnp.where(core == 0, came, kept)], axis=1
    ).reshape(own_heads * HD, width)

    segment, position = segment_table(lengths[0], group)
    valid_all = (segment < lengths.shape[1] - 1).astype(jnp.float32)[:, None]
    cosine, sine = rotary_tables(position, HD)
    allowed = (
        (segment[:, None] == segment[None, :]) & (position[:, None] >= position[None, :])
    )[None]
    normed_one = bf16(hidden_all * rms_scale(hidden_all) * gain_one)
    projected = mm(normed_one, weight_qkv) + bias_own
    split = projected.reshape(group, 3, own_heads, HD)
    query_low = bf16(rotate(split[:, 0], cosine, sine))
    key_low = bf16(rotate(split[:, 1], cosine, sine))
    value_low = bf16(split[:, 2])

    def score_rows():
        raw = (
            jnp.einsum("qhd,khd->hqk", query_low, key_low, preferred_element_type=jnp.float32)
            * score_scale
        )
        return jnp.where(allowed, raw, NEG_FILL)

    scores = score_rows()
    peak = jnp.max(scores, axis=-1, keepdims=True)
    log_total = peak + jnp.log(jnp.sum(jnp.exp(scores - peak), axis=-1, keepdims=True))
    weights_low = bf16(jnp.exp(scores - log_total))
    attended = bf16(
        jnp.einsum(
            "hqk,khd->qhd", weights_low, value_low, preferred_element_type=jnp.float32
        ).reshape(group, own_heads * HD)
    )
    middle, normed_all = remote_call(
        middle_kernel,
        chips,
        [bf16(mm(attended, weight_out)), hidden_in, gain_two[None, :]],
        [((rows, width), jnp.float32, False), ((group, width), jnp.bfloat16, True)],
        [pltpu.VMEM((rows, width), jnp.float32), pltpu.VMEM((rows, width), jnp.bfloat16)]
        + scatter_scratch(chips, rows, width)
        + gather_scratch(chips),
        1,
        70,
    )

    gate_logits = mm_nt(normed_all, router_rows)
    logits = gate_logits[:, 1 : 1 + experts]
    opener_all = jax.nn.sigmoid(gate_logits[:, :1])
    peak_logit = jnp.max(logits, axis=-1, keepdims=True)
    router_total = peak_logit + jnp.log(
        jnp.sum(jnp.exp(logits - peak_logit), axis=-1, keepdims=True)
    )
    probs_all = jnp.exp(logits - router_total)
    expert_ids = jnp.arange(experts, dtype=jnp.int32)
    mine = expert_ids[None, :] == me
    named = jnp.sum((routes_all == me).astype(jnp.float32), axis=1, keepdims=True)
    gate_own = named * jnp.sum(jnp.where(mine, probs_all, 0.0), axis=1, keepdims=True)

    routed_unit = (jnp.arange(hidden_units, dtype=jnp.int32) % pair_block < expert_block)[None, :]
    unit_scale = jnp.where(routed_unit, gate_own, opener_all)
    grad_rows = bf16(
        gathered[:, width : 2 * width].astype(jnp.float32) * valid_all
    )
    both_up = mm(normed_all, weight_up)

    gate_part = both_up[:, :hidden_units]
    up_part = both_up[:, padded : padded + hidden_units]
    hidden = bf16(jax.nn.silu(gate_part) * up_part)
    scaled_hidden = bf16(unit_scale * hidden.astype(jnp.float32))
    term_down = bf16(mm_tn(scaled_hidden, grad_rows))
    grad_down = lax.psum_scatter(term_down, "dp", scatter_dimension=0, tiled=True).astype(
        jnp.float32
    )
    grad_shared_out = grad_down[expert_block:]
    grad_expert_out = grad_down[None, :expert_block]
    combined = bf16(mm(scaled_hidden, weight_down))

    grad_hidden = mm_nt(grad_rows, weight_down)
    product = hidden.astype(jnp.float32) * grad_hidden
    dot_expert = named * jnp.sum(jnp.where(routed_unit, product, 0.0), axis=1, keepdims=True)
    dot_shared = jnp.sum(jnp.where(routed_unit, 0.0, product), axis=1, keepdims=True)
    grad_hidden = grad_hidden * unit_scale
    sigmoid_gate = jax.nn.sigmoid(gate_part)
    grad_gate = grad_hidden * up_part * sigmoid_gate * (1.0 + gate_part * (1.0 - sigmoid_gate))
    grad_up = grad_hidden * gate_part * sigmoid_gate
    wide = ((0, 0), (0, padded - hidden_units))
    grad_both_up = jnp.concatenate(
        [jnp.pad(bf16(grad_gate), wide), jnp.pad(bf16(grad_up), wide)], axis=1
    )
    term_up = bf16(mm_tn(normed_all, grad_both_up))
    up = lax.psum_scatter(term_up, "dp", scatter_dimension=0, tiled=True)
    up = up.reshape(size * block, 2, padded)[:, :, :hidden_units]
    up = up.reshape(size * block, 2, parts, pair_block)
    grad_expert_in = (
        up[:, :, :, :expert_block]
        .reshape(1, size * block, 2 * parts * expert_block)
        .astype(jnp.float32)
    )
    cut = lax.all_to_all(
        up[:, :, :, expert_block:].reshape(size, block, 2 * own_shared),
        "expert",
        split_axis=0,
        concat_axis=0,
        tiled=True,
    )
    grad_shared_in = (
        cut.reshape(size, block, 2, parts, shared_block)
        .transpose(1, 2, 3, 0, 4)
        .reshape(block, 2 * parts * size * shared_block)
        .astype(jnp.float32)
    )

    zero = jnp.zeros((), jnp.bfloat16)
    riders = jnp.concatenate(
        [
            jnp.where(mine, column, zero)
            for column in two_parts(dot_shared) + two_parts(dot_expert)
        ],
        axis=1,
    )
    riders = jnp.pad(riders, ((0, 0), (0, extra - riders.shape[1])))
    part = jnp.concatenate([bf16(mm_nt(grad_both_up, weight_up)), riders], axis=1)

    def rows_of(values):
        return lax.dynamic_slice_in_dim(values, me * rows, rows, 0)

    rider = jnp.arange(extra, dtype=jnp.int32)[:, None]
    lane = jnp.arange(128, dtype=jnp.int32)[None, :]
    collect = bf16(
        ((rider < 2 * experts) & (lane == 0))
        | ((rider >= 2 * experts) & (rider < 4 * experts) & (lane == 1 + rider % experts))
    )
    probs = jnp.pad(
        rows_of(jnp.concatenate([opener_all, probs_all], axis=1)), ((0, 0), (0, 127 - experts))
    )
    grad_middle, grad_branch, grad_heads, term_norm_two = remote_call(
        branch_kernel,
        chips,
        [part, middle, gain_two[None, :], rows_of(grad_rows), probs, collect, router_rows],
        [
            ((rows, width), jnp.float32, False),
            ((group, width), jnp.bfloat16, True),
            ((rows, 128), jnp.bfloat16, False),
            ((1, width), jnp.float32, False),
        ],
        [
            pltpu.VMEM((rows, width + extra), jnp.float32),
            pltpu.VMEM((rows, width), jnp.bfloat16),
        ]
        + scatter_scratch(chips, rows, width + extra)
        + gather_scratch(chips),
        2,
        75,
    )
    term_router = mm_tn(rows_of(normed_all), grad_heads)[:, : 1 + experts]

    grad_attended = bf16(mm_nt(grad_branch, weight_out)).reshape(group, own_heads, HD)
    weights_again = jnp.exp(score_rows() - log_total)
    grad_weights = jnp.einsum(
        "qhd,khd->hqk", grad_attended, value_low, preferred_element_type=jnp.float32
    )
    delta_rows = jnp.sum(weights_again * grad_weights, axis=-1, keepdims=True)
    grad_scores = bf16(weights_again * (grad_weights - delta_rows))
    grad_query_turned = (
        jnp.einsum("hqk,khd->qhd", grad_scores, key_low, preferred_element_type=jnp.float32)
        * score_scale
    )
    grad_key_turned = (
        jnp.einsum("hqk,qhd->khd", grad_scores, query_low, preferred_element_type=jnp.float32)
        * score_scale
    )
    grad_values = jnp.einsum(
        "hqk,qhd->khd", bf16(weights_again), grad_attended, preferred_element_type=jnp.float32
    )
    grad_projected = bf16(
        jnp.stack(
            [
                rotate_back(grad_query_turned, cosine, sine),
                rotate_back(grad_key_turned, cosine, sine),
                grad_values,
            ],
            axis=1,
        ).reshape(group, own_qkv)
    )
    input_grad, term_norm_one = remote_call(
        input_kernel,
        chips,
        [
            bf16(mm_nt(grad_projected, weight_qkv)),
            hidden_in,
            gain_one[None, :],
            grad_middle,
        ],
        [((rows, width), jnp.bfloat16, False), ((1, width), jnp.float32, False)],
        [pltpu.VMEM((rows, width), jnp.float32)] + scatter_scratch(chips, rows, width),
        3,
        40,
    )

    term_out = bf16(mm_tn(attended, grad_branch)).reshape(half, 2, block, width)
    kept = jnp.where(core == 0, term_out[:, 0], term_out[:, 1])
    given = jnp.where(core == 0, term_out[:, 1], term_out[:, 0])
    came = lax.ppermute(given, "expert", swap)
    out_blocks = jnp.concatenate(
        [jnp.where(core == 0, kept, came), jnp.where(core == 0, came, kept)], axis=0
    )
    term_qkv = mm_tn(normed_one, grad_projected)
    term_bias = jnp.sum(grad_projected.astype(jnp.float32), axis=0)
    bias_slots = jnp.where(jnp.arange(size)[:, None] == me, term_bias[None, :], 0.0)
    bias_rows = from_head(bias_slots[:, None, :]).reshape(width, bias_cols)
    small_terms = jnp.concatenate(
        [term_norm_one[0][:, None], term_norm_two[0][:, None], term_router, bias_rows], axis=1
    )
    count = small_terms.shape[1]
    small_high, small_low = two_parts(small_terms)
    small_terms = jnp.concatenate([small_high, small_low], axis=1)
    small_terms = jnp.pad(small_terms, ((0, 0), (0, extra - 2 * count)))
    back = lax.psum_scatter(
        jnp.concatenate(
            [bf16(term_qkv), small_terms, out_blocks.reshape(width, out_cols)], axis=1
        ),
        "dp",
        scatter_dimension=0,
        tiled=True,
    )
    grad_out_weight = back[:, own_qkv + extra :].reshape(block, width).astype(jnp.float32)
    back = lax.all_to_all(
        back[:, : own_qkv + extra].reshape(size, block, own_qkv + extra), "expert", split_axis=0, concat_axis=0, tiled=True
    ).astype(jnp.float32)
    grad_qkv = from_head(back[:, :, :own_qkv])
    small_sum = jnp.sum(back[:, :, own_qkv:], axis=0)
    small_sum = small_sum[:, :count] + small_sum[:, count : 2 * count]
    (output,) = remote_call(
        output_kernel,
        chips,
        [combined, middle, rows_of(valid_all)],
        [((rows, width), jnp.bfloat16, False)],
        [pltpu.VMEM((rows, width), jnp.float32)] + scatter_scratch(chips, rows, width),
        4,
        40,
    )
    grad_norm1 = small_sum[:, 0]
    grad_norm2 = small_sum[:, 1]
    grad_shared_gate = small_sum[:, 2]
    grad_router = small_sum[:, 3 : 3 + experts]
    grad_bias = small_sum[:, 3 + experts :].reshape(block * bias_cols)
    return (
        output,
        input_grad,
        grad_norm1,
        grad_qkv,
        grad_bias,
        grad_out_weight,
        grad_norm2,
        grad_router,
        grad_shared_gate,
        grad_shared_in,
        grad_shared_out,
        grad_expert_in,
        grad_expert_out,
    )


def solution(mesh):
    size, parts = mesh.shape["expert"], mesh.shape["dp"]

    def device(*arrays):
        block = arrays[5].shape[0]
        whole_heads = 2 * block == HD and parts % 2 == 0 and size % 2 == 0
        one_expert = arrays[13].shape[0] == 1
        if whole_heads and one_expert and arrays[5].shape[1] % (3 * size * HD) == 0:
            return group_device(*arrays)
        return per_device(*arrays)

    return jax.shard_map(
        device,
        mesh=mesh,
        in_specs=(
            P(("dp", "expert"), None),
            P(("dp", "expert"), None),
            P("dp", None),
            P(("dp", "expert"), None),
            P(("dp", "expert")),
            P(("dp", "expert"), None),
            P(("dp", "expert")),
            P(("dp", "expert"), None),
            P(("dp", "expert")),
            P(("dp", "expert"), None),
            P(("dp", "expert")),
            P(("dp", "expert"), None),
            P(("dp", "expert"), None),
            P("expert", "dp", None),
            P("expert", "dp", None),
        ),
        out_specs=(
            P(("dp", "expert"), None),
            P(("dp", "expert"), None),
            P(("dp", "expert")),
            P(("dp", "expert"), None),
            P(("dp", "expert")),
            P(("dp", "expert"), None),
            P(("dp", "expert")),
            P(("dp", "expert"), None),
            P(("dp", "expert")),
            P(("dp", "expert"), None),
            P(("dp", "expert"), None),
            P("expert", "dp", None),
            P("expert", "dp", None),
        ),
        check_vma=False,
    )
```

```python
import functools

import jax
import jax.numpy as jnp
from jax import lax
from jax.experimental import pallas as pl
from jax.experimental.pallas import tpu as pltpu
from jax.sharding import PartitionSpec as P

HD = 128


EPSILON = 1e-06
THETA = 1000000.0
NEG_FILL = -1e30


def rms_scale(values):
    return lax.rsqrt(jnp.mean(values * values, axis=-1, keepdims=True) + EPSILON)


def rotary_tables(positions, head_size):
    half_size = head_size // 2
    steps_up = jnp.arange(half_size, dtype=jnp.float32) * (2.0 / head_size)
    inverse = THETA ** (-steps_up)
    angles = positions.astype(jnp.float32)[:, None] * inverse[None, :]
    angles = jnp.concatenate([angles, angles], axis=-1)
    return (jnp.cos(angles)[:, None, :], jnp.sin(angles)[:, None, :])


def rotate(values, cosine, sine):
    half_size = values.shape[-1] // 2
    turned = jnp.concatenate([-values[..., half_size:], values[..., :half_size]], axis=-1)
    return values * cosine + turned * sine


def rotate_back(grad_values, cosine, sine):
    half_size = grad_values.shape[-1] // 2
    scaled = grad_values * sine
    turned = jnp.concatenate([scaled[..., half_size:], -scaled[..., :half_size]], axis=-1)
    return grad_values * cosine + turned


def swiglu(gate_up):
    half_size = gate_up.shape[-1] // 2
    return jax.nn.silu(gate_up[..., :half_size]) * gate_up[..., half_size:]


def swiglu_back(gate_up, grad_hidden):
    half_size = gate_up.shape[-1] // 2
    gate_part = gate_up[..., :half_size]
    up_part = gate_up[..., half_size:]
    sigmoid_gate = jax.nn.sigmoid(gate_part)
    grad_gate = grad_hidden * up_part * sigmoid_gate * (1.0 + gate_part * (1.0 - sigmoid_gate))
    grad_up = grad_hidden * gate_part * sigmoid_gate
    return jnp.concatenate([grad_gate, grad_up], axis=-1)


def norm_back(values, scale_rows, gain, grad_normed):
    weighted = grad_normed * gain
    inner = jnp.mean(weighted * values, axis=-1, keepdims=True)
    grad_values = scale_rows * weighted - values * scale_rows * scale_rows * scale_rows * inner
    grad_gain = jnp.sum(grad_normed * values * scale_rows, axis=0)
    return (grad_values, grad_gain)


def segment_table(length_row, count):
    ends = jnp.cumsum(length_row, dtype=jnp.int32)
    starts = ends - length_row
    places = jnp.arange(count, dtype=jnp.int32)
    segment = jnp.sum(
        (places[:, None] >= ends[None, :-1]).astype(jnp.int32), axis=1, dtype=jnp.int32
    )
    owners = segment[:, None] == jnp.arange(length_row.shape[0], dtype=jnp.int32)[None, :]
    first = jnp.sum(jnp.where(owners, starts[None, :], 0), axis=1, dtype=jnp.int32)
    return (segment, places - first)


def per_device(
    hidden_in,
    out_grad,
    lengths,
    routes,
    norm1_gain,
    qkv_weight,
    qkv_bias,
    out_weight,
    norm2_gain,
    router_weight,
    shared_gate,
    shared_in,
    shared_out,
    expert_in,
    expert_out,
):
    highest = lax.Precision.HIGHEST
    row_count, model_width = hidden_in.shape
    head_count = model_width // HD
    group_size = lax.axis_size("expert")
    group_rows = row_count * group_size
    top_count = routes.shape[1]
    expert_count = router_weight.shape[1]
    local_count = expert_in.shape[0]
    capacity = max(2, 2 * row_count * top_count // expert_count)
    slot_count = expert_count * capacity
    score_scale = HD ** (-0.5)
    dense = (
        lax.all_gather(norm1_gain, ("dp", "expert"), axis=0, tiled=True),
        lax.all_gather(qkv_weight, ("dp", "expert"), axis=0, tiled=True),
        lax.all_gather(qkv_bias, ("dp", "expert"), axis=0, tiled=True),
        lax.all_gather(out_weight, ("dp", "expert"), axis=0, tiled=True),
        lax.all_gather(norm2_gain, ("dp", "expert"), axis=0, tiled=True),
        lax.all_gather(router_weight, ("dp", "expert"), axis=0, tiled=True),
        lax.all_gather(shared_gate, ("dp", "expert"), axis=0, tiled=True),
        lax.all_gather(shared_in, ("dp", "expert"), axis=0, tiled=True),
        lax.all_gather(shared_out, ("dp", "expert"), axis=0, tiled=True),
    )
    (
        gain_first,
        weight_qkv,
        bias_first,
        weight_out,
        gain_second,
        weight_router,
        weight_gate,
        weight_shared_in,
        weight_shared_out,
    ) = dense
    weight_expert_in, weight_expert_out = (
        lax.all_gather(expert_in, "dp", axis=1, tiled=True),
        lax.all_gather(expert_out, "dp", axis=1, tiled=True),
    )
    segment_all, position_all = segment_table(lengths[0], group_rows)
    first_row = lax.axis_index("expert") * row_count
    segment_mine = lax.dynamic_slice_in_dim(segment_all, first_row, row_count, 0)
    position_mine = lax.dynamic_slice_in_dim(position_all, first_row, row_count, 0)
    valid_rows = (segment_mine < lengths.shape[1] - 1).astype(jnp.float32)[:, None]
    cosine, sine = rotary_tables(position_mine, HD)
    allowed = (
        (segment_mine[:, None] == segment_all[None, :])
        & (position_mine[:, None] >= position_all[None, :])
    )[None]
    inputs = hidden_in.astype(jnp.float32)
    scale_first = rms_scale(inputs)
    gain_one = gain_first.astype(jnp.float32)
    normed_one = (inputs * scale_first * gain_one).astype(jnp.bfloat16)
    projected = jnp.dot(
        normed_one, weight_qkv, preferred_element_type=jnp.float32
    ) + bias_first.astype(jnp.float32)
    query_low = rotate(
        projected[:, :model_width].reshape(row_count, head_count, HD), cosine, sine
    ).astype(jnp.bfloat16)
    key_low = rotate(
        projected[:, model_width : 2 * model_width].reshape(row_count, head_count, HD), cosine, sine
    ).astype(jnp.bfloat16)
    value_low = (
        projected[:, 2 * model_width :].reshape(row_count, head_count, HD).astype(jnp.bfloat16)
    )
    keys_all, values_all = (
        lax.all_gather(key_low, "expert", axis=0, tiled=True),
        lax.all_gather(value_low, "expert", axis=0, tiled=True),
    )

    def score_rows(queries):
        raw = (
            jnp.einsum("qhd,khd->hqk", queries, keys_all, preferred_element_type=jnp.float32)
            * score_scale
        )
        return jnp.where(allowed, raw, NEG_FILL)

    scores = score_rows(query_low)
    peak = jnp.max(scores, axis=-1, keepdims=True)
    log_total = peak + jnp.log(jnp.sum(jnp.exp(scores - peak), axis=-1, keepdims=True))
    weights_low = jnp.exp(scores - log_total).astype(jnp.bfloat16)
    attended = (
        jnp.einsum("hqk,khd->qhd", weights_low, values_all, preferred_element_type=jnp.float32)
        .reshape(row_count, model_width)
        .astype(jnp.bfloat16)
    )
    middle = inputs + jnp.dot(attended, weight_out, preferred_element_type=jnp.float32)
    scale_second = rms_scale(middle)
    gain_two = gain_second.astype(jnp.float32)
    normed_two = (middle * scale_second * gain_two).astype(jnp.bfloat16)
    logits = jnp.dot(normed_two, weight_router, preferred_element_type=jnp.float32)
    gate_logit = jnp.dot(normed_two, weight_gate, preferred_element_type=jnp.float32)
    peak_logit = jnp.max(logits, axis=-1, keepdims=True)
    router_total = peak_logit + jnp.log(
        jnp.sum(jnp.exp(logits - peak_logit), axis=-1, keepdims=True)
    )
    router_probs = jnp.exp(logits - router_total)
    expert_ids = jnp.arange(expert_count, dtype=jnp.int32)
    chosen = routes[:, :, None] == expert_ids[None, None, :]
    chosen_float = chosen.astype(jnp.float32)
    gates = jnp.sum(chosen_float * router_probs[:, None, :], axis=2)
    flat_hits = chosen.reshape(row_count * top_count, expert_count).astype(jnp.int32)
    earlier = jnp.cumsum(flat_hits, axis=0, dtype=jnp.int32) - flat_hits
    slot_rank = jnp.sum(earlier * flat_hits, axis=1, dtype=jnp.int32)
    slot_of = routes.reshape(-1) * capacity + slot_rank
    slot_hits = (
        (slot_of[:, None] == jnp.arange(slot_count, dtype=jnp.int32)[None, :])
        .reshape(row_count, top_count, slot_count)
        .astype(jnp.float32)
    )
    placement_map = jnp.sum(slot_hits, axis=1)
    weighted_map = jnp.sum(slot_hits * gates[:, :, None], axis=1)
    send_rows = (
        jnp.einsum(
            "ts,td->sd",
            placement_map.astype(jnp.bfloat16),
            normed_two,
            preferred_element_type=jnp.float32,
        )
        .astype(jnp.bfloat16)
        .reshape(expert_count, capacity, model_width)
    )
    arrived = lax.all_to_all(send_rows, "expert", split_axis=0, concat_axis=0, tiled=True)
    item_count = arrived.shape[1]
    grouped = arrived.reshape(group_size, local_count, item_count, model_width)
    gate_up = jnp.einsum(
        "gecd,edf->gecf", grouped, weight_expert_in, preferred_element_type=jnp.float32
    )
    hidden_low = swiglu(gate_up).astype(jnp.bfloat16)
    produced = jnp.einsum(
        "gecf,efd->gecd", hidden_low, weight_expert_out, preferred_element_type=jnp.float32
    ).astype(jnp.bfloat16)
    produced_rows = produced.reshape(group_size * local_count, item_count, model_width)
    expert_gate_up = gate_up.reshape(group_size * local_count, item_count, gate_up.shape[-1])
    back_rows = lax.all_to_all(produced_rows, "expert", split_axis=0, concat_axis=0, tiled=True)
    back_float = back_rows.reshape(slot_count, model_width).astype(jnp.float32)
    routed = jnp.dot(weighted_map, back_float, precision=highest)
    shared_up = jnp.dot(normed_two, weight_shared_in, preferred_element_type=jnp.float32)
    shared_hidden = swiglu(shared_up).astype(jnp.bfloat16)
    shared_rows = jnp.dot(shared_hidden, weight_shared_out, preferred_element_type=jnp.float32)
    opener = jax.nn.sigmoid(gate_logit)[:, None]
    output = (valid_rows * (middle + routed + opener * shared_rows)).astype(jnp.bfloat16)
    held = (
        lax.all_gather(norm1_gain, ("dp", "expert"), axis=0, tiled=True),
        lax.all_gather(qkv_weight, ("dp", "expert"), axis=0, tiled=True),
        lax.all_gather(qkv_bias, ("dp", "expert"), axis=0, tiled=True),
        lax.all_gather(out_weight, ("dp", "expert"), axis=0, tiled=True),
        lax.all_gather(norm2_gain, ("dp", "expert"), axis=0, tiled=True),
        lax.all_gather(router_weight, ("dp", "expert"), axis=0, tiled=True),
        lax.all_gather(shared_gate, ("dp", "expert"), axis=0, tiled=True),
        lax.all_gather(shared_in, ("dp", "expert"), axis=0, tiled=True),
        lax.all_gather(shared_out, ("dp", "expert"), axis=0, tiled=True),
    )
    (
        gain_first,
        weight_qkv,
        bias_first,
        weight_out,
        gain_second,
        weight_router,
        weight_gate,
        weight_shared_in,
        weight_shared_out,
    ) = held
    gain_one = gain_first.astype(jnp.float32)
    gain_two = gain_second.astype(jnp.float32)
    grad_rows = out_grad.astype(jnp.float32) * valid_rows
    grad_shared_rows = (grad_rows * opener).astype(jnp.bfloat16)
    grad_gate_logit = (
        jnp.sum(grad_rows * shared_rows, axis=-1) * opener[:, 0] * (1.0 - opener[:, 0])
    ).astype(jnp.bfloat16)
    grad_shared_hidden = jnp.einsum(
        "td,fd->tf", grad_shared_rows, weight_shared_out, preferred_element_type=jnp.float32
    )
    grad_shared_up = swiglu_back(shared_up, grad_shared_hidden).astype(jnp.bfloat16)
    term_shared_out = jnp.einsum(
        "tf,td->fd", shared_hidden, grad_shared_rows, preferred_element_type=jnp.float32
    )
    term_shared_in = jnp.einsum(
        "td,tf->df", normed_two, grad_shared_up, preferred_element_type=jnp.float32
    )
    slot_product = jnp.einsum("td,sd->ts", grad_rows, back_float, precision=highest)
    grad_gates = jnp.sum(slot_hits * slot_product[:, None, :], axis=2)
    grad_probs = jnp.sum(chosen_float * grad_gates[:, :, None], axis=1)
    grad_logits = (
        router_probs * (grad_probs - jnp.sum(router_probs * grad_probs, axis=-1, keepdims=True))
    ).astype(jnp.bfloat16)
    term_router = jnp.einsum(
        "td,te->de", normed_two, grad_logits, preferred_element_type=jnp.float32
    )
    term_gate = jnp.einsum(
        "td,t->d", normed_two, grad_gate_logit, preferred_element_type=jnp.float32
    )
    grad_result = (
        jnp.einsum("ts,td->sd", weighted_map, grad_rows, precision=highest)
        .astype(jnp.bfloat16)
        .reshape(expert_count, capacity, model_width)
    )
    grad_arrived = lax.all_to_all(grad_result, "expert", split_axis=0, concat_axis=0, tiled=True)
    grad_grouped = grad_arrived.reshape(group_size, local_count, capacity, model_width)
    gate_up_grouped = expert_gate_up.reshape(
        group_size, local_count, capacity, expert_gate_up.shape[-1]
    )
    hidden_again = swiglu(gate_up_grouped).astype(jnp.bfloat16)
    grad_hidden = jnp.einsum(
        "gecd,efd->gecf", grad_grouped, weight_expert_out, preferred_element_type=jnp.float32
    )
    grad_gate_up = swiglu_back(gate_up_grouped, grad_hidden).astype(jnp.bfloat16)
    arrived_grouped = arrived.reshape(group_size, local_count, capacity, model_width)
    term_expert_in = jnp.einsum(
        "gecd,gecf->edf", arrived_grouped, grad_gate_up, preferred_element_type=jnp.float32
    )
    term_expert_out = jnp.einsum(
        "gecf,gecd->efd", hidden_again, grad_grouped, preferred_element_type=jnp.float32
    )
    grad_sent = jnp.einsum(
        "gecf,edf->gecd", grad_gate_up, weight_expert_in, preferred_element_type=jnp.float32
    ).reshape(group_size * local_count, capacity, model_width)
    grad_slots = lax.all_to_all(
        grad_sent.astype(jnp.bfloat16), "expert", split_axis=0, concat_axis=0, tiled=True
    ).astype(grad_sent.dtype)
    grad_expert_in, grad_expert_out = (
        lax.psum_scatter(
            term_expert_in.astype(jnp.bfloat16), "dp", scatter_dimension=1, tiled=True
        ).astype(jnp.float32),
        lax.psum_scatter(
            term_expert_out.astype(jnp.bfloat16), "dp", scatter_dimension=1, tiled=True
        ).astype(jnp.float32),
    )
    grad_normed_two = jnp.einsum(
        "te,de->td", grad_logits, weight_router, preferred_element_type=jnp.float32
    )
    grad_normed_two = (
        grad_normed_two
        + grad_gate_logit.astype(jnp.float32)[:, None] * weight_gate.astype(jnp.float32)[None, :]
    )
    grad_normed_two = grad_normed_two + jnp.einsum(
        "tf,df->td", grad_shared_up, weight_shared_in, preferred_element_type=jnp.float32
    )
    grad_normed_two = grad_normed_two + jnp.dot(
        placement_map, grad_slots.reshape(slot_count, model_width), precision=highest
    )
    grad_middle_norm, term_norm_two = norm_back(middle, scale_second, gain_two, grad_normed_two)
    grad_middle = grad_rows + grad_middle_norm
    grad_norm2, grad_router, grad_shared_gate, grad_shared_in, grad_shared_out = (
        lax.psum_scatter(term_norm_two, ("dp", "expert"), scatter_dimension=0, tiled=True),
        lax.psum_scatter(term_router, ("dp", "expert"), scatter_dimension=0, tiled=True),
        lax.psum_scatter(term_gate, ("dp", "expert"), scatter_dimension=0, tiled=True),
        lax.psum_scatter(term_shared_in, ("dp", "expert"), scatter_dimension=0, tiled=True),
        lax.psum_scatter(term_shared_out, ("dp", "expert"), scatter_dimension=0, tiled=True),
    )
    grad_branch = grad_middle.astype(jnp.bfloat16)
    term_out_weight = jnp.einsum(
        "td,te->de", attended, grad_branch, preferred_element_type=jnp.float32
    )
    grad_attended = (
        jnp.einsum("te,de->td", grad_branch, weight_out, preferred_element_type=jnp.float32)
        .astype(jnp.bfloat16)
        .reshape(row_count, head_count, HD)
    )
    weights_again = jnp.exp(score_rows(query_low) - log_total)
    weights_again_low = weights_again.astype(jnp.bfloat16)
    grad_weights = jnp.einsum(
        "qhd,khd->hqk", grad_attended, values_all, preferred_element_type=jnp.float32
    )
    delta_rows = jnp.sum(weights_again * grad_weights, axis=-1, keepdims=True)
    grad_scores = (weights_again * (grad_weights - delta_rows)).astype(jnp.bfloat16)
    grad_query_turned = (
        jnp.einsum("hqk,khd->qhd", grad_scores, keys_all, preferred_element_type=jnp.float32)
        * score_scale
    )
    grad_keys_all = (
        jnp.einsum("hqk,qhd->khd", grad_scores, query_low, preferred_element_type=jnp.float32)
        * score_scale
    )
    grad_values_all = jnp.einsum(
        "hqk,qhd->khd", weights_again_low, grad_attended, preferred_element_type=jnp.float32
    )
    grad_key_turned, grad_values = (
        lax.psum_scatter(
            grad_keys_all.astype(jnp.bfloat16), "expert", scatter_dimension=0, tiled=True
        ).astype(jnp.float32),
        lax.psum_scatter(
            grad_values_all.astype(jnp.bfloat16), "expert", scatter_dimension=0, tiled=True
        ).astype(jnp.float32),
    )
    grad_projected = jnp.concatenate(
        [
            rotate_back(grad_query_turned, cosine, sine).reshape(row_count, model_width),
            rotate_back(grad_key_turned, cosine, sine).reshape(row_count, model_width),
            grad_values.reshape(row_count, model_width),
        ],
        axis=-1,
    ).astype(jnp.bfloat16)
    term_bias = jnp.sum(grad_projected.astype(jnp.float32), axis=0)
    term_qkv = jnp.einsum(
        "td,tf->df", normed_one, grad_projected, preferred_element_type=jnp.float32
    )
    grad_normed_one = jnp.einsum(
        "tf,df->td", grad_projected, weight_qkv, preferred_element_type=jnp.float32
    )
    grad_input_norm, term_norm_one = norm_back(inputs, scale_first, gain_one, grad_normed_one)
    input_grad = (grad_middle + grad_input_norm).astype(jnp.bfloat16)
    grad_norm1, grad_qkv, grad_bias, grad_out_weight = (
        lax.psum_scatter(term_norm_one, ("dp", "expert"), scatter_dimension=0, tiled=True),
        lax.psum_scatter(term_qkv, ("dp", "expert"), scatter_dimension=0, tiled=True),
        lax.psum_scatter(term_bias, ("dp", "expert"), scatter_dimension=0, tiled=True),
        lax.psum_scatter(term_out_weight, ("dp", "expert"), scatter_dimension=0, tiled=True),
    )
    return (
        output,
        input_grad,
        grad_norm1,
        grad_qkv,
        grad_bias,
        grad_out_weight,
        grad_norm2,
        grad_router,
        grad_shared_gate,
        grad_shared_in,
        grad_shared_out,
        grad_expert_in,
        grad_expert_out,
    )


MESH_IDS = pl.DeviceIdType.MESH
STRIP = 16


class Line:
    def __init__(self, chips, wide):
        me = lax.axis_index("expert")
        group = lax.axis_index("dp")
        self.chips = chips
        self.wide = wide
        self.z = me // 2
        self.core = lax.rem(me, 2)
        self.x = lax.rem(group, 2)
        self.group = group
        self.below = self.z > 0
        self.above = self.z < chips - 1

    def at(self, z, core):
        return {"expert": 2 * z + core}

    def beside(self):
        return {"dp": self.group + 1 - 2 * self.x, "expert": 2 * self.z + self.core}

    def meet(self):
        barrier = pltpu.get_barrier_semaphore()

        def hello(target):
            pl.semaphore_signal(barrier, inc=1, device_id=target, device_id_type=MESH_IDS)

        hello(self.at(self.z, 1 - self.core))
        pl.when(self.above)(lambda: hello(self.at(self.z + 1, self.core)))
        pl.when(self.below)(lambda: hello(self.at(self.z - 1, self.core)))
        if self.wide:
            hello(self.beside())
        peers = 1 + jnp.minimum(self.z, 1) + jnp.minimum(self.chips - 1 - self.z, 1)
        pl.semaphore_wait(barrier, peers + (1 if self.wide else 0))


def gather_scratch(chips, wide):
    items = 2 * chips - 1
    pair = [pltpu.SemaphoreType.DMA((items,)) for _ in range(6 if wide else 2)]
    return [
        pltpu.SemaphoreType.DMA((2, chips - 1)),
        pltpu.SemaphoreType.DMA((2, chips - 1)),
        pltpu.SemaphoreType.DMA,
    ] + pair


class Gather:
    def __init__(self, line, own, out, scratch):
        self.line, self.own, self.out = line, own, out
        self.send, self.recv, self.local = scratch[:3]
        self.pair = scratch[3:]
        self.wide = len(self.pair) == 6
        self.rows = own.shape[0]

    def block(self, group, chip, which):
        place = 2 * chip + which
        if self.wide:
            place = place + group * (2 * self.line.chips)
        return self.out.at[pl.ds(place * self.rows, self.rows)]

    def mine(self, chip, which):
        return self.block(self.line.x, chip, which)

    def theirs(self, chip, which):
        return self.block(1 - self.line.x, chip, which)

    def origin(self, step, up):
        return self.line.z - step if up else self.line.z + step

    def hop(self, step, up):
        z, core = self.line.z, self.line.core
        origin = self.origin(step, up)
        return pltpu.make_async_remote_copy(
            src_ref=self.own if step == 0 else self.mine(origin, core),
            dst_ref=self.mine(origin, core),
            send_sem=self.send.at[0 if up else 1, step],
            recv_sem=self.recv.at[0 if up else 1, step],
            device_id=self.line.at(z + 1 if up else z - 1, core),
            device_id_type=MESH_IDS,
        )

    def arrival(self, step, up):
        z, core = self.line.z, self.line.core
        return pltpu.make_async_remote_copy(
            src_ref=self.own,
            dst_ref=self.mine(self.origin(step + 1, up), core),
            send_sem=self.send.at[0 if up else 1, step],
            recv_sem=self.recv.at[0 if up else 1, step],
            device_id=self.line.at(z - 1 if up else z + 1, core),
            device_id_type=MESH_IDS,
        )

    def across(self, index, source, target, kind):
        line = self.line
        return pltpu.make_async_remote_copy(
            src_ref=source,
            dst_ref=target,
            send_sem=self.pair[2 * kind].at[index],
            recv_sem=self.pair[2 * kind + 1].at[index],
            device_id=line.beside() if kind == 1 else line.at(line.z, 1 - line.core),
            device_id_type=MESH_IDS,
        )

    def sends(self, step, up):
        line = self.line
        if up:
            return (line.z >= step) & line.above
        return (line.z + step <= line.chips - 1) & line.below

    def items(self):
        line = self.line
        found = [(0, line.z, None)]
        for step in range(line.chips - 1):
            found.append((1 + step, line.z - 1 - step, line.z - 1 - step >= 0))
            found.append(
                (line.chips + step, line.z + 1 + step, line.z + 1 + step <= line.chips - 1)
            )
        return found

    def spread(self, index, origin, source):
        core = self.line.core
        self.across(index, source, self.mine(origin, core), 0).start()
        if self.wide:
            self.across(index, source, self.mine(origin, core), 1).start()

    def begin(self):
        line = self.line
        pltpu.make_async_copy(self.own, self.mine(line.z, line.core), self.local).start()

    def push(self, step):
        line = self.line
        for up in (True, False):
            pl.when(self.sends(step, up))(lambda up=up: self.hop(step, up).start())
        if step == 0:
            self.spread(0, line.z, self.own)

    def pull(self, step):
        for index, origin, comes in self.items():
            if index not in (1 + step, self.line.chips + step):
                continue

            def take(index=index, origin=origin):
                self.arrival(step, index < self.line.chips).wait_recv()
                self.spread(index, origin, self.mine(origin, self.line.core))

            pl.when(comes)(take)

    def end(self):
        line, core = self.line, self.line.core

        def each(act):
            for index, origin, comes in self.items():
                if comes is None:
                    act(index, origin)
                else:
                    pl.when(comes)(lambda index=index, origin=origin: act(index, origin))

        def turn(index, origin):
            landed = self.theirs(origin, core)
            self.across(index, landed, landed, 1).wait_recv()
            self.across(index, landed, landed, 2).start()

        def settle(index, origin):
            here = self.mine(origin, core)
            self.across(index, here, here, 0).wait_send()
            self.across(index, here, self.mine(origin, 1 - core), 0).wait_recv()
            if self.wide:
                there = self.theirs(origin, core)
                self.across(index, here, here, 1).wait_send()
                self.across(index, there, there, 2).wait_send()
                self.across(index, there, self.theirs(origin, 1 - core), 2).wait_recv()

        if self.wide:
            each(turn)
        each(settle)
        for step in range(line.chips - 1):
            for up in (True, False):
                pl.when(self.sends(step, up))(
                    lambda step=step, up=up: self.hop(step, up).wait_send()
                )
        pltpu.make_async_copy(self.own, self.mine(line.z, core), self.local).wait()


def gather_lines(*gathers):
    chips = gathers[0].line.chips
    for one in gathers:
        one.begin()
    for step in range(chips - 1):
        for one in gathers:
            one.push(step)
        for one in gathers:
            one.pull(step)
    for one in gathers:
        one.end()


def scatter_scratch(chips, rows, width, wide):
    groups = 2 if wide else 1
    found = [
        pltpu.VMEM((groups, chips, rows, width), jnp.bfloat16),
        pltpu.VMEM((2, chips, rows, width), jnp.bfloat16),
        pltpu.SemaphoreType.DMA((groups, chips)),
        pltpu.SemaphoreType.DMA((groups, chips)),
        pltpu.SemaphoreType.DMA((2, chips)),
        pltpu.SemaphoreType.DMA((2, chips)),
    ]
    if wide:
        found += [
            pltpu.VMEM((chips, rows, width), jnp.bfloat16),
            pltpu.SemaphoreType.DMA((chips,)),
            pltpu.SemaphoreType.DMA((chips,)),
        ]
    return found


def strips(rows, body):
    @pl.loop(0, rows // STRIP)
    def _(index):
        body(pl.ds(pl.multiple_of(index * STRIP, STRIP), STRIP))


def scatter_line(line, part, total, scratch):
    chips, z, core = line.chips, line.z, line.core
    rows = total.shape[0]
    held, come, pair_send, pair_recv, send, recv = scratch[:6]
    wide = len(scratch) == 9
    if wide:
        aside, side_send, side_recv = scratch[6:]

    def start_of(other, chip, which):
        place = 2 * chip + which
        if wide:
            place = place + (1 - line.x if other else line.x) * (2 * chips)
        return place * rows

    def across(other, chip):
        return pltpu.make_async_remote_copy(
            src_ref=part.at[pl.ds(start_of(other, chip, 1 - core), rows)],
            dst_ref=held.at[other, chip],
            send_sem=pair_send.at[other, chip],
            recv_sem=pair_recv.at[other, chip],
            device_id=line.at(z, 1 - core),
            device_id_type=MESH_IDS,
        )

    def beside(chip):
        return pltpu.make_async_remote_copy(
            src_ref=held.at[1, chip],
            dst_ref=aside.at[chip],
            send_sem=side_send.at[chip],
            recv_sem=side_recv.at[chip],
            device_id=line.beside(),
            device_id_type=MESH_IDS,
        )

    def hop(chip, up, target):
        way = 0 if up else 1
        return pltpu.make_async_remote_copy(
            src_ref=held.at[0, chip],
            dst_ref=come.at[way, chip],
            send_sem=send.at[way, chip],
            recv_sem=recv.at[way, chip],
            device_id=line.at(target, core),
            device_id_type=MESH_IDS,
        )

    def value(other, chip, strip, ways):
        first = start_of(other, chip, core)
        mine = part[pl.ds(pl.multiple_of(first + strip.start, STRIP), STRIP), :]
        summed = mine.astype(jnp.float32) + held[other, chip, strip, :].astype(jnp.float32)
        if wide and other == 0:
            summed = summed + aside[chip, strip, :].astype(jnp.float32)
        for way in ways:
            summed = summed + come[way, chip, strip, :].astype(jnp.float32)
        return summed

    def add(other, chip, ways):
        def body(strip):
            held[other, chip, strip, :] = value(other, chip, strip, ways).astype(jnp.bfloat16)

        strips(rows, body)

    def up_chip(step):
        return chips - 1 - step + z

    def down_chip(step):
        return step - (chips - 1 - z)

    def up_sends(step):
        return (z <= step) & line.above

    def down_sends(step):
        return (step >= chips - 1 - z) & line.below

    def each(act):
        for step in range(chips - 1):
            pl.when(up_sends(step))(lambda step=step: act(up_chip(step), True))
            pl.when(down_sends(step))(lambda step=step: act(down_chip(step), False))

    if wide:
        each(lambda chip, up: across(1, chip).start())
        across(1, z).start()
    each(lambda chip, up: across(0, chip).start())
    across(0, z).start()

    def give(chip):
        across(1, chip).wait_recv()
        add(1, chip, ())
        beside(chip).start()

    if wide:
        each(lambda chip, up: give(chip))
        give(z)

    def ready(chip):
        across(0, chip).wait_recv()
        if wide:
            beside(chip).wait_recv()

    def forward(chip, up):
        ready(chip)
        way = 0 if up else 1

        def with_arrival():
            hop(chip, up, z).wait_recv()
            add(0, chip, (way,))

        more = line.below if up else line.above
        pl.when(more)(with_arrival)
        pl.when(jnp.logical_not(more))(lambda: add(0, chip, ()))
        hop(chip, up, z + 1 if up else z - 1).start()

    each(forward)
    ready(z)
    pl.when(line.below)(lambda: hop(z, True, z).wait_recv())
    pl.when(line.above)(lambda: hop(z, False, z).wait_recv())

    def last(ways):
        def body(strip):
            total[strip, :] = value(0, z, strip, ways)

        strips(rows, body)

    pl.when(line.below & line.above)(lambda: last((0, 1)))
    pl.when(jnp.logical_not(line.below))(lambda: last((1,)))
    pl.when(jnp.logical_not(line.above))(lambda: last((0,)))

    def settle(chip):
        across(0, chip).wait_send()
        if wide:
            across(1, chip).wait_send()
            beside(chip).wait_send()

    def settle_hop(chip, up):
        settle(chip)
        hop(chip, up, z + 1 if up else z - 1).wait_send()

    each(settle_hop)
    settle(z)


def gather_kernel(chips, near, far, near_all, far_all, *scratch):
    line = Line(chips, True)
    line.meet()
    gather_lines(
        Gather(line, near, near_all, scratch[:5]), Gather(line, far, far_all, scratch[5:])
    )


def middle_kernel(chips, part, hidden, gain, middle, normed_all, total, normed, *scratch):
    line = Line(chips, True)
    line.meet()
    scatter_line(line, part, total, scratch[:6])

    def body(strip):
        rows = hidden[strip, :].astype(jnp.float32) + total[strip, :]
        middle[strip, :] = rows
        normed[strip, :] = (rows * rms_scale(rows) * gain[...]).astype(jnp.bfloat16)

    strips(hidden.shape[0], body)
    gather_lines(Gather(line, normed, normed_all, scratch[6:]))


def branch_kernel(
    chips, part, middle, gain, out_grad, probs, collect, router,
    grad_middle, grad_all, heads, term, total, turned, *scratch
):
    line = Line(chips, True)
    line.meet()
    scatter_line(line, part, total, scratch[:9])
    width = middle.shape[1]
    term[...] = jnp.zeros_like(term)

    def body(strip):
        tail = jnp.dot(
            total[strip, width:].astype(jnp.bfloat16), collect[...],
            preferred_element_type=jnp.float32,
        )
        prob = probs[strip, :]
        lane = lax.broadcasted_iota(jnp.int32, prob.shape, 1)
        inner = jnp.sum(jnp.where(lane > 0, prob * tail, 0.0), axis=1, keepdims=True)
        head = jnp.where(lane > 0, prob * (tail - inner), tail * prob * (1.0 - prob))
        head = head.astype(jnp.bfloat16)
        heads[strip, :] = head
        grad = total[strip, :width] + jnp.dot(
            head, router[...], preferred_element_type=jnp.float32
        )
        rows = middle[strip, :]
        scale = rms_scale(rows)
        weighted = grad * gain[...]
        mean = jnp.mean(weighted * rows, axis=-1, keepdims=True)
        term[...] += jnp.sum(grad * rows * scale, axis=0, keepdims=True)
        result = (
            out_grad[strip, :].astype(jnp.float32)
            + scale * weighted
            - rows * scale * scale * scale * mean
        )
        grad_middle[strip, :] = result
        turned[strip, :] = result.astype(jnp.bfloat16)

    strips(middle.shape[0], body)
    gather_lines(Gather(line, turned, grad_all, scratch[9:]))


def input_kernel(chips, part, hidden, gain, grad_middle, input_grad, term, total, *scratch):
    line = Line(chips, False)
    line.meet()
    scatter_line(line, part, total, scratch)
    term[...] = jnp.zeros_like(term)

    def body(strip):
        grad = total[strip, :]
        rows = hidden[strip, :].astype(jnp.float32)
        scale = rms_scale(rows)
        weighted = grad * gain[...]
        mean = jnp.mean(weighted * rows, axis=-1, keepdims=True)
        term[...] += jnp.sum(grad * rows * scale, axis=0, keepdims=True)
        result = (
            grad_middle[strip, :] + scale * weighted - rows * scale * scale * scale * mean
        )
        input_grad[strip, :] = result.astype(jnp.bfloat16)

    strips(hidden.shape[0], body)


def output_kernel(chips, part, middle, valid, output, total, *scratch):
    line = Line(chips, True)
    line.meet()
    scatter_line(line, part, total, scratch)

    def body(strip):
        rows = valid[strip, :] * (middle[strip, :] + total[strip, :])
        output[strip, :] = rows.astype(jnp.bfloat16)

    strips(middle.shape[0], body)


def remote_call(kernel, chips, inputs, outputs, scratch, number, micros):
    moved = sum(a.size * a.dtype.itemsize for a in inputs)
    return pl.pallas_call(
        functools.partial(kernel, chips),
        out_shape=[jax.ShapeDtypeStruct(shape, kind) for shape, kind, _ in outputs],
        in_specs=[pl.BlockSpec(memory_space=pltpu.VMEM)] * len(inputs),
        out_specs=[
            pl.BlockSpec(memory_space=pl.ANY if far else pltpu.VMEM) for _, _, far in outputs
        ],
        scratch_shapes=scratch,
        compiler_params=pltpu.CompilerParams(collective_id=number, has_side_effects=True),
        cost_estimate=pl.CostEstimate(
            flops=int(micros * 1e9), bytes_accessed=moved, transcendentals=0
        ),
    )(*inputs)

def bf16(values):
    return values.astype(jnp.bfloat16)


def two_parts(values):
    high = lax.reduce_precision(values, exponent_bits=8, mantissa_bits=7)
    return (bf16(high), bf16(values - high))


def mm(left, right):
    return jnp.dot(left, right, preferred_element_type=jnp.float32)


def mm_nt(left, right):
    return lax.dot_general(
        left, right, (((1,), (1,)), ((), ())), preferred_element_type=jnp.float32
    )


def mm_tn(left, right):
    return lax.dot_general(
        left, right, (((0,), (0,)), ((), ())), preferred_element_type=jnp.float32
    )


def group_device(
    hidden_in,
    out_grad,
    lengths,
    routes,
    norm1_gain,
    qkv_weight,
    qkv_bias,
    out_weight,
    norm2_gain,
    router_weight,
    shared_gate,
    shared_in,
    shared_out,
    expert_in,
    expert_out,
):
    size = lax.axis_size("expert")
    parts = lax.axis_size("dp")
    me = lax.axis_index("expert")
    core = me % 2
    rows, width = hidden_in.shape
    group = rows * size
    heads = width // HD
    own_heads = heads // size
    half = parts // 2
    places = size // 2
    block = width // (parts * size)
    top = routes.shape[1]
    experts = router_weight.shape[1]
    score_scale = HD ** (-0.5)
    bias_cols = 3 * width // (parts * size) // block
    extra = 128
    shared_block = shared_out.shape[0]
    expert_block = expert_out.shape[1]
    pair_block = expert_block + shared_block
    hidden_units = half * pair_block
    own_shared = parts * shared_block
    chips = places
    data = lax.axis_index("dp")
    side_by = data % 2
    above = data // 2
    slots = 2 * size
    slot = side_by * size + me
    swap_side = [(g, g ^ 1) for g in range(parts)]
    swap_above = [(g, g ^ 2) for g in range(parts)]
    own_qkv = 3 * own_heads * HD

    def by_head(columns):
        count = columns.shape[0]
        cut = columns.reshape(count, 3, 2, half, places, HD)
        return cut.transpose(4, 2, 0, 1, 3, 5).reshape(size, count, own_qkv)

    def from_head(pieces):
        count = pieces.shape[1]
        cut = pieces.reshape(places, 2, count, 3, half, HD)
        return cut.transpose(2, 3, 1, 4, 0, 5).reshape(count, 3 * width)

    def ordered(which, own, other, axis):
        first = jnp.where(which == 0, own, other)
        second = jnp.where(which == 0, other, own)
        return jnp.concatenate([first, second], axis=axis)

    def rows_of(values, first):
        return lax.dynamic_slice_in_dim(values, first * rows, rows, 0)

    small = jnp.concatenate(
        [
            norm1_gain[:, None],
            norm2_gain[:, None],
            shared_gate[:, None],
            router_weight,
            qkv_bias.reshape(block, bias_cols),
        ],
        axis=1,
    )
    small = jnp.pad(small, ((0, 0), (0, extra - small.shape[1])))
    first = jnp.concatenate(
        [by_head(qkv_weight), jnp.broadcast_to(small[None], (size, block, extra))], axis=2
    )
    first = lax.all_to_all(first, "expert", split_axis=0, concat_axis=0, tiled=True)
    first = first.reshape(size * block, own_qkv + extra)
    out_cols = width * block // (size * block)
    qkv_full = lax.all_gather(
        jnp.concatenate([first, out_weight.reshape(size * block, out_cols)], axis=1),
        "dp",
        axis=0,
        tiled=True,
    )

    down = jnp.concatenate([expert_out[0], shared_out], axis=0)
    down_came = lax.ppermute(down, "dp", swap_above)

    def units(values, count):
        cut = values.reshape(size * block, 2, half, 2, count)
        return cut.transpose(3, 1, 2, 4, 0).reshape(2, 2 * half * count, size * block)

    def aside(values):
        kept = lax.dynamic_index_in_dim(values, side_by, 0, keepdims=False)
        given = lax.dynamic_index_in_dim(values, 1 - side_by, 0, keepdims=False)
        return kept, lax.ppermute(given, "dp", swap_side)

    routed_kept, routed_came = aside(units(expert_in[0], expert_block))

    segment, position = segment_table(lengths[0], group)
    valid_all = (segment < lengths.shape[1] - 1).astype(jnp.float32)[:, None]
    valid_rows = rows_of(valid_all, me)
    grad_own = bf16(out_grad.astype(jnp.float32) * valid_rows)
    side = jnp.pad(bf16(routes), ((0, 0), (0, extra - top)))
    far = jnp.concatenate([grad_own, side], axis=1)
    far, first = lax.optimization_barrier((far, first))
    hidden_all, far_all = remote_call(
        gather_kernel,
        chips,
        [hidden_in, far],
        [
            ((group, width), jnp.bfloat16, True),
            ((2 * group, width + extra), jnp.bfloat16, True),
        ],
        gather_scratch(chips, False) + gather_scratch(chips, True),
        0,
        75,
    )
    hidden_all, far_all, routed_came, down_came = lax.optimization_barrier(
        (hidden_all, far_all, routed_came, down_came)
    )
    weight_down = ordered(above, down, down_came, 0)
    routed_up = ordered(side_by, routed_kept, routed_came, 1)
    routed_came = lax.ppermute(routed_up, "dp", swap_above)

    cut = shared_in.reshape(block, 2, parts, size, shared_block)
    cut = cut.transpose(3, 0, 1, 2, 4).reshape(size, block, 2 * own_shared)
    cut, hidden_all = lax.optimization_barrier((cut, hidden_all))
    cut = lax.all_to_all(cut, "expert", split_axis=0, concat_axis=0, tiled=True)
    hidden_all = hidden_all.astype(jnp.float32)
    grad_rows = far_all[:, :width]
    routes_all = far_all[:, width : width + top].astype(jnp.int32)

    weight_qkv = qkv_full[:, :own_qkv]
    small = qkv_full[:, own_qkv : own_qkv + extra]
    gain_one = small[:, 0].astype(jnp.float32)
    gain_two = small[:, 1].astype(jnp.float32)
    router_rows = jnp.pad(small[:, 2 : 3 + experts].T, ((0, 127 - experts), (0, 0)))
    bias_all = by_head(small[:, 3 + experts : 3 + experts + bias_cols].reshape(1, 3 * width))
    bias_own = lax.dynamic_index_in_dim(bias_all, me, 0, keepdims=False).astype(jnp.float32)

    swap = [(i, i ^ 1) for i in range(size)]

    def own_half(values):
        return lax.dynamic_slice_in_dim(values, core * half, half, 0)

    def other_half(values):
        return lax.dynamic_slice_in_dim(values, (1 - core) * half, half, 0)

    out_blocks = qkv_full[:, own_qkv + extra :].reshape(parts, block, width)
    kept = own_half(out_blocks)
    came = lax.ppermute(other_half(out_blocks), "expert", swap)
    weight_out = jnp.stack(
        [jnp.where(core == 0, kept, came), jnp.where(core == 0, came, kept)], axis=1
    ).reshape(own_heads * HD, width)

    cosine, sine = rotary_tables(position, HD)
    allowed = (
        (segment[:, None] == segment[None, :]) & (position[:, None] >= position[None, :])
    )[None]
    normed_one = bf16(hidden_all * rms_scale(hidden_all) * gain_one)
    projected = mm(normed_one, weight_qkv) + bias_own
    split = projected.reshape(group, 3, own_heads, HD)
    query_low = bf16(rotate(split[:, 0], cosine, sine))
    key_low = bf16(rotate(split[:, 1], cosine, sine))
    value_low = bf16(split[:, 2])

    def score_rows():
        raw = (
            jnp.einsum("qhd,khd->hqk", query_low, key_low, preferred_element_type=jnp.float32)
            * score_scale
        )
        return jnp.where(allowed, raw, NEG_FILL)

    scores = score_rows()
    peak = jnp.max(scores, axis=-1, keepdims=True)
    log_total = peak + jnp.log(jnp.sum(jnp.exp(scores - peak), axis=-1, keepdims=True))
    weights_low = bf16(jnp.exp(scores - log_total))
    attended = bf16(
        jnp.einsum(
            "hqk,khd->qhd", weights_low, value_low, preferred_element_type=jnp.float32
        ).reshape(group, own_heads * HD)
    )
    part, routed_came = lax.optimization_barrier((bf16(mm(attended, weight_out)), routed_came))
    shared_kept, shared_came = aside(units(cut.reshape(size * block, 2 * own_shared), shared_block))
    shared_up = ordered(side_by, shared_kept, shared_came, 1)
    shared_came = lax.ppermute(shared_up, "dp", swap_above)
    middle, normed_all = remote_call(
        middle_kernel,
        chips,
        [part, hidden_in, gain_two[None, :]],
        [((rows, width), jnp.float32, False), ((2 * group, width), jnp.bfloat16, True)],
        [pltpu.VMEM((rows, width), jnp.float32), pltpu.VMEM((rows, width), jnp.bfloat16)]
        + scatter_scratch(chips, rows, width, False)
        + gather_scratch(chips, True),
        1,
        85,
    )

    normed_all, shared_came = lax.optimization_barrier((normed_all, shared_came))
    weight_up = jnp.concatenate(
        [
            ordered(above, routed_up, routed_came, 1).reshape(2, half, expert_block, width),
            ordered(above, shared_up, shared_came, 1).reshape(2, half, shared_block, width),
        ],
        axis=2,
    ).reshape(2 * hidden_units, width)

    gate_logits = mm_nt(normed_all, router_rows)
    logits = gate_logits[:, 1 : 1 + experts]
    opener_all = jax.nn.sigmoid(gate_logits[:, :1])
    peak_logit = jnp.max(logits, axis=-1, keepdims=True)
    router_total = peak_logit + jnp.log(
        jnp.sum(jnp.exp(logits - peak_logit), axis=-1, keepdims=True)
    )
    probs_all = jnp.exp(logits - router_total)
    expert_ids = jnp.arange(experts, dtype=jnp.int32)
    mine = expert_ids[None, :] == me
    named = jnp.sum((routes_all == me).astype(jnp.float32), axis=1, keepdims=True)
    gate_own = named * jnp.sum(jnp.where(mine, probs_all, 0.0), axis=1, keepdims=True)

    routed_unit = (jnp.arange(hidden_units, dtype=jnp.int32) % pair_block < expert_block)[:, None]
    unit_scale = jnp.where(routed_unit, gate_own.T, opener_all.T)
    both_up = mm_nt(weight_up, normed_all)
    gate_part = both_up[:hidden_units]
    up_part = both_up[hidden_units:]
    hidden = bf16(jax.nn.silu(gate_part) * up_part)
    scaled_hidden = bf16(unit_scale * hidden.astype(jnp.float32))

    def half_rows(values, which):
        return lax.dynamic_slice_in_dim(values, which * pair_block, pair_block, 0)

    sent_down = bf16(mm(half_rows(scaled_hidden, 1 - above), grad_rows))
    term_down = mm(half_rows(scaled_hidden, above), grad_rows)
    came_down = lax.ppermute(sent_down, "dp", swap_above)
    combined = bf16(mm_tn(scaled_hidden, weight_down))

    grad_hidden = mm_nt(weight_down, grad_rows)
    product = hidden.astype(jnp.float32) * grad_hidden
    dot_expert = named * jnp.sum(jnp.where(routed_unit, product, 0.0), axis=0)[:, None]
    dot_shared = jnp.sum(jnp.where(routed_unit, 0.0, product), axis=0)[:, None]
    grad_hidden = grad_hidden * unit_scale
    sigmoid_gate = jax.nn.sigmoid(gate_part)
    grad_gate = grad_hidden * up_part * sigmoid_gate * (1.0 + gate_part * (1.0 - sigmoid_gate))
    grad_up = grad_hidden * gate_part * sigmoid_gate
    grad_both_up = jnp.concatenate([bf16(grad_gate), bf16(grad_up)], axis=0)
    half_width = width // 2

    def half_cols(values, which):
        return lax.dynamic_slice_in_dim(values, which * half_width, half_width, 1)

    sent_up = bf16(mm(grad_both_up, half_cols(normed_all, 1 - above)))
    came_up = lax.ppermute(sent_up, "dp", swap_above)
    term_up = mm(grad_both_up, half_cols(normed_all, above))

    taken = jnp.arange(slots, dtype=jnp.int32)[None, :] == slot
    zero = jnp.zeros((), jnp.bfloat16)
    riders = jnp.concatenate(
        [
            jnp.where(taken, column, zero)
            for column in two_parts(dot_shared) + two_parts(dot_expert)
        ],
        axis=1,
    )
    riders = jnp.pad(riders, ((0, 0), (0, extra - riders.shape[1])))
    part = jnp.concatenate([bf16(mm_tn(grad_both_up, weight_up)), riders], axis=1)
    part, sent_up, sent_down = lax.optimization_barrier((part, sent_up, sent_down))

    rider = jnp.arange(extra, dtype=jnp.int32)[:, None]
    lane = jnp.arange(128, dtype=jnp.int32)[None, :]
    collect = bf16(
        ((rider < 2 * slots) & (lane == 0))
        | ((rider >= 2 * slots) & (rider < 4 * slots) & (lane == 1 + rider % size))
    )
    probs = jnp.pad(
        rows_of(jnp.concatenate([opener_all, probs_all], axis=1), slot),
        ((0, 0), (0, 127 - experts)),
    )
    grad_middle, grad_branch, grad_heads, term_norm_two = remote_call(
        branch_kernel,
        chips,
        [part, middle, gain_two[None, :], grad_own, probs, collect, router_rows],
        [
            ((rows, width), jnp.float32, False),
            ((group, width), jnp.bfloat16, True),
            ((rows, 128), jnp.bfloat16, False),
            ((1, width), jnp.float32, False),
        ],
        [
            pltpu.VMEM((rows, width + extra), jnp.float32),
            pltpu.VMEM((rows, width), jnp.bfloat16),
        ]
        + scatter_scratch(chips, rows, width + extra, True)
        + gather_scratch(chips, False),
        2,
        90,
    )
    grad_branch, came_up = lax.optimization_barrier((grad_branch, came_up))
    term_router = mm_tn(rows_of(normed_all, slot), grad_heads)[:, : 1 + experts]

    up = bf16(term_up + came_up.astype(jnp.float32))
    quarter = half_width // 2
    side_kept = lax.dynamic_slice_in_dim(up, side_by * quarter, quarter, 1)
    side_came = lax.ppermute(
        lax.dynamic_slice_in_dim(up, (1 - side_by) * quarter, quarter, 1), "dp", swap_side
    )

    grad_attended = bf16(mm_nt(grad_branch, weight_out)).reshape(group, own_heads, HD)
    weights_again = jnp.exp(score_rows() - log_total)
    grad_weights = jnp.einsum(
        "qhd,khd->hqk", grad_attended, value_low, preferred_element_type=jnp.float32
    )
    delta_rows = jnp.sum(weights_again * grad_weights, axis=-1, keepdims=True)
    grad_scores = bf16(weights_again * (grad_weights - delta_rows))
    grad_query_turned = (
        jnp.einsum("hqk,khd->qhd", grad_scores, key_low, preferred_element_type=jnp.float32)
        * score_scale
    )
    grad_key_turned = (
        jnp.einsum("hqk,qhd->khd", grad_scores, query_low, preferred_element_type=jnp.float32)
        * score_scale
    )
    grad_values = jnp.einsum(
        "hqk,qhd->khd", bf16(weights_again), grad_attended, preferred_element_type=jnp.float32
    )
    grad_projected = bf16(
        jnp.stack(
            [
                rotate_back(grad_query_turned, cosine, sine),
                rotate_back(grad_key_turned, cosine, sine),
                grad_values,
            ],
            axis=1,
        ).reshape(group, own_qkv)
    )
    part = bf16(mm_nt(grad_projected, weight_qkv))
    term_out = bf16(mm_tn(attended, grad_branch)).reshape(half, 2, block, width)
    kept = jnp.where(core == 0, term_out[:, 0], term_out[:, 1])
    given = jnp.where(core == 0, term_out[:, 1], term_out[:, 0])
    came = lax.ppermute(given, "expert", swap)
    out_blocks = jnp.concatenate(
        [jnp.where(core == 0, kept, came), jnp.where(core == 0, came, kept)], axis=0
    )
    back = jnp.concatenate(
        [bf16(mm_tn(normed_one, grad_projected)), out_blocks.reshape(width, out_cols)], axis=1
    )
    part, back, came_down, side_came = lax.optimization_barrier((part, back, came_down, side_came))
    back = lax.psum_scatter(back, "dp", scatter_dimension=0, tiled=True)
    grad_out_weight = back[:, own_qkv:].reshape(block, width).astype(jnp.float32)
    input_grad, term_norm_one = remote_call(
        input_kernel,
        chips,
        [part, hidden_in, gain_one[None, :], grad_middle],
        [((rows, width), jnp.bfloat16, False), ((1, width), jnp.float32, False)],
        [pltpu.VMEM((rows, width), jnp.float32)] + scatter_scratch(chips, rows, width, False),
        3,
        40,
    )
    grad_down = term_down + came_down.astype(jnp.float32)
    grad_shared_out = grad_down[expert_block:]
    grad_expert_out = grad_down[None, :expert_block]
    up = ordered(side_by, side_kept[None], side_came[None], 0)
    up = up.reshape(2, 2, half, pair_block, quarter)
    grad_expert_in = (
        up[:, :, :, :expert_block]
        .transpose(4, 1, 2, 0, 3)
        .reshape(1, quarter, 2 * parts * expert_block)
        .astype(jnp.float32)
    )
    cut = lax.all_to_all(
        up[:, :, :, expert_block:].transpose(4, 1, 2, 0, 3).reshape(size, block, 2 * own_shared),
        "expert",
        split_axis=0,
        concat_axis=0,
        tiled=True,
    )
    grad_shared_in = (
        cut.reshape(size, block, 2, parts, shared_block)
        .transpose(1, 2, 3, 0, 4)
        .reshape(block, 2 * parts * size * shared_block)
        .astype(jnp.float32)
    )
    back = lax.all_to_all(
        back[:, :own_qkv].reshape(size, block, own_qkv),
        "expert",
        split_axis=0,
        concat_axis=0,
        tiled=True,
    )
    grad_qkv = from_head(back).astype(jnp.float32)

    term_bias = jnp.sum(grad_projected.astype(jnp.float32), axis=0)
    bias_slots = jnp.where(jnp.arange(size)[:, None] == me, term_bias[None, :], 0.0)
    bias_rows = from_head(bias_slots[:, None, :]).reshape(width, bias_cols)
    small_terms = jnp.concatenate(
        [term_norm_one[0][:, None], term_norm_two[0][:, None], term_router, bias_rows], axis=1
    )
    count = small_terms.shape[1]
    small_terms = lax.all_to_all(
        small_terms.T.reshape(count, parts * size, block).transpose(1, 0, 2),
        ("dp", "expert"),
        split_axis=0,
        concat_axis=0,
        tiled=True,
    )
    small_sum = jnp.sum(small_terms, axis=0)
    combined, input_grad = lax.optimization_barrier((combined, input_grad))
    (output,) = remote_call(
        output_kernel,
        chips,
        [combined, middle, valid_rows],
        [((rows, width), jnp.bfloat16, False)],
        [pltpu.VMEM((rows, width), jnp.float32)] + scatter_scratch(chips, rows, width, True),
        4,
        55,
    )
    grad_norm1 = small_sum[0]
    grad_norm2 = small_sum[1]
    grad_shared_gate = small_sum[2]
    grad_router = small_sum[3 : 3 + experts].T
    grad_bias = small_sum[3 + experts :].T.reshape(block * bias_cols)
    return (
        output,
        input_grad,
        grad_norm1,
        grad_qkv,
        grad_bias,
        grad_out_weight,
        grad_norm2,
        grad_router,
        grad_shared_gate,
        grad_shared_in,
        grad_shared_out,
        grad_expert_in,
        grad_expert_out,
    )


def solution(mesh):
    size, parts = mesh.shape["expert"], mesh.shape["dp"]

    def device(*arrays):
        block = arrays[5].shape[0]
        whole_heads = 2 * block == HD and parts == 4 and size % 2 == 0
        one_expert = arrays[13].shape[0] == 1
        if whole_heads and one_expert and arrays[5].shape[1] % (3 * size * HD) == 0:
            return group_device(*arrays)
        return per_device(*arrays)

    return jax.shard_map(
        device,
        mesh=mesh,
        in_specs=(
            P(("dp", "expert"), None),
            P(("dp", "expert"), None),
            P("dp", None),
            P(("dp", "expert"), None),
            P(("dp", "expert")),
            P(("dp", "expert"), None),
            P(("dp", "expert")),
            P(("dp", "expert"), None),
            P(("dp", "expert")),
            P(("dp", "expert"), None),
            P(("dp", "expert")),
            P(("dp", "expert"), None),
            P(("dp", "expert"), None),
            P("expert", "dp", None),
            P("expert", "dp", None),
        ),
        out_specs=(
            P(("dp", "expert"), None),
            P(("dp", "expert"), None),
            P(("dp", "expert")),
            P(("dp", "expert"), None),
            P(("dp", "expert")),
            P(("dp", "expert"), None),
            P(("dp", "expert")),
            P(("dp", "expert"), None),
            P(("dp", "expert")),
            P(("dp", "expert"), None),
            P(("dp", "expert"), None),
            P("expert", "dp", None),
            P("expert", "dp", None),
        ),
        check_vma=False,
    )
```

```python
import functools

import jax
import jax.numpy as jnp
from jax import lax
from jax.experimental import pallas as pl
from jax.experimental.pallas import tpu as pltpu
from jax.sharding import PartitionSpec as P

HD = 128


EPSILON = 1e-06
THETA = 1000000.0
NEG_FILL = -1e30


def rms_scale(values):
    return lax.rsqrt(jnp.mean(values * values, axis=-1, keepdims=True) + EPSILON)


def rotary_tables(positions, head_size):
    half_size = head_size // 2
    steps_up = jnp.arange(half_size, dtype=jnp.float32) * (2.0 / head_size)
    inverse = THETA ** (-steps_up)
    angles = positions.astype(jnp.float32)[:, None] * inverse[None, :]
    angles = jnp.concatenate([angles, angles], axis=-1)
    return (jnp.cos(angles)[:, None, :], jnp.sin(angles)[:, None, :])


def rotate(values, cosine, sine):
    half_size = values.shape[-1] // 2
    turned = jnp.concatenate([-values[..., half_size:], values[..., :half_size]], axis=-1)
    return values * cosine + turned * sine


def rotate_back(grad_values, cosine, sine):
    half_size = grad_values.shape[-1] // 2
    scaled = grad_values * sine
    turned = jnp.concatenate([scaled[..., half_size:], -scaled[..., :half_size]], axis=-1)
    return grad_values * cosine + turned


def swiglu(gate_up):
    half_size = gate_up.shape[-1] // 2
    return jax.nn.silu(gate_up[..., :half_size]) * gate_up[..., half_size:]


def swiglu_back(gate_up, grad_hidden):
    half_size = gate_up.shape[-1] // 2
    gate_part = gate_up[..., :half_size]
    up_part = gate_up[..., half_size:]
    sigmoid_gate = jax.nn.sigmoid(gate_part)
    grad_gate = grad_hidden * up_part * sigmoid_gate * (1.0 + gate_part * (1.0 - sigmoid_gate))
    grad_up = grad_hidden * gate_part * sigmoid_gate
    return jnp.concatenate([grad_gate, grad_up], axis=-1)


def norm_back(values, scale_rows, gain, grad_normed):
    weighted = grad_normed * gain
    inner = jnp.mean(weighted * values, axis=-1, keepdims=True)
    grad_values = scale_rows * weighted - values * scale_rows * scale_rows * scale_rows * inner
    grad_gain = jnp.sum(grad_normed * values * scale_rows, axis=0)
    return (grad_values, grad_gain)


def segment_table(length_row, count):
    ends = jnp.cumsum(length_row, dtype=jnp.int32)
    starts = ends - length_row
    places = jnp.arange(count, dtype=jnp.int32)
    segment = jnp.sum(
        (places[:, None] >= ends[None, :-1]).astype(jnp.int32), axis=1, dtype=jnp.int32
    )
    owners = segment[:, None] == jnp.arange(length_row.shape[0], dtype=jnp.int32)[None, :]
    first = jnp.sum(jnp.where(owners, starts[None, :], 0), axis=1, dtype=jnp.int32)
    return (segment, places - first)


def per_device(
    hidden_in,
    out_grad,
    lengths,
    routes,
    norm1_gain,
    qkv_weight,
    qkv_bias,
    out_weight,
    norm2_gain,
    router_weight,
    shared_gate,
    shared_in,
    shared_out,
    expert_in,
    expert_out,
):
    highest = lax.Precision.HIGHEST
    row_count, model_width = hidden_in.shape
    head_count = model_width // HD
    group_size = lax.axis_size("expert")
    group_rows = row_count * group_size
    top_count = routes.shape[1]
    expert_count = router_weight.shape[1]
    local_count = expert_in.shape[0]
    capacity = max(2, 2 * row_count * top_count // expert_count)
    slot_count = expert_count * capacity
    score_scale = HD ** (-0.5)
    dense = (
        lax.all_gather(norm1_gain, ("dp", "expert"), axis=0, tiled=True),
        lax.all_gather(qkv_weight, ("dp", "expert"), axis=0, tiled=True),
        lax.all_gather(qkv_bias, ("dp", "expert"), axis=0, tiled=True),
        lax.all_gather(out_weight, ("dp", "expert"), axis=0, tiled=True),
        lax.all_gather(norm2_gain, ("dp", "expert"), axis=0, tiled=True),
        lax.all_gather(router_weight, ("dp", "expert"), axis=0, tiled=True),
        lax.all_gather(shared_gate, ("dp", "expert"), axis=0, tiled=True),
        lax.all_gather(shared_in, ("dp", "expert"), axis=0, tiled=True),
        lax.all_gather(shared_out, ("dp", "expert"), axis=0, tiled=True),
    )
    (
        gain_first,
        weight_qkv,
        bias_first,
        weight_out,
        gain_second,
        weight_router,
        weight_gate,
        weight_shared_in,
        weight_shared_out,
    ) = dense
    weight_expert_in, weight_expert_out = (
        lax.all_gather(expert_in, "dp", axis=1, tiled=True),
        lax.all_gather(expert_out, "dp", axis=1, tiled=True),
    )
    segment_all, position_all = segment_table(lengths[0], group_rows)
    first_row = lax.axis_index("expert") * row_count
    segment_mine = lax.dynamic_slice_in_dim(segment_all, first_row, row_count, 0)
    position_mine = lax.dynamic_slice_in_dim(position_all, first_row, row_count, 0)
    valid_rows = (segment_mine < lengths.shape[1] - 1).astype(jnp.float32)[:, None]
    cosine, sine = rotary_tables(position_mine, HD)
    allowed = (
        (segment_mine[:, None] == segment_all[None, :])
        & (position_mine[:, None] >= position_all[None, :])
    )[None]
    inputs = hidden_in.astype(jnp.float32)
    scale_first = rms_scale(inputs)
    gain_one = gain_first.astype(jnp.float32)
    normed_one = (inputs * scale_first * gain_one).astype(jnp.bfloat16)
    projected = jnp.dot(
        normed_one, weight_qkv, preferred_element_type=jnp.float32
    ) + bias_first.astype(jnp.float32)
    query_low = rotate(
        projected[:, :model_width].reshape(row_count, head_count, HD), cosine, sine
    ).astype(jnp.bfloat16)
    key_low = rotate(
        projected[:, model_width : 2 * model_width].reshape(row_count, head_count, HD), cosine, sine
    ).astype(jnp.bfloat16)
    value_low = (
        projected[:, 2 * model_width :].reshape(row_count, head_count, HD).astype(jnp.bfloat16)
    )
    keys_all, values_all = (
        lax.all_gather(key_low, "expert", axis=0, tiled=True),
        lax.all_gather(value_low, "expert", axis=0, tiled=True),
    )

    def score_rows(queries):
        raw = (
            jnp.einsum("qhd,khd->hqk", queries, keys_all, preferred_element_type=jnp.float32)
            * score_scale
        )
        return jnp.where(allowed, raw, NEG_FILL)

    scores = score_rows(query_low)
    peak = jnp.max(scores, axis=-1, keepdims=True)
    log_total = peak + jnp.log(jnp.sum(jnp.exp(scores - peak), axis=-1, keepdims=True))
    weights_low = jnp.exp(scores - log_total).astype(jnp.bfloat16)
    attended = (
        jnp.einsum("hqk,khd->qhd", weights_low, values_all, preferred_element_type=jnp.float32)
        .reshape(row_count, model_width)
        .astype(jnp.bfloat16)
    )
    middle = inputs + jnp.dot(attended, weight_out, preferred_element_type=jnp.float32)
    scale_second = rms_scale(middle)
    gain_two = gain_second.astype(jnp.float32)
    normed_two = (middle * scale_second * gain_two).astype(jnp.bfloat16)
    logits = jnp.dot(normed_two, weight_router, preferred_element_type=jnp.float32)
    gate_logit = jnp.dot(normed_two, weight_gate, preferred_element_type=jnp.float32)
    peak_logit = jnp.max(logits, axis=-1, keepdims=True)
    router_total = peak_logit + jnp.log(
        jnp.sum(jnp.exp(logits - peak_logit), axis=-1, keepdims=True)
    )
    router_probs = jnp.exp(logits - router_total)
    expert_ids = jnp.arange(expert_count, dtype=jnp.int32)
    chosen = routes[:, :, None] == expert_ids[None, None, :]
    chosen_float = chosen.astype(jnp.float32)
    gates = jnp.sum(chosen_float * router_probs[:, None, :], axis=2)
    flat_hits = chosen.reshape(row_count * top_count, expert_count).astype(jnp.int32)
    earlier = jnp.cumsum(flat_hits, axis=0, dtype=jnp.int32) - flat_hits
    slot_rank = jnp.sum(earlier * flat_hits, axis=1, dtype=jnp.int32)
    slot_of = routes.reshape(-1) * capacity + slot_rank
    slot_hits = (
        (slot_of[:, None] == jnp.arange(slot_count, dtype=jnp.int32)[None, :])
        .reshape(row_count, top_count, slot_count)
        .astype(jnp.float32)
    )
    placement_map = jnp.sum(slot_hits, axis=1)
    weighted_map = jnp.sum(slot_hits * gates[:, :, None], axis=1)
    send_rows = (
        jnp.einsum(
            "ts,td->sd",
            placement_map.astype(jnp.bfloat16),
            normed_two,
            preferred_element_type=jnp.float32,
        )
        .astype(jnp.bfloat16)
        .reshape(expert_count, capacity, model_width)
    )
    arrived = lax.all_to_all(send_rows, "expert", split_axis=0, concat_axis=0, tiled=True)
    item_count = arrived.shape[1]
    grouped = arrived.reshape(group_size, local_count, item_count, model_width)
    gate_up = jnp.einsum(
        "gecd,edf->gecf", grouped, weight_expert_in, preferred_element_type=jnp.float32
    )
    hidden_low = swiglu(gate_up).astype(jnp.bfloat16)
    produced = jnp.einsum(
        "gecf,efd->gecd", hidden_low, weight_expert_out, preferred_element_type=jnp.float32
    ).astype(jnp.bfloat16)
    produced_rows = produced.reshape(group_size * local_count, item_count, model_width)
    expert_gate_up = gate_up.reshape(group_size * local_count, item_count, gate_up.shape[-1])
    back_rows = lax.all_to_all(produced_rows, "expert", split_axis=0, concat_axis=0, tiled=True)
    back_float = back_rows.reshape(slot_count, model_width).astype(jnp.float32)
    routed = jnp.dot(weighted_map, back_float, precision=highest)
    shared_up = jnp.dot(normed_two, weight_shared_in, preferred_element_type=jnp.float32)
    shared_hidden = swiglu(shared_up).astype(jnp.bfloat16)
    shared_rows = jnp.dot(shared_hidden, weight_shared_out, preferred_element_type=jnp.float32)
    opener = jax.nn.sigmoid(gate_logit)[:, None]
    output = (valid_rows * (middle + routed + opener * shared_rows)).astype(jnp.bfloat16)
    held = (
        lax.all_gather(norm1_gain, ("dp", "expert"), axis=0, tiled=True),
        lax.all_gather(qkv_weight, ("dp", "expert"), axis=0, tiled=True),
        lax.all_gather(qkv_bias, ("dp", "expert"), axis=0, tiled=True),
        lax.all_gather(out_weight, ("dp", "expert"), axis=0, tiled=True),
        lax.all_gather(norm2_gain, ("dp", "expert"), axis=0, tiled=True),
        lax.all_gather(router_weight, ("dp", "expert"), axis=0, tiled=True),
        lax.all_gather(shared_gate, ("dp", "expert"), axis=0, tiled=True),
        lax.all_gather(shared_in, ("dp", "expert"), axis=0, tiled=True),
        lax.all_gather(shared_out, ("dp", "expert"), axis=0, tiled=True),
    )
    (
        gain_first,
        weight_qkv,
        bias_first,
        weight_out,
        gain_second,
        weight_router,
        weight_gate,
        weight_shared_in,
        weight_shared_out,
    ) = held
    gain_one = gain_first.astype(jnp.float32)
    gain_two = gain_second.astype(jnp.float32)
    grad_rows = out_grad.astype(jnp.float32) * valid_rows
    grad_shared_rows = (grad_rows * opener).astype(jnp.bfloat16)
    grad_gate_logit = (
        jnp.sum(grad_rows * shared_rows, axis=-1) * opener[:, 0] * (1.0 - opener[:, 0])
    ).astype(jnp.bfloat16)
    grad_shared_hidden = jnp.einsum(
        "td,fd->tf", grad_shared_rows, weight_shared_out, preferred_element_type=jnp.float32
    )
    grad_shared_up = swiglu_back(shared_up, grad_shared_hidden).astype(jnp.bfloat16)
    term_shared_out = jnp.einsum(
        "tf,td->fd", shared_hidden, grad_shared_rows, preferred_element_type=jnp.float32
    )
    term_shared_in = jnp.einsum(
        "td,tf->df", normed_two, grad_shared_up, preferred_element_type=jnp.float32
    )
    slot_product = jnp.einsum("td,sd->ts", grad_rows, back_float, precision=highest)
    grad_gates = jnp.sum(slot_hits * slot_product[:, None, :], axis=2)
    grad_probs = jnp.sum(chosen_float * grad_gates[:, :, None], axis=1)
    grad_logits = (
        router_probs * (grad_probs - jnp.sum(router_probs * grad_probs, axis=-1, keepdims=True))
    ).astype(jnp.bfloat16)
    term_router = jnp.einsum(
        "td,te->de", normed_two, grad_logits, preferred_element_type=jnp.float32
    )
    term_gate = jnp.einsum(
        "td,t->d", normed_two, grad_gate_logit, preferred_element_type=jnp.float32
    )
    grad_result = (
        jnp.einsum("ts,td->sd", weighted_map, grad_rows, precision=highest)
        .astype(jnp.bfloat16)
        .reshape(expert_count, capacity, model_width)
    )
    grad_arrived = lax.all_to_all(grad_result, "expert", split_axis=0, concat_axis=0, tiled=True)
    grad_grouped = grad_arrived.reshape(group_size, local_count, capacity, model_width)
    gate_up_grouped = expert_gate_up.reshape(
        group_size, local_count, capacity, expert_gate_up.shape[-1]
    )
    hidden_again = swiglu(gate_up_grouped).astype(jnp.bfloat16)
    grad_hidden = jnp.einsum(
        "gecd,efd->gecf", grad_grouped, weight_expert_out, preferred_element_type=jnp.float32
    )
    grad_gate_up = swiglu_back(gate_up_grouped, grad_hidden).astype(jnp.bfloat16)
    arrived_grouped = arrived.reshape(group_size, local_count, capacity, model_width)
    term_expert_in = jnp.einsum(
        "gecd,gecf->edf", arrived_grouped, grad_gate_up, preferred_element_type=jnp.float32
    )
    term_expert_out = jnp.einsum(
        "gecf,gecd->efd", hidden_again, grad_grouped, preferred_element_type=jnp.float32
    )
    grad_sent = jnp.einsum(
        "gecf,edf->gecd", grad_gate_up, weight_expert_in, preferred_element_type=jnp.float32
    ).reshape(group_size * local_count, capacity, model_width)
    grad_slots = lax.all_to_all(
        grad_sent.astype(jnp.bfloat16), "expert", split_axis=0, concat_axis=0, tiled=True
    ).astype(grad_sent.dtype)
    grad_expert_in, grad_expert_out = (
        lax.psum_scatter(
            term_expert_in.astype(jnp.bfloat16), "dp", scatter_dimension=1, tiled=True
        ).astype(jnp.float32),
        lax.psum_scatter(
            term_expert_out.astype(jnp.bfloat16), "dp", scatter_dimension=1, tiled=True
        ).astype(jnp.float32),
    )
    grad_normed_two = jnp.einsum(
        "te,de->td", grad_logits, weight_router, preferred_element_type=jnp.float32
    )
    grad_normed_two = (
        grad_normed_two
        + grad_gate_logit.astype(jnp.float32)[:, None] * weight_gate.astype(jnp.float32)[None, :]
    )
    grad_normed_two = grad_normed_two + jnp.einsum(
        "tf,df->td", grad_shared_up, weight_shared_in, preferred_element_type=jnp.float32
    )
    grad_normed_two = grad_normed_two + jnp.dot(
        placement_map, grad_slots.reshape(slot_count, model_width), precision=highest
    )
    grad_middle_norm, term_norm_two = norm_back(middle, scale_second, gain_two, grad_normed_two)
    grad_middle = grad_rows + grad_middle_norm
    grad_norm2, grad_router, grad_shared_gate, grad_shared_in, grad_shared_out = (
        lax.psum_scatter(term_norm_two, ("dp", "expert"), scatter_dimension=0, tiled=True),
        lax.psum_scatter(term_router, ("dp", "expert"), scatter_dimension=0, tiled=True),
        lax.psum_scatter(term_gate, ("dp", "expert"), scatter_dimension=0, tiled=True),
        lax.psum_scatter(term_shared_in, ("dp", "expert"), scatter_dimension=0, tiled=True),
        lax.psum_scatter(term_shared_out, ("dp", "expert"), scatter_dimension=0, tiled=True),
    )
    grad_branch = grad_middle.astype(jnp.bfloat16)
    term_out_weight = jnp.einsum(
        "td,te->de", attended, grad_branch, preferred_element_type=jnp.float32
    )
    grad_attended = (
        jnp.einsum("te,de->td", grad_branch, weight_out, preferred_element_type=jnp.float32)
        .astype(jnp.bfloat16)
        .reshape(row_count, head_count, HD)
    )
    weights_again = jnp.exp(score_rows(query_low) - log_total)
    weights_again_low = weights_again.astype(jnp.bfloat16)
    grad_weights = jnp.einsum(
        "qhd,khd->hqk", grad_attended, values_all, preferred_element_type=jnp.float32
    )
    delta_rows = jnp.sum(weights_again * grad_weights, axis=-1, keepdims=True)
    grad_scores = (weights_again * (grad_weights - delta_rows)).astype(jnp.bfloat16)
    grad_query_turned = (
        jnp.einsum("hqk,khd->qhd", grad_scores, keys_all, preferred_element_type=jnp.float32)
        * score_scale
    )
    grad_keys_all = (
        jnp.einsum("hqk,qhd->khd", grad_scores, query_low, preferred_element_type=jnp.float32)
        * score_scale
    )
    grad_values_all = jnp.einsum(
        "hqk,qhd->khd", weights_again_low, grad_attended, preferred_element_type=jnp.float32
    )
    grad_key_turned, grad_values = (
        lax.psum_scatter(
            grad_keys_all.astype(jnp.bfloat16), "expert", scatter_dimension=0, tiled=True
        ).astype(jnp.float32),
        lax.psum_scatter(
            grad_values_all.astype(jnp.bfloat16), "expert", scatter_dimension=0, tiled=True
        ).astype(jnp.float32),
    )
    grad_projected = jnp.concatenate(
        [
            rotate_back(grad_query_turned, cosine, sine).reshape(row_count, model_width),
            rotate_back(grad_key_turned, cosine, sine).reshape(row_count, model_width),
            grad_values.reshape(row_count, model_width),
        ],
        axis=-1,
    ).astype(jnp.bfloat16)
    term_bias = jnp.sum(grad_projected.astype(jnp.float32), axis=0)
    term_qkv = jnp.einsum(
        "td,tf->df", normed_one, grad_projected, preferred_element_type=jnp.float32
    )
    grad_normed_one = jnp.einsum(
        "tf,df->td", grad_projected, weight_qkv, preferred_element_type=jnp.float32
    )
    grad_input_norm, term_norm_one = norm_back(inputs, scale_first, gain_one, grad_normed_one)
    input_grad = (grad_middle + grad_input_norm).astype(jnp.bfloat16)
    grad_norm1, grad_qkv, grad_bias, grad_out_weight = (
        lax.psum_scatter(term_norm_one, ("dp", "expert"), scatter_dimension=0, tiled=True),
        lax.psum_scatter(term_qkv, ("dp", "expert"), scatter_dimension=0, tiled=True),
        lax.psum_scatter(term_bias, ("dp", "expert"), scatter_dimension=0, tiled=True),
        lax.psum_scatter(term_out_weight, ("dp", "expert"), scatter_dimension=0, tiled=True),
    )
    return (
        output,
        input_grad,
        grad_norm1,
        grad_qkv,
        grad_bias,
        grad_out_weight,
        grad_norm2,
        grad_router,
        grad_shared_gate,
        grad_shared_in,
        grad_shared_out,
        grad_expert_in,
        grad_expert_out,
    )


MESH_IDS = pl.DeviceIdType.MESH
STRIP = 16


class Line:
    def __init__(self, chips, wide):
        me = lax.axis_index("expert")
        group = lax.axis_index("dp")
        self.chips = chips
        self.wide = wide
        self.z = me // 2
        self.core = lax.rem(me, 2)
        self.x = lax.rem(group, 2)
        self.group = group
        self.below = self.z > 0
        self.above = self.z < chips - 1

    def at(self, z, core):
        return {"expert": 2 * z + core}

    def beside(self):
        return {"dp": self.group + 1 - 2 * self.x, "expert": 2 * self.z + self.core}

    def meet(self):
        barrier = pltpu.get_barrier_semaphore()

        def hello(target):
            pl.semaphore_signal(barrier, inc=1, device_id=target, device_id_type=MESH_IDS)

        hello(self.at(self.z, 1 - self.core))
        pl.when(self.above)(lambda: hello(self.at(self.z + 1, self.core)))
        pl.when(self.below)(lambda: hello(self.at(self.z - 1, self.core)))
        if self.wide:
            hello(self.beside())
        peers = 1 + jnp.minimum(self.z, 1) + jnp.minimum(self.chips - 1 - self.z, 1)
        pl.semaphore_wait(barrier, peers + (1 if self.wide else 0))


def gather_scratch(chips, wide):
    items = 2 * chips - 1
    pair = [pltpu.SemaphoreType.DMA((items,)) for _ in range(6 if wide else 2)]
    return [
        pltpu.SemaphoreType.DMA((2, chips - 1)),
        pltpu.SemaphoreType.DMA((2, chips - 1)),
        pltpu.SemaphoreType.DMA,
    ] + pair


class Gather:
    def __init__(self, line, own, out, scratch):
        self.line, self.own, self.out = line, own, out
        self.send, self.recv, self.local = scratch[:3]
        self.pair = scratch[3:]
        self.wide = len(self.pair) == 6
        self.rows = own.shape[0]

    def block(self, group, chip, which):
        place = 2 * chip + which
        if self.wide:
            place = place + group * (2 * self.line.chips)
        return self.out.at[pl.ds(place * self.rows, self.rows)]

    def mine(self, chip, which):
        return self.block(0, chip, which)

    def theirs(self, chip, which):
        return self.block(1, chip, which)

    def origin(self, step, up):
        return self.line.z - step if up else self.line.z + step

    def hop(self, step, up):
        z, core = self.line.z, self.line.core
        origin = self.origin(step, up)
        return pltpu.make_async_remote_copy(
            src_ref=self.own if step == 0 else self.mine(origin, core),
            dst_ref=self.mine(origin, core),
            send_sem=self.send.at[0 if up else 1, step],
            recv_sem=self.recv.at[0 if up else 1, step],
            device_id=self.line.at(z + 1 if up else z - 1, core),
            device_id_type=MESH_IDS,
        )

    def arrival(self, step, up):
        z, core = self.line.z, self.line.core
        return pltpu.make_async_remote_copy(
            src_ref=self.own,
            dst_ref=self.mine(self.origin(step + 1, up), core),
            send_sem=self.send.at[0 if up else 1, step],
            recv_sem=self.recv.at[0 if up else 1, step],
            device_id=self.line.at(z - 1 if up else z + 1, core),
            device_id_type=MESH_IDS,
        )

    def across(self, index, source, target, kind):
        line = self.line
        return pltpu.make_async_remote_copy(
            src_ref=source,
            dst_ref=target,
            send_sem=self.pair[2 * kind].at[index],
            recv_sem=self.pair[2 * kind + 1].at[index],
            device_id=line.beside() if kind == 1 else line.at(line.z, 1 - line.core),
            device_id_type=MESH_IDS,
        )

    def sends(self, step, up):
        line = self.line
        if up:
            return (line.z >= step) & line.above
        return (line.z + step <= line.chips - 1) & line.below

    def items(self):
        line = self.line
        found = [(0, line.z, None)]
        for step in range(line.chips - 1):
            found.append((1 + step, line.z - 1 - step, line.z - 1 - step >= 0))
            found.append(
                (line.chips + step, line.z + 1 + step, line.z + 1 + step <= line.chips - 1)
            )
        return found

    def spread(self, index, origin, source):
        core = self.line.core
        self.across(index, source, self.mine(origin, core), 0).start()
        if self.wide:
            self.across(index, source, self.theirs(origin, core), 1).start()

    def begin(self):
        line = self.line
        pltpu.make_async_copy(self.own, self.mine(line.z, line.core), self.local).start()

    def push(self, step):
        line = self.line
        for up in (True, False):
            pl.when(self.sends(step, up))(lambda up=up: self.hop(step, up).start())
        if step == 0:
            self.spread(0, line.z, self.own)

    def pull(self, step):
        for index, origin, comes in self.items():
            if index not in (1 + step, self.line.chips + step):
                continue

            def take(index=index, origin=origin):
                self.arrival(step, index < self.line.chips).wait_recv()
                self.spread(index, origin, self.mine(origin, self.line.core))

            pl.when(comes)(take)

    def end(self):
        line, core = self.line, self.line.core

        def each(act):
            for index, origin, comes in self.items():
                if comes is None:
                    act(index, origin)
                else:
                    pl.when(comes)(lambda index=index, origin=origin: act(index, origin))

        def turn(index, origin):
            landed = self.theirs(origin, core)
            self.across(index, landed, landed, 1).wait_recv()
            self.across(index, landed, landed, 2).start()

        def settle(index, origin):
            here = self.mine(origin, core)
            self.across(index, here, here, 0).wait_send()
            self.across(index, here, self.mine(origin, 1 - core), 0).wait_recv()
            if self.wide:
                there = self.theirs(origin, core)
                self.across(index, here, here, 1).wait_send()
                self.across(index, there, there, 2).wait_send()
                self.across(index, there, self.theirs(origin, 1 - core), 2).wait_recv()

        if self.wide:
            each(turn)
        each(settle)
        for step in range(line.chips - 1):
            for up in (True, False):
                pl.when(self.sends(step, up))(
                    lambda step=step, up=up: self.hop(step, up).wait_send()
                )
        pltpu.make_async_copy(self.own, self.mine(line.z, core), self.local).wait()


def gather_lines(*gathers, late=None):
    chips = gathers[0].line.chips
    for one in gathers:
        one.begin()
    for step in range(chips - 1):
        for one in gathers:
            one.push(step)
        for one in gathers:
            one.pull(step)
    if late is not None:
        late()
    for one in gathers:
        one.end()


def scatter_scratch(chips, rows, width, wide):
    groups = 2 if wide else 1
    found = [
        pltpu.VMEM((groups, chips, rows, width), jnp.bfloat16),
        pltpu.VMEM((2, chips, rows, width), jnp.bfloat16),
        pltpu.SemaphoreType.DMA((groups, chips)),
        pltpu.SemaphoreType.DMA((groups, chips)),
        pltpu.SemaphoreType.DMA((2, chips)),
        pltpu.SemaphoreType.DMA((2, chips)),
    ]
    if wide:
        found += [
            pltpu.VMEM((chips, rows, width), jnp.bfloat16),
            pltpu.SemaphoreType.DMA((chips,)),
            pltpu.SemaphoreType.DMA((chips,)),
        ]
    return found


def strips(rows, body):
    @pl.loop(0, rows // STRIP)
    def _(index):
        body(pl.ds(pl.multiple_of(index * STRIP, STRIP), STRIP))


def scatter_line(line, part, total, scratch):
    chips, z, core = line.chips, line.z, line.core
    rows = total.shape[0]
    held, come, pair_send, pair_recv, send, recv = scratch[:6]
    wide = len(scratch) == 9
    if wide:
        aside, side_send, side_recv = scratch[6:]

    def start_of(other, chip, which):
        place = 2 * chip + which
        if wide:
            place = place + other * (2 * chips)
        return place * rows

    def across(other, chip):
        return pltpu.make_async_remote_copy(
            src_ref=part.at[pl.ds(start_of(other, chip, 1 - core), rows)],
            dst_ref=held.at[other, chip],
            send_sem=pair_send.at[other, chip],
            recv_sem=pair_recv.at[other, chip],
            device_id=line.at(z, 1 - core),
            device_id_type=MESH_IDS,
        )

    def beside(chip):
        return pltpu.make_async_remote_copy(
            src_ref=held.at[1, chip],
            dst_ref=aside.at[chip],
            send_sem=side_send.at[chip],
            recv_sem=side_recv.at[chip],
            device_id=line.beside(),
            device_id_type=MESH_IDS,
        )

    def hop(chip, up, target):
        way = 0 if up else 1
        return pltpu.make_async_remote_copy(
            src_ref=held.at[0, chip],
            dst_ref=come.at[way, chip],
            send_sem=send.at[way, chip],
            recv_sem=recv.at[way, chip],
            device_id=line.at(target, core),
            device_id_type=MESH_IDS,
        )

    def value(other, chip, strip, ways):
        first = start_of(other, chip, core)
        mine = part[pl.ds(pl.multiple_of(first + strip.start, STRIP), STRIP), :]
        summed = mine.astype(jnp.float32) + held[other, chip, strip, :].astype(jnp.float32)
        if wide and other == 0:
            summed = summed + aside[chip, strip, :].astype(jnp.float32)
        for way in ways:
            summed = summed + come[way, chip, strip, :].astype(jnp.float32)
        return summed

    def add(other, chip, ways):
        def body(strip):
            held[other, chip, strip, :] = value(other, chip, strip, ways).astype(jnp.bfloat16)

        strips(rows, body)

    def up_chip(step):
        return chips - 1 - step + z

    def down_chip(step):
        return step - (chips - 1 - z)

    def up_sends(step):
        return (z <= step) & line.above

    def down_sends(step):
        return (step >= chips - 1 - z) & line.below

    def each(act):
        for step in range(chips - 1):
            pl.when(up_sends(step))(lambda step=step: act(up_chip(step), True))
            pl.when(down_sends(step))(lambda step=step: act(down_chip(step), False))

    if wide:
        each(lambda chip, up: across(1, chip).start())
        across(1, z).start()
    each(lambda chip, up: across(0, chip).start())
    across(0, z).start()

    def give(chip):
        across(1, chip).wait_recv()
        add(1, chip, ())
        beside(chip).start()

    if wide:
        each(lambda chip, up: give(chip))
        give(z)

    def ready(chip):
        across(0, chip).wait_recv()
        if wide:
            beside(chip).wait_recv()

    def forward(chip, up):
        ready(chip)
        way = 0 if up else 1

        def with_arrival():
            hop(chip, up, z).wait_recv()
            add(0, chip, (way,))

        more = line.below if up else line.above
        pl.when(more)(with_arrival)
        pl.when(jnp.logical_not(more))(lambda: add(0, chip, ()))
        hop(chip, up, z + 1 if up else z - 1).start()

    each(forward)
    ready(z)
    pl.when(line.below)(lambda: hop(z, True, z).wait_recv())
    pl.when(line.above)(lambda: hop(z, False, z).wait_recv())

    def last(ways):
        def body(strip):
            total[strip, :] = value(0, z, strip, ways)

        strips(rows, body)

    pl.when(line.below & line.above)(lambda: last((0, 1)))
    pl.when(jnp.logical_not(line.below))(lambda: last((1,)))
    pl.when(jnp.logical_not(line.above))(lambda: last((0,)))

    def settle(chip):
        across(0, chip).wait_send()
        if wide:
            across(1, chip).wait_send()
            beside(chip).wait_send()

    def settle_hop(chip, up):
        settle(chip)
        hop(chip, up, z + 1 if up else z - 1).wait_send()

    each(settle_hop)
    settle(z)


def gather_kernel(chips, near, near_all, *scratch):
    line = Line(chips, False)
    line.meet()
    gather_lines(Gather(line, near, near_all, scratch))


def aside_scratch(chips):
    return [pltpu.SemaphoreType.DMA((chips,)) for _ in range(4)]


class Aside:
    def __init__(self, line, own, out, scratch):
        self.line, self.own, self.out = line, own, out
        self.sems = scratch
        self.rows = own.shape[0] // (2 * line.chips)

    def copy(self, chip, kind, which):
        line = self.line
        place = pl.ds((2 * chip + which) * self.rows, self.rows)
        source = self.out if kind else self.own
        return pltpu.make_async_remote_copy(
            src_ref=source.at[place],
            dst_ref=self.out.at[place],
            send_sem=self.sems[2 * kind].at[chip],
            recv_sem=self.sems[2 * kind + 1].at[chip],
            device_id=line.at(line.z, 1 - line.core) if kind else line.beside(),
            device_id_type=MESH_IDS,
        )

    def begin(self):
        for chip in range(self.line.chips):
            self.copy(chip, 0, self.line.core).start()

    def turn(self):
        for chip in range(self.line.chips):
            self.copy(chip, 0, self.line.core).wait_recv()
            self.copy(chip, 1, self.line.core).start()

    def end(self):
        core = self.line.core
        for chip in range(self.line.chips):
            self.copy(chip, 0, core).wait_send()
            self.copy(chip, 1, core).wait_send()
            self.copy(chip, 1, 1 - core).wait_recv()


def middle_kernel(
    chips, part, hidden, gain, near, middle, normed_all, far, total, normed, *scratch
):
    line = Line(chips, True)
    line.meet()
    aside = Aside(line, near, far, scratch[15:])
    aside.begin()
    scatter_line(line, part, total, scratch[:6])

    def body(strip):
        rows = hidden[strip, :].astype(jnp.float32) + total[strip, :]
        middle[strip, :] = rows
        normed[strip, :] = (rows * rms_scale(rows) * gain[...]).astype(jnp.bfloat16)

    strips(hidden.shape[0], body)
    gather_lines(Gather(line, normed, normed_all, scratch[6:15]), late=aside.turn)
    aside.end()


def branch_kernel(
    chips, part, middle, gain, out_grad, probs, collect, router,
    grad_middle, grad_all, heads, term, total, turned, *scratch
):
    line = Line(chips, True)
    line.meet()
    scatter_line(line, part, total, scratch[:9])
    width = middle.shape[1]
    term[...] = jnp.zeros_like(term)

    def body(strip):
        tail = jnp.dot(
            total[strip, width:].astype(jnp.bfloat16), collect[...],
            preferred_element_type=jnp.float32,
        )
        prob = probs[strip, :]
        lane = lax.broadcasted_iota(jnp.int32, prob.shape, 1)
        inner = jnp.sum(jnp.where(lane > 0, prob * tail, 0.0), axis=1, keepdims=True)
        head = jnp.where(lane > 0, prob * (tail - inner), tail * prob * (1.0 - prob))
        head = head.astype(jnp.bfloat16)
        heads[strip, :] = head
        grad = total[strip, :width] + jnp.dot(
            head, router[...], preferred_element_type=jnp.float32
        )
        rows = middle[strip, :]
        scale = rms_scale(rows)
        weighted = grad * gain[...]
        mean = jnp.mean(weighted * rows, axis=-1, keepdims=True)
        term[...] += jnp.sum(grad * rows * scale, axis=0, keepdims=True)
        result = (
            out_grad[strip, :].astype(jnp.float32)
            + scale * weighted
            - rows * scale * scale * scale * mean
        )
        grad_middle[strip, :] = result
        turned[strip, :] = result.astype(jnp.bfloat16)

    strips(middle.shape[0], body)
    gather_lines(Gather(line, turned, grad_all, scratch[9:]))


def input_kernel(chips, part, hidden, gain, grad_middle, input_grad, term, total, *scratch):
    line = Line(chips, False)
    line.meet()
    scatter_line(line, part, total, scratch)
    term[...] = jnp.zeros_like(term)

    def body(strip):
        grad = total[strip, :]
        rows = hidden[strip, :].astype(jnp.float32)
        scale = rms_scale(rows)
        weighted = grad * gain[...]
        mean = jnp.mean(weighted * rows, axis=-1, keepdims=True)
        term[...] += jnp.sum(grad * rows * scale, axis=0, keepdims=True)
        result = (
            grad_middle[strip, :] + scale * weighted - rows * scale * scale * scale * mean
        )
        input_grad[strip, :] = result.astype(jnp.bfloat16)

    strips(hidden.shape[0], body)


def remote_call(kernel, chips, inputs, outputs, scratch, number, micros, far=0):
    moved = sum(a.size * a.dtype.itemsize for a in inputs)
    return pl.pallas_call(
        functools.partial(kernel, chips),
        out_shape=[jax.ShapeDtypeStruct(shape, kind) for shape, kind, _ in outputs],
        in_specs=[pl.BlockSpec(memory_space=pltpu.VMEM)] * (len(inputs) - far)
        + [pl.BlockSpec(memory_space=pl.ANY)] * far,
        out_specs=[
            pl.BlockSpec(memory_space=pl.ANY if kept else pltpu.VMEM) for _, _, kept in outputs
        ],
        scratch_shapes=scratch,
        compiler_params=pltpu.CompilerParams(collective_id=number, has_side_effects=True),
        cost_estimate=pl.CostEstimate(
            flops=int(micros * 1e9), bytes_accessed=moved, transcendentals=0
        ),
    )(*inputs)

def bf16(values):
    return values.astype(jnp.bfloat16)


def two_parts(values):
    high = lax.reduce_precision(values, exponent_bits=8, mantissa_bits=7)
    return (bf16(high), bf16(values - high))


def mm(left, right):
    return jnp.dot(left, right, preferred_element_type=jnp.float32)


def mm_nt(left, right):
    return lax.dot_general(
        left, right, (((1,), (1,)), ((), ())), preferred_element_type=jnp.float32
    )


def mm_tn(left, right):
    return lax.dot_general(
        left, right, (((0,), (0,)), ((), ())), preferred_element_type=jnp.float32
    )


def group_device(
    hidden_in,
    out_grad,
    lengths,
    routes,
    norm1_gain,
    qkv_weight,
    qkv_bias,
    out_weight,
    norm2_gain,
    router_weight,
    shared_gate,
    shared_in,
    shared_out,
    expert_in,
    expert_out,
):
    size = lax.axis_size("expert")
    parts = lax.axis_size("dp")
    me = lax.axis_index("expert")
    core = me % 2
    rows, width = hidden_in.shape
    group = rows * size
    heads = width // HD
    own_heads = heads // size
    half = parts // 2
    places = size // 2
    block = width // (parts * size)
    top = routes.shape[1]
    experts = router_weight.shape[1]
    score_scale = HD ** (-0.5)
    bias_cols = 3 * width // (parts * size) // block
    extra = 128
    shared_block = shared_out.shape[0]
    expert_block = expert_out.shape[1]
    pair_block = expert_block + shared_block
    hidden_units = half * pair_block
    own_shared = parts * shared_block
    chips = places
    data = lax.axis_index("dp")
    side_by = data % 2
    above = data // 2
    slots = 2 * size
    slot = side_by * size + me
    swap_side = [(g, g ^ 1) for g in range(parts)]
    swap_above = [(g, g ^ 2) for g in range(parts)]
    own_qkv = 3 * own_heads * HD

    def by_head(columns):
        count = columns.shape[0]
        cut = columns.reshape(count, 3, 2, half, places, HD)
        return cut.transpose(4, 2, 0, 1, 3, 5).reshape(size, count, own_qkv)

    def from_head(pieces):
        count = pieces.shape[1]
        cut = pieces.reshape(places, 2, count, 3, half, HD)
        return cut.transpose(2, 3, 1, 4, 0, 5).reshape(count, 3 * width)

    def ordered(which, own, other, axis):
        first = jnp.where(which == 0, own, other)
        second = jnp.where(which == 0, other, own)
        return jnp.concatenate([first, second], axis=axis)

    def rows_of(values, first):
        return lax.dynamic_slice_in_dim(values, first * rows, rows, 0)

    small = jnp.concatenate(
        [
            norm1_gain[:, None],
            norm2_gain[:, None],
            shared_gate[:, None],
            router_weight,
            qkv_bias.reshape(block, bias_cols),
        ],
        axis=1,
    )
    small = jnp.pad(small, ((0, 0), (0, extra - small.shape[1])))
    first = jnp.concatenate(
        [by_head(qkv_weight), jnp.broadcast_to(small[None], (size, block, extra))], axis=2
    )
    first = lax.all_to_all(first, "expert", split_axis=0, concat_axis=0, tiled=True)
    first = first.reshape(size * block, own_qkv + extra)
    out_cols = width * block // (size * block)
    qkv_full = lax.all_gather(
        jnp.concatenate([first, out_weight.reshape(size * block, out_cols)], axis=1),
        "dp",
        axis=0,
        tiled=True,
    )

    down = jnp.concatenate([expert_out[0], shared_out], axis=0)
    down_came = lax.ppermute(down, "dp", swap_above)

    def units(values, count):
        cut = values.reshape(size * block, 2, half, 2, count)
        return cut.transpose(3, 1, 2, 4, 0).reshape(2, 2 * half * count, size * block)

    def aside(values):
        kept = lax.dynamic_index_in_dim(values, side_by, 0, keepdims=False)
        given = lax.dynamic_index_in_dim(values, 1 - side_by, 0, keepdims=False)
        return kept, lax.ppermute(given, "dp", swap_side)

    routed_kept, routed_came = aside(units(expert_in[0], expert_block))

    segment, position = segment_table(lengths[0], group)
    valid_all = (segment < lengths.shape[1] - 1).astype(jnp.float32)[:, None]
    valid_rows = rows_of(valid_all, me)
    grad_own = bf16(out_grad.astype(jnp.float32) * valid_rows)
    side = jnp.pad(bf16(routes), ((0, 0), (0, extra - top)))
    near, first = lax.optimization_barrier((hidden_in, first))
    (hidden_all,) = remote_call(
        gather_kernel,
        chips,
        [near],
        [((group, width), jnp.bfloat16, True)],
        gather_scratch(chips, False),
        0,
        40,
    )
    far = jnp.concatenate([grad_own, side], axis=1)
    far, qkv_full = lax.optimization_barrier((far, qkv_full))
    near_rows = lax.all_gather(far, "expert", axis=0, tiled=True)

    cut = shared_in.reshape(block, 2, parts, size, shared_block)
    cut = cut.transpose(3, 0, 1, 2, 4).reshape(size, block, 2 * own_shared)
    cut, hidden_all = lax.optimization_barrier((cut, hidden_all))
    cut = lax.all_to_all(cut, "expert", split_axis=0, concat_axis=0, tiled=True)
    shared_kept, shared_came = aside(units(cut.reshape(size * block, 2 * own_shared), shared_block))
    hidden_all = hidden_all.astype(jnp.float32)

    weight_qkv = qkv_full[:, :own_qkv]
    small = qkv_full[:, own_qkv : own_qkv + extra]
    gain_one = small[:, 0].astype(jnp.float32)
    gain_two = small[:, 1].astype(jnp.float32)
    router_rows = jnp.pad(small[:, 2 : 3 + experts].T, ((0, 127 - experts), (0, 0)))
    bias_all = by_head(small[:, 3 + experts : 3 + experts + bias_cols].reshape(1, 3 * width))
    bias_own = lax.dynamic_index_in_dim(bias_all, me, 0, keepdims=False).astype(jnp.float32)

    swap = [(i, i ^ 1) for i in range(size)]

    def own_half(values):
        return lax.dynamic_slice_in_dim(values, core * half, half, 0)

    def other_half(values):
        return lax.dynamic_slice_in_dim(values, (1 - core) * half, half, 0)

    out_blocks = qkv_full[:, own_qkv + extra :].reshape(parts, block, width)
    kept = own_half(out_blocks)
    came = lax.ppermute(other_half(out_blocks), "expert", swap)
    weight_out = jnp.stack(
        [jnp.where(core == 0, kept, came), jnp.where(core == 0, came, kept)], axis=1
    ).reshape(own_heads * HD, width)

    cosine, sine = rotary_tables(position, HD)
    allowed = (
        (segment[:, None] == segment[None, :]) & (position[:, None] >= position[None, :])
    )[None]
    normed_one = bf16(hidden_all * rms_scale(hidden_all) * gain_one)
    projected = mm(normed_one, weight_qkv) + bias_own
    split = projected.reshape(group, 3, own_heads, HD)
    query_low = bf16(rotate(split[:, 0], cosine, sine))
    key_low = bf16(rotate(split[:, 1], cosine, sine))
    value_low = bf16(split[:, 2])

    def score_rows():
        raw = (
            jnp.einsum("qhd,khd->hqk", query_low, key_low, preferred_element_type=jnp.float32)
            * score_scale
        )
        return jnp.where(allowed, raw, NEG_FILL)

    scores = score_rows()
    peak = jnp.max(scores, axis=-1, keepdims=True)
    log_total = peak + jnp.log(jnp.sum(jnp.exp(scores - peak), axis=-1, keepdims=True))
    weights_low = bf16(jnp.exp(scores - log_total))
    attended = bf16(
        jnp.einsum(
            "hqk,khd->qhd", weights_low, value_low, preferred_element_type=jnp.float32
        ).reshape(group, own_heads * HD)
    )
    part = bf16(mm(attended, weight_out))
    part, near_rows, routed_came, shared_came = lax.optimization_barrier(
        (part, near_rows, routed_came, shared_came)
    )
    routed_up = ordered(side_by, routed_kept, routed_came, 1)
    routed_came = lax.ppermute(routed_up, "dp", swap_above)
    shared_up = ordered(side_by, shared_kept, shared_came, 1)
    shared_came = lax.ppermute(shared_up, "dp", swap_above)
    part, routed_up, shared_up = lax.optimization_barrier((part, routed_up, shared_up))
    middle, normed_all, far_rows = remote_call(
        middle_kernel,
        chips,
        [part, hidden_in, gain_two[None, :], near_rows],
        [
            ((rows, width), jnp.float32, False),
            ((2 * group, width), jnp.bfloat16, True),
            ((group, width + extra), jnp.bfloat16, True),
        ],
        [pltpu.VMEM((rows, width), jnp.float32), pltpu.VMEM((rows, width), jnp.bfloat16)]
        + scatter_scratch(chips, rows, width, False)
        + gather_scratch(chips, True)
        + aside_scratch(chips),
        1,
        85,
        1,
    )

    normed_all, routed_came, shared_came, down_came = lax.optimization_barrier(
        (normed_all, routed_came, shared_came, down_came)
    )
    weight_down = ordered(above, down, down_came, 0)
    grad_rows = jnp.concatenate([near_rows[:, :width], far_rows[:, :width]], axis=0)
    routes_all = jnp.concatenate(
        [near_rows[:, width : width + top], far_rows[:, width : width + top]], axis=0
    ).astype(jnp.int32)
    weight_up = jnp.concatenate(
        [
            ordered(above, routed_up, routed_came, 1).reshape(2, half, expert_block, width),
            ordered(above, shared_up, shared_came, 1).reshape(2, half, shared_block, width),
        ],
        axis=2,
    ).reshape(2 * hidden_units, width)

    gate_logits = mm_nt(normed_all, router_rows)
    logits = gate_logits[:, 1 : 1 + experts]
    opener_all = jax.nn.sigmoid(gate_logits[:, :1])
    peak_logit = jnp.max(logits, axis=-1, keepdims=True)
    router_total = peak_logit + jnp.log(
        jnp.sum(jnp.exp(logits - peak_logit), axis=-1, keepdims=True)
    )
    probs_all = jnp.exp(logits - router_total)
    expert_ids = jnp.arange(experts, dtype=jnp.int32)
    mine = expert_ids[None, :] == me
    named = jnp.sum((routes_all == me).astype(jnp.float32), axis=1, keepdims=True)
    gate_own = named * jnp.sum(jnp.where(mine, probs_all, 0.0), axis=1, keepdims=True)

    routed_unit = (jnp.arange(hidden_units, dtype=jnp.int32) % pair_block < expert_block)[:, None]
    unit_scale = jnp.where(routed_unit, gate_own.T, opener_all.T)
    both_up = mm_nt(weight_up, normed_all)
    gate_part = both_up[:hidden_units]
    up_part = both_up[hidden_units:]
    hidden = bf16(jax.nn.silu(gate_part) * up_part)
    scaled_hidden = bf16(unit_scale * hidden.astype(jnp.float32))

    def half_rows(values, which):
        return lax.dynamic_slice_in_dim(values, which * pair_block, pair_block, 0)

    sent_down = bf16(mm(half_rows(scaled_hidden, 1 - above), grad_rows))
    term_down = mm(half_rows(scaled_hidden, above), grad_rows)
    came_down = lax.ppermute(sent_down, "dp", swap_above)
    near_part = bf16(mm_tn(scaled_hidden[:, :group], weight_down))
    far_part = bf16(mm_tn(scaled_hidden[:, group:], weight_down))
    near_sum = lax.psum_scatter(near_part, "expert", scatter_dimension=0, tiled=True)
    far_sum = lax.psum_scatter(far_part, "expert", scatter_dimension=0, tiled=True)
    far_came = lax.ppermute(far_sum, "dp", swap_side)

    grad_hidden = mm_nt(weight_down, grad_rows)
    product = hidden.astype(jnp.float32) * grad_hidden
    dot_expert = named * jnp.sum(jnp.where(routed_unit, product, 0.0), axis=0)[:, None]
    dot_shared = jnp.sum(jnp.where(routed_unit, 0.0, product), axis=0)[:, None]
    grad_hidden = grad_hidden * unit_scale
    sigmoid_gate = jax.nn.sigmoid(gate_part)
    grad_gate = grad_hidden * up_part * sigmoid_gate * (1.0 + gate_part * (1.0 - sigmoid_gate))
    grad_up = grad_hidden * gate_part * sigmoid_gate
    grad_both_up = jnp.concatenate([bf16(grad_gate), bf16(grad_up)], axis=0)
    half_width = width // 2

    def half_cols(values, which):
        return lax.dynamic_slice_in_dim(values, which * half_width, half_width, 1)

    sent_up = bf16(mm(grad_both_up, half_cols(normed_all, 1 - above)))
    came_up = lax.ppermute(sent_up, "dp", swap_above)
    term_up = mm(grad_both_up, half_cols(normed_all, above))

    taken = jnp.arange(slots, dtype=jnp.int32)[None, :] == slot
    zero = jnp.zeros((), jnp.bfloat16)
    riders = jnp.concatenate(
        [
            jnp.where(taken, column, zero)
            for column in two_parts(dot_shared) + two_parts(dot_expert)
        ],
        axis=1,
    )
    riders = jnp.pad(riders, ((0, 0), (0, extra - riders.shape[1])))
    part = jnp.concatenate([bf16(mm_tn(grad_both_up, weight_up)), riders], axis=1)
    part, sent_up, sent_down, near_part, far_part = lax.optimization_barrier(
        (part, sent_up, sent_down, near_part, far_part)
    )

    rider = jnp.arange(extra, dtype=jnp.int32)[:, None]
    lane = jnp.arange(128, dtype=jnp.int32)[None, :]
    collect = bf16(
        ((rider < 2 * slots) & (lane == 0))
        | ((rider >= 2 * slots) & (rider < 4 * slots) & (lane == 1 + rider % size))
    )
    probs = jnp.pad(
        rows_of(jnp.concatenate([opener_all, probs_all], axis=1), me),
        ((0, 0), (0, 127 - experts)),
    )
    grad_middle, grad_branch, grad_heads, term_norm_two = remote_call(
        branch_kernel,
        chips,
        [part, middle, gain_two[None, :], grad_own, probs, collect, router_rows],
        [
            ((rows, width), jnp.float32, False),
            ((group, width), jnp.bfloat16, True),
            ((rows, 128), jnp.bfloat16, False),
            ((1, width), jnp.float32, False),
        ],
        [
            pltpu.VMEM((rows, width + extra), jnp.float32),
            pltpu.VMEM((rows, width), jnp.bfloat16),
        ]
        + scatter_scratch(chips, rows, width + extra, True)
        + gather_scratch(chips, False),
        2,
        90,
    )
    grad_branch, came_up = lax.optimization_barrier((grad_branch, came_up))
    term_router = mm_tn(rows_of(normed_all, me), grad_heads)[:, : 1 + experts]

    up = bf16(term_up + came_up.astype(jnp.float32))
    quarter = half_width // 2
    side_kept = lax.dynamic_slice_in_dim(up, side_by * quarter, quarter, 1)
    side_came = lax.ppermute(
        lax.dynamic_slice_in_dim(up, (1 - side_by) * quarter, quarter, 1), "dp", swap_side
    )

    grad_attended = bf16(mm_nt(grad_branch, weight_out)).reshape(group, own_heads, HD)
    weights_again = jnp.exp(score_rows() - log_total)
    grad_weights = jnp.einsum(
        "qhd,khd->hqk", grad_attended, value_low, preferred_element_type=jnp.float32
    )
    delta_rows = jnp.sum(weights_again * grad_weights, axis=-1, keepdims=True)
    grad_scores = bf16(weights_again * (grad_weights - delta_rows))
    grad_query_turned = (
        jnp.einsum("hqk,khd->qhd", grad_scores, key_low, preferred_element_type=jnp.float32)
        * score_scale
    )
    grad_key_turned = (
        jnp.einsum("hqk,qhd->khd", grad_scores, query_low, preferred_element_type=jnp.float32)
        * score_scale
    )
    grad_values = jnp.einsum(
        "hqk,qhd->khd", bf16(weights_again), grad_attended, preferred_element_type=jnp.float32
    )
    grad_projected = bf16(
        jnp.stack(
            [
                rotate_back(grad_query_turned, cosine, sine),
                rotate_back(grad_key_turned, cosine, sine),
                grad_values,
            ],
            axis=1,
        ).reshape(group, own_qkv)
    )
    part = bf16(mm_nt(grad_projected, weight_qkv))
    term_out = bf16(mm_tn(attended, grad_branch)).reshape(half, 2, block, width)
    kept = jnp.where(core == 0, term_out[:, 0], term_out[:, 1])
    given = jnp.where(core == 0, term_out[:, 1], term_out[:, 0])
    came = lax.ppermute(given, "expert", swap)
    out_blocks = jnp.concatenate(
        [jnp.where(core == 0, kept, came), jnp.where(core == 0, came, kept)], axis=0
    )
    back = jnp.concatenate(
        [bf16(mm_tn(normed_one, grad_projected)), out_blocks.reshape(width, out_cols)], axis=1
    )
    part, back, came_down, near_sum, far_sum = lax.optimization_barrier(
        (part, back, came_down, near_sum, far_sum)
    )
    back = lax.psum_scatter(back, "dp", scatter_dimension=0, tiled=True)
    grad_out_weight = back[:, own_qkv:].reshape(block, width).astype(jnp.float32)
    input_grad, term_norm_one = remote_call(
        input_kernel,
        chips,
        [part, hidden_in, gain_one[None, :], grad_middle],
        [((rows, width), jnp.bfloat16, False), ((1, width), jnp.float32, False)],
        [pltpu.VMEM((rows, width), jnp.float32)] + scatter_scratch(chips, rows, width, False),
        3,
        40,
    )
    grad_down = term_down + came_down.astype(jnp.float32)
    grad_shared_out = grad_down[expert_block:]
    grad_expert_out = grad_down[None, :expert_block]
    up = ordered(side_by, side_kept[None], side_came[None], 0)
    up = up.reshape(2, 2, half, pair_block, quarter)
    grad_expert_in = (
        up[:, :, :, :expert_block]
        .transpose(4, 1, 2, 0, 3)
        .reshape(1, quarter, 2 * parts * expert_block)
        .astype(jnp.float32)
    )
    cut = lax.all_to_all(
        up[:, :, :, expert_block:].transpose(4, 1, 2, 0, 3).reshape(size, block, 2 * own_shared),
        "expert",
        split_axis=0,
        concat_axis=0,
        tiled=True,
    )
    grad_shared_in = (
        cut.reshape(size, block, 2, parts, shared_block)
        .transpose(1, 2, 3, 0, 4)
        .reshape(block, 2 * parts * size * shared_block)
        .astype(jnp.float32)
    )
    back = lax.all_to_all(
        back[:, :own_qkv].reshape(size, block, own_qkv),
        "expert",
        split_axis=0,
        concat_axis=0,
        tiled=True,
    )
    grad_qkv = from_head(back).astype(jnp.float32)

    term_bias = jnp.sum(grad_projected.astype(jnp.float32), axis=0)
    bias_slots = jnp.where(jnp.arange(size)[:, None] == me, term_bias[None, :], 0.0)
    bias_rows = from_head(bias_slots[:, None, :]).reshape(width, bias_cols)
    small_terms = jnp.concatenate(
        [term_norm_one[0][:, None], term_norm_two[0][:, None], term_router, bias_rows], axis=1
    )
    count = small_terms.shape[1]
    small_terms = lax.all_to_all(
        small_terms.T.reshape(count, parts * size, block).transpose(1, 0, 2),
        ("dp", "expert"),
        split_axis=0,
        concat_axis=0,
        tiled=True,
    )
    small_sum = jnp.sum(small_terms, axis=0)
    output = bf16(
        valid_rows * (middle + near_sum.astype(jnp.float32) + far_came.astype(jnp.float32))
    )
    grad_norm1 = small_sum[0]
    grad_norm2 = small_sum[1]
    grad_shared_gate = small_sum[2]
    grad_router = small_sum[3 : 3 + experts].T
    grad_bias = small_sum[3 + experts :].T.reshape(block * bias_cols)
    return (
        output,
        input_grad,
        grad_norm1,
        grad_qkv,
        grad_bias,
        grad_out_weight,
        grad_norm2,
        grad_router,
        grad_shared_gate,
        grad_shared_in,
        grad_shared_out,
        grad_expert_in,
        grad_expert_out,
    )


def solution(mesh):
    size, parts = mesh.shape["expert"], mesh.shape["dp"]

    def device(*arrays):
        block = arrays[5].shape[0]
        whole_heads = 2 * block == HD and parts == 4 and size % 2 == 0
        one_expert = arrays[13].shape[0] == 1
        if whole_heads and one_expert and arrays[5].shape[1] % (3 * size * HD) == 0:
            return group_device(*arrays)
        return per_device(*arrays)

    return jax.shard_map(
        device,
        mesh=mesh,
        in_specs=(
            P(("dp", "expert"), None),
            P(("dp", "expert"), None),
            P("dp", None),
            P(("dp", "expert"), None),
            P(("dp", "expert")),
            P(("dp", "expert"), None),
            P(("dp", "expert")),
            P(("dp", "expert"), None),
            P(("dp", "expert")),
            P(("dp", "expert"), None),
            P(("dp", "expert")),
            P(("dp", "expert"), None),
            P(("dp", "expert"), None),
            P("expert", "dp", None),
            P("expert", "dp", None),
        ),
        out_specs=(
            P(("dp", "expert"), None),
            P(("dp", "expert"), None),
            P(("dp", "expert")),
            P(("dp", "expert"), None),
            P(("dp", "expert")),
            P(("dp", "expert"), None),
            P(("dp", "expert")),
            P(("dp", "expert"), None),
            P(("dp", "expert")),
            P(("dp", "expert"), None),
            P(("dp", "expert"), None),
            P("expert", "dp", None),
            P("expert", "dp", None),
        ),
        check_vma=False,
    )
```

```python
import functools

import jax
import jax.numpy as jnp
from jax import lax
from jax.experimental import pallas as pl
from jax.experimental.pallas import tpu as pltpu
from jax.sharding import PartitionSpec as P

HD = 128


EPSILON = 1e-06
THETA = 1000000.0
NEG_FILL = -1e30


def rms_scale(values):
    return lax.rsqrt(jnp.mean(values * values, axis=-1, keepdims=True) + EPSILON)


def rotary_tables(positions, head_size):
    half_size = head_size // 2
    steps_up = jnp.arange(half_size, dtype=jnp.float32) * (2.0 / head_size)
    inverse = THETA ** (-steps_up)
    angles = positions.astype(jnp.float32)[:, None] * inverse[None, :]
    angles = jnp.concatenate([angles, angles], axis=-1)
    return (jnp.cos(angles)[:, None, :], jnp.sin(angles)[:, None, :])


def rotate(values, cosine, sine):
    half_size = values.shape[-1] // 2
    turned = jnp.concatenate([-values[..., half_size:], values[..., :half_size]], axis=-1)
    return values * cosine + turned * sine


def rotate_back(grad_values, cosine, sine):
    half_size = grad_values.shape[-1] // 2
    scaled = grad_values * sine
    turned = jnp.concatenate([scaled[..., half_size:], -scaled[..., :half_size]], axis=-1)
    return grad_values * cosine + turned


def swiglu(gate_up):
    half_size = gate_up.shape[-1] // 2
    return jax.nn.silu(gate_up[..., :half_size]) * gate_up[..., half_size:]


def swiglu_back(gate_up, grad_hidden):
    half_size = gate_up.shape[-1] // 2
    gate_part = gate_up[..., :half_size]
    up_part = gate_up[..., half_size:]
    sigmoid_gate = jax.nn.sigmoid(gate_part)
    grad_gate = grad_hidden * up_part * sigmoid_gate * (1.0 + gate_part * (1.0 - sigmoid_gate))
    grad_up = grad_hidden * gate_part * sigmoid_gate
    return jnp.concatenate([grad_gate, grad_up], axis=-1)


def norm_back(values, scale_rows, gain, grad_normed):
    weighted = grad_normed * gain
    inner = jnp.mean(weighted * values, axis=-1, keepdims=True)
    grad_values = scale_rows * weighted - values * scale_rows * scale_rows * scale_rows * inner
    grad_gain = jnp.sum(grad_normed * values * scale_rows, axis=0)
    return (grad_values, grad_gain)


def segment_table(length_row, count):
    ends = jnp.cumsum(length_row, dtype=jnp.int32)
    starts = ends - length_row
    places = jnp.arange(count, dtype=jnp.int32)
    segment = jnp.sum(
        (places[:, None] >= ends[None, :-1]).astype(jnp.int32), axis=1, dtype=jnp.int32
    )
    owners = segment[:, None] == jnp.arange(length_row.shape[0], dtype=jnp.int32)[None, :]
    first = jnp.sum(jnp.where(owners, starts[None, :], 0), axis=1, dtype=jnp.int32)
    return (segment, places - first)


def per_device(
    hidden_in,
    out_grad,
    lengths,
    routes,
    norm1_gain,
    qkv_weight,
    qkv_bias,
    out_weight,
    norm2_gain,
    router_weight,
    shared_gate,
    shared_in,
    shared_out,
    expert_in,
    expert_out,
):
    highest = lax.Precision.HIGHEST
    row_count, model_width = hidden_in.shape
    head_count = model_width // HD
    group_size = lax.axis_size("expert")
    group_rows = row_count * group_size
    top_count = routes.shape[1]
    expert_count = router_weight.shape[1]
    local_count = expert_in.shape[0]
    capacity = max(2, 2 * row_count * top_count // expert_count)
    slot_count = expert_count * capacity
    score_scale = HD ** (-0.5)
    dense = (
        lax.all_gather(norm1_gain, ("dp", "expert"), axis=0, tiled=True),
        lax.all_gather(qkv_weight, ("dp", "expert"), axis=0, tiled=True),
        lax.all_gather(qkv_bias, ("dp", "expert"), axis=0, tiled=True),
        lax.all_gather(out_weight, ("dp", "expert"), axis=0, tiled=True),
        lax.all_gather(norm2_gain, ("dp", "expert"), axis=0, tiled=True),
        lax.all_gather(router_weight, ("dp", "expert"), axis=0, tiled=True),
        lax.all_gather(shared_gate, ("dp", "expert"), axis=0, tiled=True),
        lax.all_gather(shared_in, ("dp", "expert"), axis=0, tiled=True),
        lax.all_gather(shared_out, ("dp", "expert"), axis=0, tiled=True),
    )
    (
        gain_first,
        weight_qkv,
        bias_first,
        weight_out,
        gain_second,
        weight_router,
        weight_gate,
        weight_shared_in,
        weight_shared_out,
    ) = dense
    weight_expert_in, weight_expert_out = (
        lax.all_gather(expert_in, "dp", axis=1, tiled=True),
        lax.all_gather(expert_out, "dp", axis=1, tiled=True),
    )
    segment_all, position_all = segment_table(lengths[0], group_rows)
    first_row = lax.axis_index("expert") * row_count
    segment_mine = lax.dynamic_slice_in_dim(segment_all, first_row, row_count, 0)
    position_mine = lax.dynamic_slice_in_dim(position_all, first_row, row_count, 0)
    valid_rows = (segment_mine < lengths.shape[1] - 1).astype(jnp.float32)[:, None]
    cosine, sine = rotary_tables(position_mine, HD)
    allowed = (
        (segment_mine[:, None] == segment_all[None, :])
        & (position_mine[:, None] >= position_all[None, :])
    )[None]
    inputs = hidden_in.astype(jnp.float32)
    scale_first = rms_scale(inputs)
    gain_one = gain_first.astype(jnp.float32)
    normed_one = (inputs * scale_first * gain_one).astype(jnp.bfloat16)
    projected = jnp.dot(
        normed_one, weight_qkv, preferred_element_type=jnp.float32
    ) + bias_first.astype(jnp.float32)
    query_low = rotate(
        projected[:, :model_width].reshape(row_count, head_count, HD), cosine, sine
    ).astype(jnp.bfloat16)
    key_low = rotate(
        projected[:, model_width : 2 * model_width].reshape(row_count, head_count, HD), cosine, sine
    ).astype(jnp.bfloat16)
    value_low = (
        projected[:, 2 * model_width :].reshape(row_count, head_count, HD).astype(jnp.bfloat16)
    )
    keys_all, values_all = (
        lax.all_gather(key_low, "expert", axis=0, tiled=True),
        lax.all_gather(value_low, "expert", axis=0, tiled=True),
    )

    def score_rows(queries):
        raw = (
            jnp.einsum("qhd,khd->hqk", queries, keys_all, preferred_element_type=jnp.float32)
            * score_scale
        )
        return jnp.where(allowed, raw, NEG_FILL)

    scores = score_rows(query_low)
    peak = jnp.max(scores, axis=-1, keepdims=True)
    log_total = peak + jnp.log(jnp.sum(jnp.exp(scores - peak), axis=-1, keepdims=True))
    weights_low = jnp.exp(scores - log_total).astype(jnp.bfloat16)
    attended = (
        jnp.einsum("hqk,khd->qhd", weights_low, values_all, preferred_element_type=jnp.float32)
        .reshape(row_count, model_width)
        .astype(jnp.bfloat16)
    )
    middle = inputs + jnp.dot(attended, weight_out, preferred_element_type=jnp.float32)
    scale_second = rms_scale(middle)
    gain_two = gain_second.astype(jnp.float32)
    normed_two = (middle * scale_second * gain_two).astype(jnp.bfloat16)
    logits = jnp.dot(normed_two, weight_router, preferred_element_type=jnp.float32)
    gate_logit = jnp.dot(normed_two, weight_gate, preferred_element_type=jnp.float32)
    peak_logit = jnp.max(logits, axis=-1, keepdims=True)
    router_total = peak_logit + jnp.log(
        jnp.sum(jnp.exp(logits - peak_logit), axis=-1, keepdims=True)
    )
    router_probs = jnp.exp(logits - router_total)
    expert_ids = jnp.arange(expert_count, dtype=jnp.int32)
    chosen = routes[:, :, None] == expert_ids[None, None, :]
    chosen_float = chosen.astype(jnp.float32)
    gates = jnp.sum(chosen_float * router_probs[:, None, :], axis=2)
    flat_hits = chosen.reshape(row_count * top_count, expert_count).astype(jnp.int32)
    earlier = jnp.cumsum(flat_hits, axis=0, dtype=jnp.int32) - flat_hits
    slot_rank = jnp.sum(earlier * flat_hits, axis=1, dtype=jnp.int32)
    slot_of = routes.reshape(-1) * capacity + slot_rank
    slot_hits = (
        (slot_of[:, None] == jnp.arange(slot_count, dtype=jnp.int32)[None, :])
        .reshape(row_count, top_count, slot_count)
        .astype(jnp.float32)
    )
    placement_map = jnp.sum(slot_hits, axis=1)
    weighted_map = jnp.sum(slot_hits * gates[:, :, None], axis=1)
    send_rows = (
        jnp.einsum(
            "ts,td->sd",
            placement_map.astype(jnp.bfloat16),
            normed_two,
            preferred_element_type=jnp.float32,
        )
        .astype(jnp.bfloat16)
        .reshape(expert_count, capacity, model_width)
    )
    arrived = lax.all_to_all(send_rows, "expert", split_axis=0, concat_axis=0, tiled=True)
    item_count = arrived.shape[1]
    grouped = arrived.reshape(group_size, local_count, item_count, model_width)
    gate_up = jnp.einsum(
        "gecd,edf->gecf", grouped, weight_expert_in, preferred_element_type=jnp.float32
    )
    hidden_low = swiglu(gate_up).astype(jnp.bfloat16)
    produced = jnp.einsum(
        "gecf,efd->gecd", hidden_low, weight_expert_out, preferred_element_type=jnp.float32
    ).astype(jnp.bfloat16)
    produced_rows = produced.reshape(group_size * local_count, item_count, model_width)
    expert_gate_up = gate_up.reshape(group_size * local_count, item_count, gate_up.shape[-1])
    back_rows = lax.all_to_all(produced_rows, "expert", split_axis=0, concat_axis=0, tiled=True)
    back_float = back_rows.reshape(slot_count, model_width).astype(jnp.float32)
    routed = jnp.dot(weighted_map, back_float, precision=highest)
    shared_up = jnp.dot(normed_two, weight_shared_in, preferred_element_type=jnp.float32)
    shared_hidden = swiglu(shared_up).astype(jnp.bfloat16)
    shared_rows = jnp.dot(shared_hidden, weight_shared_out, preferred_element_type=jnp.float32)
    opener = jax.nn.sigmoid(gate_logit)[:, None]
    output = (valid_rows * (middle + routed + opener * shared_rows)).astype(jnp.bfloat16)
    held = (
        lax.all_gather(norm1_gain, ("dp", "expert"), axis=0, tiled=True),
        lax.all_gather(qkv_weight, ("dp", "expert"), axis=0, tiled=True),
        lax.all_gather(qkv_bias, ("dp", "expert"), axis=0, tiled=True),
        lax.all_gather(out_weight, ("dp", "expert"), axis=0, tiled=True),
        lax.all_gather(norm2_gain, ("dp", "expert"), axis=0, tiled=True),
        lax.all_gather(router_weight, ("dp", "expert"), axis=0, tiled=True),
        lax.all_gather(shared_gate, ("dp", "expert"), axis=0, tiled=True),
        lax.all_gather(shared_in, ("dp", "expert"), axis=0, tiled=True),
        lax.all_gather(shared_out, ("dp", "expert"), axis=0, tiled=True),
    )
    (
        gain_first,
        weight_qkv,
        bias_first,
        weight_out,
        gain_second,
        weight_router,
        weight_gate,
        weight_shared_in,
        weight_shared_out,
    ) = held
    gain_one = gain_first.astype(jnp.float32)
    gain_two = gain_second.astype(jnp.float32)
    grad_rows = out_grad.astype(jnp.float32) * valid_rows
    grad_shared_rows = (grad_rows * opener).astype(jnp.bfloat16)
    grad_gate_logit = (
        jnp.sum(grad_rows * shared_rows, axis=-1) * opener[:, 0] * (1.0 - opener[:, 0])
    ).astype(jnp.bfloat16)
    grad_shared_hidden = jnp.einsum(
        "td,fd->tf", grad_shared_rows, weight_shared_out, preferred_element_type=jnp.float32
    )
    grad_shared_up = swiglu_back(shared_up, grad_shared_hidden).astype(jnp.bfloat16)
    term_shared_out = jnp.einsum(
        "tf,td->fd", shared_hidden, grad_shared_rows, preferred_element_type=jnp.float32
    )
    term_shared_in = jnp.einsum(
        "td,tf->df", normed_two, grad_shared_up, preferred_element_type=jnp.float32
    )
    slot_product = jnp.einsum("td,sd->ts", grad_rows, back_float, precision=highest)
    grad_gates = jnp.sum(slot_hits * slot_product[:, None, :], axis=2)
    grad_probs = jnp.sum(chosen_float * grad_gates[:, :, None], axis=1)
    grad_logits = (
        router_probs * (grad_probs - jnp.sum(router_probs * grad_probs, axis=-1, keepdims=True))
    ).astype(jnp.bfloat16)
    term_router = jnp.einsum(
        "td,te->de", normed_two, grad_logits, preferred_element_type=jnp.float32
    )
    term_gate = jnp.einsum(
        "td,t->d", normed_two, grad_gate_logit, preferred_element_type=jnp.float32
    )
    grad_result = (
        jnp.einsum("ts,td->sd", weighted_map, grad_rows, precision=highest)
        .astype(jnp.bfloat16)
        .reshape(expert_count, capacity, model_width)
    )
    grad_arrived = lax.all_to_all(grad_result, "expert", split_axis=0, concat_axis=0, tiled=True)
    grad_grouped = grad_arrived.reshape(group_size, local_count, capacity, model_width)
    gate_up_grouped = expert_gate_up.reshape(
        group_size, local_count, capacity, expert_gate_up.shape[-1]
    )
    hidden_again = swiglu(gate_up_grouped).astype(jnp.bfloat16)
    grad_hidden = jnp.einsum(
        "gecd,efd->gecf", grad_grouped, weight_expert_out, preferred_element_type=jnp.float32
    )
    grad_gate_up = swiglu_back(gate_up_grouped, grad_hidden).astype(jnp.bfloat16)
    arrived_grouped = arrived.reshape(group_size, local_count, capacity, model_width)
    term_expert_in = jnp.einsum(
        "gecd,gecf->edf", arrived_grouped, grad_gate_up, preferred_element_type=jnp.float32
    )
    term_expert_out = jnp.einsum(
        "gecf,gecd->efd", hidden_again, grad_grouped, preferred_element_type=jnp.float32
    )
    grad_sent = jnp.einsum(
        "gecf,edf->gecd", grad_gate_up, weight_expert_in, preferred_element_type=jnp.float32
    ).reshape(group_size * local_count, capacity, model_width)
    grad_slots = lax.all_to_all(
        grad_sent.astype(jnp.bfloat16), "expert", split_axis=0, concat_axis=0, tiled=True
    ).astype(grad_sent.dtype)
    grad_expert_in, grad_expert_out = (
        lax.psum_scatter(
            term_expert_in.astype(jnp.bfloat16), "dp", scatter_dimension=1, tiled=True
        ).astype(jnp.float32),
        lax.psum_scatter(
            term_expert_out.astype(jnp.bfloat16), "dp", scatter_dimension=1, tiled=True
        ).astype(jnp.float32),
    )
    grad_normed_two = jnp.einsum(
        "te,de->td", grad_logits, weight_router, preferred_element_type=jnp.float32
    )
    grad_normed_two = (
        grad_normed_two
        + grad_gate_logit.astype(jnp.float32)[:, None] * weight_gate.astype(jnp.float32)[None, :]
    )
    grad_normed_two = grad_normed_two + jnp.einsum(
        "tf,df->td", grad_shared_up, weight_shared_in, preferred_element_type=jnp.float32
    )
    grad_normed_two = grad_normed_two + jnp.dot(
        placement_map, grad_slots.reshape(slot_count, model_width), precision=highest
    )
    grad_middle_norm, term_norm_two = norm_back(middle, scale_second, gain_two, grad_normed_two)
    grad_middle = grad_rows + grad_middle_norm
    grad_norm2, grad_router, grad_shared_gate, grad_shared_in, grad_shared_out = (
        lax.psum_scatter(term_norm_two, ("dp", "expert"), scatter_dimension=0, tiled=True),
        lax.psum_scatter(term_router, ("dp", "expert"), scatter_dimension=0, tiled=True),
        lax.psum_scatter(term_gate, ("dp", "expert"), scatter_dimension=0, tiled=True),
        lax.psum_scatter(term_shared_in, ("dp", "expert"), scatter_dimension=0, tiled=True),
        lax.psum_scatter(term_shared_out, ("dp", "expert"), scatter_dimension=0, tiled=True),
    )
    grad_branch = grad_middle.astype(jnp.bfloat16)
    term_out_weight = jnp.einsum(
        "td,te->de", attended, grad_branch, preferred_element_type=jnp.float32
    )
    grad_attended = (
        jnp.einsum("te,de->td", grad_branch, weight_out, preferred_element_type=jnp.float32)
        .astype(jnp.bfloat16)
        .reshape(row_count, head_count, HD)
    )
    weights_again = jnp.exp(score_rows(query_low) - log_total)
    weights_again_low = weights_again.astype(jnp.bfloat16)
    grad_weights = jnp.einsum(
        "qhd,khd->hqk", grad_attended, values_all, preferred_element_type=jnp.float32
    )
    delta_rows = jnp.sum(weights_again * grad_weights, axis=-1, keepdims=True)
    grad_scores = (weights_again * (grad_weights - delta_rows)).astype(jnp.bfloat16)
    grad_query_turned = (
        jnp.einsum("hqk,khd->qhd", grad_scores, keys_all, preferred_element_type=jnp.float32)
        * score_scale
    )
    grad_keys_all = (
        jnp.einsum("hqk,qhd->khd", grad_scores, query_low, preferred_element_type=jnp.float32)
        * score_scale
    )
    grad_values_all = jnp.einsum(
        "hqk,qhd->khd", weights_again_low, grad_attended, preferred_element_type=jnp.float32
    )
    grad_key_turned, grad_values = (
        lax.psum_scatter(
            grad_keys_all.astype(jnp.bfloat16), "expert", scatter_dimension=0, tiled=True
        ).astype(jnp.float32),
        lax.psum_scatter(
            grad_values_all.astype(jnp.bfloat16), "expert", scatter_dimension=0, tiled=True
        ).astype(jnp.float32),
    )
    grad_projected = jnp.concatenate(
        [
            rotate_back(grad_query_turned, cosine, sine).reshape(row_count, model_width),
            rotate_back(grad_key_turned, cosine, sine).reshape(row_count, model_width),
            grad_values.reshape(row_count, model_width),
        ],
        axis=-1,
    ).astype(jnp.bfloat16)
    term_bias = jnp.sum(grad_projected.astype(jnp.float32), axis=0)
    term_qkv = jnp.einsum(
        "td,tf->df", normed_one, grad_projected, preferred_element_type=jnp.float32
    )
    grad_normed_one = jnp.einsum(
        "tf,df->td", grad_projected, weight_qkv, preferred_element_type=jnp.float32
    )
    grad_input_norm, term_norm_one = norm_back(inputs, scale_first, gain_one, grad_normed_one)
    input_grad = (grad_middle + grad_input_norm).astype(jnp.bfloat16)
    grad_norm1, grad_qkv, grad_bias, grad_out_weight = (
        lax.psum_scatter(term_norm_one, ("dp", "expert"), scatter_dimension=0, tiled=True),
        lax.psum_scatter(term_qkv, ("dp", "expert"), scatter_dimension=0, tiled=True),
        lax.psum_scatter(term_bias, ("dp", "expert"), scatter_dimension=0, tiled=True),
        lax.psum_scatter(term_out_weight, ("dp", "expert"), scatter_dimension=0, tiled=True),
    )
    return (
        output,
        input_grad,
        grad_norm1,
        grad_qkv,
        grad_bias,
        grad_out_weight,
        grad_norm2,
        grad_router,
        grad_shared_gate,
        grad_shared_in,
        grad_shared_out,
        grad_expert_in,
        grad_expert_out,
    )


MESH_IDS = pl.DeviceIdType.MESH
STRIP = 16


class Line:
    def __init__(self, chips):
        me = lax.axis_index("expert")
        self.chips = chips
        self.z = me // 2
        self.core = lax.rem(me, 2)
        self.below = self.z > 0
        self.above = self.z < chips - 1

    def at(self, z, core):
        return {"expert": 2 * z + core}

    def meet(self):
        barrier = pltpu.get_barrier_semaphore()

        def hello(z, core):
            pl.semaphore_signal(
                barrier, inc=1, device_id=self.at(z, core), device_id_type=MESH_IDS
            )

        hello(self.z, 1 - self.core)
        pl.when(self.above)(lambda: hello(self.z + 1, self.core))
        pl.when(self.below)(lambda: hello(self.z - 1, self.core))
        peers = 1 + jnp.minimum(self.z, 1) + jnp.minimum(self.chips - 1 - self.z, 1)
        pl.semaphore_wait(barrier, peers)


def gather_scratch(chips):
    return [
        pltpu.SemaphoreType.DMA((2, chips - 1)),
        pltpu.SemaphoreType.DMA((2, chips - 1)),
        pltpu.SemaphoreType.DMA((2 * chips - 1,)),
        pltpu.SemaphoreType.DMA((2 * chips - 1,)),
        pltpu.SemaphoreType.DMA,
    ]


def gather_line(line, own, out, send, recv, pair_send, pair_recv, local):
    chips, z, core = line.chips, line.z, line.core
    rows = own.shape[0]

    def block(chip, which):
        return out.at[pl.ds((2 * chip + which) * rows, rows)]

    def hop(step, up):
        origin = z - step if up else z + step
        return pltpu.make_async_remote_copy(
            src_ref=own if step == 0 else block(origin, core),
            dst_ref=block(origin, core),
            send_sem=send.at[0 if up else 1, step],
            recv_sem=recv.at[0 if up else 1, step],
            device_id=line.at(z + 1 if up else z - 1, core),
            device_id_type=MESH_IDS,
        )

    def arrival(step, up):
        origin = z - 1 - step if up else z + 1 + step
        return pltpu.make_async_remote_copy(
            src_ref=own,
            dst_ref=block(origin, core),
            send_sem=send.at[0 if up else 1, step],
            recv_sem=recv.at[0 if up else 1, step],
            device_id=line.at(z - 1 if up else z + 1, core),
            device_id_type=MESH_IDS,
        )

    def across(index, origin, source, which):
        return pltpu.make_async_remote_copy(
            src_ref=source,
            dst_ref=block(origin, which),
            send_sem=pair_send.at[index],
            recv_sem=pair_recv.at[index],
            device_id=line.at(z, 1 - core),
            device_id_type=MESH_IDS,
        )

    def sends(step, up):
        return (z >= step) & line.above if up else (z + step <= chips - 1) & line.below

    def comes(step, up):
        return z - 1 - step >= 0 if up else z + 1 + step <= chips - 1

    def pair_of(step, up):
        return 1 + step + (0 if up else chips - 1)

    keep = pltpu.make_async_copy(own, block(z, core), local)
    keep.start()
    for step in range(chips - 1):
        for up in (True, False):
            pl.when(sends(step, up))(lambda step=step, up=up: hop(step, up).start())
        if step == 0:
            across(0, z, own, core).start()
        for up in (True, False):

            def take(step=step, up=up):
                arrival(step, up).wait_recv()
                origin = z - 1 - step if up else z + 1 + step
                across(pair_of(step, up), origin, block(origin, core), core).start()

            pl.when(comes(step, up))(take)
    across(0, z, own, core).wait_send()
    across(0, z, own, 1 - core).wait_recv()
    for step in range(chips - 1):
        for up in (True, False):
            pl.when(sends(step, up))(lambda step=step, up=up: hop(step, up).wait_send())

            def settle(step=step, up=up):
                origin = z - 1 - step if up else z + 1 + step
                across(pair_of(step, up), origin, block(origin, core), core).wait_send()
                across(pair_of(step, up), origin, block(origin, core), 1 - core).wait_recv()

            pl.when(comes(step, up))(settle)
    keep.wait()


def scatter_scratch(chips, rows, width):
    return [
        pltpu.VMEM((chips, rows, width), jnp.bfloat16),
        pltpu.VMEM((2, chips, rows, width), jnp.bfloat16),
        pltpu.SemaphoreType.DMA((chips,)),
        pltpu.SemaphoreType.DMA((chips,)),
        pltpu.SemaphoreType.DMA((2, chips)),
        pltpu.SemaphoreType.DMA((2, chips)),
    ]


def strips(rows, body):
    @pl.loop(0, rows // STRIP)
    def _(index):
        body(pl.ds(pl.multiple_of(index * STRIP, STRIP), STRIP))


def scatter_line(line, part, total, held, come, pair_send, pair_recv, send, recv, aside=None):
    chips, z, core = line.chips, line.z, line.core
    rows = total.shape[0]

    def start_of(chip, which):
        return (2 * chip + which) * rows

    def across(chip):
        return pltpu.make_async_remote_copy(
            src_ref=part.at[pl.ds(start_of(chip, 1 - core), rows)],
            dst_ref=held.at[chip],
            send_sem=pair_send.at[chip],
            recv_sem=pair_recv.at[chip],
            device_id=line.at(z, 1 - core),
            device_id_type=MESH_IDS,
        )

    def hop(chip, up, target):
        way = 0 if up else 1
        return pltpu.make_async_remote_copy(
            src_ref=held.at[chip],
            dst_ref=come.at[way, chip],
            send_sem=send.at[way, chip],
            recv_sem=recv.at[way, chip],
            device_id=line.at(target, core),
            device_id_type=MESH_IDS,
        )

    def value(chip, strip, ways):
        first = start_of(chip, core)
        mine = part[pl.ds(pl.multiple_of(first + strip.start, STRIP), STRIP), :]
        summed = mine.astype(jnp.float32) + held[chip, strip, :].astype(jnp.float32)
        if aside is not None:
            summed = summed + aside[chip, strip, :].astype(jnp.float32)
        for way in ways:
            summed = summed + come[way, chip, strip, :].astype(jnp.float32)
        return summed

    def add(chip, ways):
        def body(strip):
            held[chip, strip, :] = value(chip, strip, ways).astype(jnp.bfloat16)

        strips(rows, body)

    def forward(chip, up):
        across(chip).wait_recv()
        way = 0 if up else 1

        def with_arrival():
            hop(chip, up, z).wait_recv()
            add(chip, (way,))

        more = line.below if up else line.above
        pl.when(more)(with_arrival)
        pl.when(jnp.logical_not(more))(lambda: add(chip, ()))
        hop(chip, up, z + 1 if up else z - 1).start()

    def up_chip(step):
        return chips - 1 - step + z

    def down_chip(step):
        return step - (chips - 1 - z)

    def up_sends(step):
        return (z <= step) & line.above

    def down_sends(step):
        return (step >= chips - 1 - z) & line.below

    def each(act):
        for step in range(chips - 1):
            pl.when(up_sends(step))(lambda step=step: act(up_chip(step), True))
            pl.when(down_sends(step))(lambda step=step: act(down_chip(step), False))

    each(lambda chip, up: across(chip).start())
    across(z).start()
    each(forward)
    across(z).wait_recv()
    pl.when(line.below)(lambda: hop(z, True, z).wait_recv())
    pl.when(line.above)(lambda: hop(z, False, z).wait_recv())

    def last(ways):
        def body(strip):
            total[strip, :] = value(z, strip, ways)

        strips(rows, body)

    inner = line.below & line.above
    pl.when(inner)(lambda: last((0, 1)))
    pl.when(jnp.logical_not(line.below))(lambda: last((1,)))
    pl.when(jnp.logical_not(line.above))(lambda: last((0,)))

    def settle(chip, up):
        across(chip).wait_send()
        hop(chip, up, z + 1 if up else z - 1).wait_send()

    each(settle)
    across(z).wait_send()


def gather_kernel(chips, own, out, *scratch):
    line = Line(chips)
    line.meet()
    gather_line(line, own, out, *scratch)


def middle_kernel(chips, part, hidden, gain, middle, normed_all, total, normed, *scratch):
    line = Line(chips)
    line.meet()
    scatter_line(line, part, total, *scratch[:6])

    def body(strip):
        rows = hidden[strip, :].astype(jnp.float32) + total[strip, :]
        middle[strip, :] = rows
        normed[strip, :] = (rows * rms_scale(rows) * gain[...]).astype(jnp.bfloat16)

    strips(hidden.shape[0], body)
    gather_line(line, normed, normed_all, *scratch[6:])


def branch_kernel(
    chips, part, aside, middle, gain, out_grad, probs, collect, router,
    grad_middle, grad_all, heads, term, total, turned, *scratch
):
    line = Line(chips)
    line.meet()
    scatter_line(line, part, total, *scratch[:6], aside=aside)
    width = middle.shape[1]
    term[...] = jnp.zeros_like(term)

    def body(strip):
        tail = jnp.dot(
            total[strip, width:].astype(jnp.bfloat16), collect[...],
            preferred_element_type=jnp.float32,
        )
        prob = probs[strip, :]
        lane = lax.broadcasted_iota(jnp.int32, prob.shape, 1)
        inner = jnp.sum(jnp.where(lane > 0, prob * tail, 0.0), axis=1, keepdims=True)
        head = jnp.where(lane > 0, prob * (tail - inner), tail * prob * (1.0 - prob))
        head = head.astype(jnp.bfloat16)
        heads[strip, :] = head
        grad = total[strip, :width] + jnp.dot(
            head, router[...], preferred_element_type=jnp.float32
        )
        rows = middle[strip, :]
        scale = rms_scale(rows)
        weighted = grad * gain[...]
        mean = jnp.mean(weighted * rows, axis=-1, keepdims=True)
        term[...] += jnp.sum(grad * rows * scale, axis=0, keepdims=True)
        result = (
            out_grad[strip, :].astype(jnp.float32)
            + scale * weighted
            - rows * scale * scale * scale * mean
        )
        grad_middle[strip, :] = result
        turned[strip, :] = result.astype(jnp.bfloat16)

    strips(middle.shape[0], body)
    gather_line(line, turned, grad_all, *scratch[6:])


def input_kernel(chips, part, hidden, gain, grad_middle, input_grad, term, total, *scratch):
    line = Line(chips)
    line.meet()
    scatter_line(line, part, total, *scratch)
    term[...] = jnp.zeros_like(term)

    def body(strip):
        grad = total[strip, :]
        rows = hidden[strip, :].astype(jnp.float32)
        scale = rms_scale(rows)
        weighted = grad * gain[...]
        mean = jnp.mean(weighted * rows, axis=-1, keepdims=True)
        term[...] += jnp.sum(grad * rows * scale, axis=0, keepdims=True)
        result = (
            grad_middle[strip, :] + scale * weighted - rows * scale * scale * scale * mean
        )
        input_grad[strip, :] = result.astype(jnp.bfloat16)

    strips(hidden.shape[0], body)


UNIT_STRIP = 16


def nt_dot(left, right):
    return lax.dot_general(
        left, right, (((1,), (1,)), ((), ())), preferred_element_type=jnp.float32
    )


def experts_kernel(experts, top, split, near, place, normed, grads, side, router, down, *rest):
    if near:
        routed, routed_came, shared, shared_came = rest[:4]
        hidden, grad_up, heads, dots, weight, up, back, scale, sums = rest[4:]
    else:
        weight, hidden, grad_up, heads, dots, up, back, scale, sums = rest
    step = pl.program_id(0)
    above, me = place[0], place[1]
    rows = normed.shape[0]
    units = down.shape[1]
    width = down.shape[2]
    chunk = min(256, rows)

    @pl.when(step == 0)
    def _():
        logits = nt_dot(router[...], normed[...])
        row = lax.broadcasted_iota(jnp.int32, logits.shape, 0)
        opener = jax.nn.sigmoid(logits)
        choice = jnp.where((row >= 1) & (row <= experts), logits, NEG_FILL)
        peak = jnp.max(choice, axis=0, keepdims=True)
        total = peak + jnp.log(jnp.sum(jnp.exp(choice - peak), axis=0, keepdims=True))
        probs = jnp.exp(choice - total)
        heads[...] = jnp.where(row == 0, opener, probs)
        names = side[...].astype(jnp.float32)
        lane = lax.broadcasted_iota(jnp.int32, names.shape, 1)
        match = jnp.where(
            (lane < top) & (names == me.astype(jnp.float32)), 1.0, 0.0
        ).astype(jnp.bfloat16)
        named = nt_dot(jnp.ones((16, names.shape[1]), jnp.bfloat16), match)[0:1]
        own = jnp.sum(jnp.where(row == me + 1, probs, 0.0), axis=0, keepdims=True)
        scale[0:1, :] = named * own
        scale[1:2, :] = opener[0:1]
        scale[2:3, :] = named
        sums[...] = jnp.zeros_like(sums)

    if near:
        first = pl.multiple_of(above * (width // 2), 128)
        second = pl.multiple_of((1 - above) * (width // 2), 128)
        cut = routed.shape[2]
        for kind in range(2):
            weight[kind, 0, :cut, pl.ds(first, width // 2)] = routed[kind, 0]
            weight[kind, 0, :cut, pl.ds(second, width // 2)] = routed_came[kind, 0]
            weight[kind, 0, cut:, pl.ds(first, width // 2)] = shared[kind, 0]
            weight[kind, 0, cut:, pl.ds(second, width // 2)] = shared_came[kind, 0]

    @pl.loop(0, rows // chunk)
    def _(index):
        span = pl.ds(pl.multiple_of(index * chunk, chunk), chunk)
        for kind in range(2):
            up[kind, :, span] = nt_dot(weight[kind, 0], normed[span, :])
        back[:, span] = nt_dot(down[0], grads[span, :])

    def part(first, last, which):
        @pl.loop(first // UNIT_STRIP, last // UNIT_STRIP)
        def _(index):
            strip = pl.ds(pl.multiple_of(index * UNIT_STRIP, UNIT_STRIP), UNIT_STRIP)
            gate = up[0, strip, :]
            value = up[1, strip, :]
            grad = back[strip, :]
            sigmoid = jax.nn.sigmoid(gate)
            act = gate * sigmoid
            unit = (act * value).astype(jnp.bfloat16)
            wide = unit.astype(jnp.float32)
            factor = scale[which : which + 1, :]
            hidden[0, strip, :] = (wide * factor).astype(jnp.bfloat16)
            product = wide * grad
            sums[which, :, :] += product[:8] + product[8:]
            grad = grad * factor
            slope = grad * value * sigmoid * (1.0 + gate * (1.0 - sigmoid))
            grad_up[0, 0, strip, :] = slope.astype(jnp.bfloat16)
            grad_up[1, 0, strip, :] = (grad * act).astype(jnp.bfloat16)

    part(0, split, 0)
    part(split, units, 1)

    @pl.when(step == pl.num_programs(0) - 1)
    def _():
        routed_dot = scale[2:3, :] * jnp.sum(sums[0], axis=0, keepdims=True)
        shared_dot = jnp.sum(sums[1], axis=0, keepdims=True)
        row = lax.broadcasted_iota(jnp.int32, (16, rows), 0)
        both = jnp.where(row < 2, shared_dot, routed_dot)
        high = both.astype(jnp.bfloat16).astype(jnp.float32)
        value = jnp.where((row == 0) | (row == 2), high, both - high)
        dots[...] = jnp.where(row < 4, value, 0.0).astype(jnp.bfloat16)


def experts_call(place, normed, grads, side, router, down, weights, experts, top, split):
    rows, width = normed.shape
    steps, units = down.shape[:2]
    near = len(weights) == 4

    def whole(shape):
        return pl.BlockSpec(
            shape, lambda i, place: (0,) * len(shape), pipeline_mode=pl.Buffered(1)
        )

    def piece(array):
        return pl.BlockSpec(
            (2, 1) + array.shape[2:],
            lambda i, place: (0, place[0] + i - 2 * place[0] * i, 0, 0),
        )

    full = pl.BlockSpec((2, 1, units, width), lambda i, place: (0, i, 0, 0))
    outs = [
        jax.ShapeDtypeStruct((steps, units, rows), jnp.bfloat16),
        jax.ShapeDtypeStruct((2, steps, units, rows), jnp.bfloat16),
        jax.ShapeDtypeStruct((16, rows), jnp.float32),
        jax.ShapeDtypeStruct((16, rows), jnp.bfloat16),
    ]
    out_specs = [
        pl.BlockSpec((1, units, rows), lambda i, place: (i, 0, 0)),
        pl.BlockSpec((2, 1, units, rows), lambda i, place: (0, i, 0, 0)),
        pl.BlockSpec((16, rows), lambda i, place: (0, 0)),
        pl.BlockSpec((16, rows), lambda i, place: (0, 0)),
    ]
    if near:
        outs.append(jax.ShapeDtypeStruct((2, steps, units, width), jnp.bfloat16))
        out_specs.append(full)
    return pl.pallas_call(
        functools.partial(experts_kernel, experts, top, split, near),
        out_shape=outs,
        grid_spec=pltpu.PrefetchScalarGridSpec(
            num_scalar_prefetch=1,
            grid=(steps,),
            in_specs=[
                whole(normed.shape),
                whole(grads.shape),
                whole(side.shape),
                whole(router.shape),
                pl.BlockSpec((1, units, width), lambda i, place: (i, 0, 0)),
            ]
            + ([piece(array) for array in weights] if near else [full]),
            out_specs=out_specs,
            scratch_shapes=[
                pltpu.VMEM((2, units, rows), jnp.float32),
                pltpu.VMEM((units, rows), jnp.float32),
                pltpu.VMEM((8, rows), jnp.float32),
                pltpu.VMEM((2, 8, rows), jnp.float32),
            ],
        ),
        cost_estimate=pl.CostEstimate(
            flops=int(4e9), bytes_accessed=int(1e6), transcendentals=0
        ),
    )(place, normed, grads, side, router, down, *weights)


def weight_grad_kernel(place, left, right, *rest):
    *plus, out = rest
    total = jnp.dot(left[...], right[...], preferred_element_type=jnp.float32)
    if plus:
        total = total + plus[0][...].astype(jnp.float32)
    out[...] = total.astype(jnp.bfloat16)


def weight_grad(column, left, right, plus=None):
    count, rows = left.shape
    width = right.shape[1] // 2
    tile = count // 6
    tiled = pl.BlockSpec((tile, width), lambda i, column: (i, 0))
    return pl.pallas_call(
        weight_grad_kernel,
        out_shape=jax.ShapeDtypeStruct((count, width), jnp.bfloat16),
        grid_spec=pltpu.PrefetchScalarGridSpec(
            num_scalar_prefetch=1,
            grid=(6,),
            in_specs=[
                pl.BlockSpec((tile, rows), lambda i, column: (i, 0)),
                pl.BlockSpec((rows, width), lambda i, column: (0, column[0])),
            ]
            + ([tiled] if plus is not None else []),
            out_specs=tiled,
        ),
        cost_estimate=pl.CostEstimate(
            flops=int(3e9), bytes_accessed=int(1e6), transcendentals=0
        ),
    )(column, left, right, *([plus] if plus is not None else []))


def remote_call(kernel, chips, inputs, outputs, scratch, number, micros):
    moved = sum(a.size * a.dtype.itemsize for a in inputs)
    return pl.pallas_call(
        functools.partial(kernel, chips),
        out_shape=[jax.ShapeDtypeStruct(shape, kind) for shape, kind, _ in outputs],
        in_specs=[pl.BlockSpec(memory_space=pltpu.VMEM)] * len(inputs),
        out_specs=[
            pl.BlockSpec(memory_space=pl.ANY if far else pltpu.VMEM) for _, _, far in outputs
        ],
        scratch_shapes=scratch,
        compiler_params=pltpu.CompilerParams(collective_id=number, has_side_effects=True),
        cost_estimate=pl.CostEstimate(
            flops=int(micros * 1e9), bytes_accessed=moved, transcendentals=0
        ),
    )(*inputs)


def bf16(values):
    return values.astype(jnp.bfloat16)


def two_parts(values):
    high = lax.reduce_precision(values, exponent_bits=8, mantissa_bits=7)
    return (bf16(high), bf16(values - high))


def mm(left, right):
    return jnp.dot(left, right, preferred_element_type=jnp.float32)


def mm_nt(left, right):
    return lax.dot_general(
        left, right, (((1,), (1,)), ((), ())), preferred_element_type=jnp.float32
    )


def mm_tn(left, right):
    return lax.dot_general(
        left, right, (((0,), (0,)), ((), ())), preferred_element_type=jnp.float32
    )


def group_device(
    hidden_in,
    out_grad,
    lengths,
    routes,
    norm1_gain,
    qkv_weight,
    qkv_bias,
    out_weight,
    norm2_gain,
    router_weight,
    shared_gate,
    shared_in,
    shared_out,
    expert_in,
    expert_out,
):
    size = lax.axis_size("expert")
    parts = lax.axis_size("dp")
    me = lax.axis_index("expert")
    core = me % 2
    rows, width = hidden_in.shape
    group = rows * size
    heads = width // HD
    own_heads = heads // size
    half = parts // 2
    places = size // 2
    block = width // (parts * size)
    top = routes.shape[1]
    experts = router_weight.shape[1]
    score_scale = HD ** (-0.5)
    bias_cols = 3 * width // (parts * size) // block
    extra = 128
    shared_block = shared_out.shape[0]
    expert_block = expert_out.shape[1]
    pair_block = expert_block + shared_block
    hidden_units = half * pair_block
    own_shared = parts * shared_block
    chips = places
    data = lax.axis_index("dp")
    side_by = data % 2
    above = data // 2
    slots = 2 * size
    slot = side_by * size + me
    swap = [(i, i ^ 1) for i in range(size)]
    swap_side = [(g, g ^ 1) for g in range(parts)]
    swap_above = [(g, g ^ 2) for g in range(parts)]
    own_qkv = 3 * own_heads * HD

    def by_head(columns):
        count = columns.shape[0]
        cut = columns.reshape(count, 3, 2, half, places, HD)
        return cut.transpose(4, 2, 0, 1, 3, 5).reshape(size, count, own_qkv)

    def from_head(pieces):
        count = pieces.shape[1]
        cut = pieces.reshape(places, 2, count, 3, half, HD)
        return cut.transpose(2, 3, 1, 4, 0, 5).reshape(count, 3 * width)

    def ordered(which, own, other, axis):
        first = jnp.where(which == 0, own, other)
        second = jnp.where(which == 0, other, own)
        return jnp.concatenate([first, second], axis=axis)

    def by_core(values, which):
        blocks = values.reshape(chips, 2, rows, values.shape[1])
        blocks = lax.dynamic_index_in_dim(blocks, which, 1, keepdims=False)
        return blocks.reshape(chips * rows, values.shape[1])

    def beside(values):
        came = lax.ppermute(by_core(values, core), "dp", swap_side)
        return jnp.concatenate([came, lax.ppermute(came, "expert", swap)], axis=0)

    def rows_of(values, first):
        return lax.dynamic_slice_in_dim(values, first * rows, rows, 0)

    down = jnp.concatenate([expert_out[0], shared_out], axis=0)
    down_came = lax.ppermute(down, "dp", swap_above)

    def units(values, count):
        cut = values.reshape(size * block, 2, half, 2, count)
        return cut.transpose(3, 1, 2, 4, 0).reshape(2, 2 * half * count, size * block)

    def aside(values):
        kept = lax.dynamic_index_in_dim(values, side_by, 0, keepdims=False)
        given = lax.dynamic_index_in_dim(values, 1 - side_by, 0, keepdims=False)
        return kept, lax.ppermute(given, "dp", swap_side)

    routed_kept, routed_came = aside(units(expert_in[0], expert_block))

    small = jnp.concatenate(
        [
            norm1_gain[:, None],
            norm2_gain[:, None],
            shared_gate[:, None],
            router_weight,
            qkv_bias.reshape(block, bias_cols),
        ],
        axis=1,
    )
    small = jnp.pad(small, ((0, 0), (0, extra - small.shape[1])))
    first = jnp.concatenate(
        [by_head(qkv_weight), jnp.broadcast_to(small[None], (size, block, extra))], axis=2
    )
    first = lax.all_to_all(first, "expert", split_axis=0, concat_axis=0, tiled=True)
    first = first.reshape(size * block, own_qkv + extra)
    out_cols = width * block // (size * block)
    qkv_full = lax.all_gather(
        jnp.concatenate([first, out_weight.reshape(size * block, out_cols)], axis=1),
        "dp",
        axis=0,
        tiled=True,
    )

    segment, position = segment_table(lengths[0], group)
    valid_all = (segment < lengths.shape[1] - 1).astype(jnp.float32)[:, None]
    valid_rows = rows_of(valid_all, me)
    grad_own = bf16(out_grad.astype(jnp.float32) * valid_rows)
    side = jnp.pad(bf16(routes), ((0, 0), (0, extra - top)))
    cut = shared_in.reshape(block, 2, parts, size, shared_block)
    cut = cut.transpose(3, 0, 1, 2, 4).reshape(size, block, 2 * own_shared)
    cut, first = lax.optimization_barrier((cut, first))
    cut = lax.all_to_all(cut, "expert", split_axis=0, concat_axis=0, tiled=True)

    near = jnp.concatenate([hidden_in, side], axis=1)
    near, first = lax.optimization_barrier((near, first))
    (gathered,) = remote_call(
        gather_kernel,
        chips,
        [near],
        [((group, width + extra), jnp.bfloat16, True)],
        gather_scratch(chips),
        0,
        40,
    )
    near_grad, qkv_full = lax.optimization_barrier((grad_own, qkv_full))
    near_grad = lax.all_gather(near_grad, "expert", axis=0, tiled=True)

    cut, gathered = lax.optimization_barrier((cut, gathered))
    shared_kept, shared_came = aside(units(cut.reshape(size * block, 2 * own_shared), shared_block))
    hidden_all = gathered[:, :width].astype(jnp.float32)
    near_side = gathered[:, width:]
    far_side = beside(near_side)
    routed_came, qkv_full = lax.optimization_barrier((routed_came, qkv_full))
    routed_up = ordered(side_by, routed_kept, routed_came, 1)
    routed_came = lax.ppermute(routed_up, "dp", swap_above)

    weight_qkv = qkv_full[:, :own_qkv]
    small = qkv_full[:, own_qkv : own_qkv + extra]
    gain_one = small[:, 0].astype(jnp.float32)
    gain_two = small[:, 1].astype(jnp.float32)
    router_rows = jnp.pad(small[:, 2 : 3 + experts].T, ((0, 127 - experts), (0, 0)))
    bias_all = by_head(small[:, 3 + experts : 3 + experts + bias_cols].reshape(1, 3 * width))
    bias_own = lax.dynamic_index_in_dim(bias_all, me, 0, keepdims=False).astype(jnp.float32)

    def own_half(values):
        return lax.dynamic_slice_in_dim(values, core * half, half, 0)

    def other_half(values):
        return lax.dynamic_slice_in_dim(values, (1 - core) * half, half, 0)

    out_blocks = qkv_full[:, own_qkv + extra :].reshape(parts, block, width)
    kept = own_half(out_blocks)
    came = lax.ppermute(other_half(out_blocks), "expert", swap)
    weight_out = jnp.stack(
        [jnp.where(core == 0, kept, came), jnp.where(core == 0, came, kept)], axis=1
    ).reshape(own_heads * HD, width)

    cosine, sine = rotary_tables(position, HD)
    allowed = (
        (segment[:, None] == segment[None, :]) & (position[:, None] >= position[None, :])
    )[None]
    normed_one = bf16(hidden_all * rms_scale(hidden_all) * gain_one)
    projected = mm(normed_one, weight_qkv) + bias_own
    split = projected.reshape(group, 3, own_heads, HD)
    query_low = bf16(rotate(split[:, 0], cosine, sine))
    key_low = bf16(rotate(split[:, 1], cosine, sine))
    value_low = bf16(split[:, 2])

    def score_rows():
        raw = (
            jnp.einsum("qhd,khd->hqk", query_low, key_low, preferred_element_type=jnp.float32)
            * score_scale
        )
        return jnp.where(allowed, raw, NEG_FILL)

    scores = score_rows()
    peak = jnp.max(scores, axis=-1, keepdims=True)
    log_total = peak + jnp.log(jnp.sum(jnp.exp(scores - peak), axis=-1, keepdims=True))
    weights_low = bf16(jnp.exp(scores - log_total))
    attended = bf16(
        jnp.einsum(
            "hqk,khd->qhd", weights_low, value_low, preferred_element_type=jnp.float32
        ).reshape(group, own_heads * HD)
    )
    part = bf16(mm(attended, weight_out))
    far_grad = by_core(near_grad, core)
    part, far_grad, shared_came = lax.optimization_barrier((part, far_grad, shared_came))
    far_grad = lax.ppermute(far_grad, "dp", swap_side)
    shared_up = ordered(side_by, shared_kept, shared_came, 1)
    shared_came = lax.ppermute(shared_up, "dp", swap_above)
    part, routed_up, shared_up = lax.optimization_barrier((part, routed_up, shared_up))
    middle, normed = remote_call(
        middle_kernel,
        chips,
        [part, hidden_in, gain_two[None, :]],
        [((rows, width), jnp.float32, False), ((group, width), jnp.bfloat16, True)],
        [pltpu.VMEM((rows, width), jnp.float32), pltpu.VMEM((rows, width), jnp.bfloat16)]
        + scatter_scratch(chips, rows, width)
        + gather_scratch(chips),
        1,
        75,
    )
    far_normed = beside(normed)
    far_grad = jnp.concatenate([far_grad, lax.ppermute(far_grad, "expert", swap)], axis=0)
    normed, routed_came, shared_came, down_came = lax.optimization_barrier(
        (normed, routed_came, shared_came, down_came)
    )
    weight_down = jnp.stack([down, down_came])
    place = jnp.stack([above, me]).astype(jnp.int32)
    cell = jnp.arange(16, dtype=jnp.int32)[:, None]
    spot = bf16((cell < 4) & (jnp.arange(extra)[None, :] == cell * slots + slot))
    router_few = router_rows[:16]
    near_hidden, near_up, near_heads, near_dots, weight_up = experts_call(
        place,
        normed,
        near_grad,
        near_side,
        router_few,
        weight_down,
        [
            piece.reshape(2, half, piece.shape[0] // 4, width // 2)
            for piece in (routed_up, routed_came, shared_up, shared_came)
        ],
        experts,
        top,
        expert_block,
    )
    column = place[:1]
    near_up = near_up.reshape(2 * hidden_units, group)
    near_hidden = near_hidden.reshape(hidden_units, group)
    flat_up = weight_up.reshape(2 * hidden_units, width)
    flat_down = weight_down.reshape(hidden_units, width)
    near_sent = weight_grad(1 - column, near_up, normed)
    part = jnp.concatenate([bf16(mm_tn(near_up, flat_up)), bf16(mm_tn(near_dots, spot))], axis=1)
    near_output = bf16(mm_tn(near_hidden, flat_down))
    far_normed, far_grad, near_sent, part, near_output = lax.optimization_barrier(
        (far_normed, far_grad, near_sent, part, near_output)
    )
    far_hidden, far_up, _, far_dots = experts_call(
        place,
        far_normed,
        far_grad,
        far_side,
        router_few,
        weight_down,
        [weight_up],
        experts,
        top,
        expert_block,
    )
    far_up = far_up.reshape(2 * hidden_units, group)
    far_hidden = far_hidden.reshape(hidden_units, group)

    def pair_sum(values):
        came = lax.ppermute(values[group // 2 :], "expert", swap)
        return bf16(values[: group // 2].astype(jnp.float32) + came.astype(jnp.float32))

    far_part = jnp.concatenate(
        [bf16(mm_tn(far_up, flat_up)), bf16(mm_tn(far_dots, spot))], axis=1
    )
    far_sum = pair_sum(far_part)
    sent_up = weight_grad(1 - column, far_up, far_normed, near_sent)
    far_sum, sent_up, far_hidden, near_hidden, near_up, far_up = lax.optimization_barrier(
        (far_sum, sent_up, far_hidden, near_hidden, near_up, far_up)
    )
    aside_part = lax.ppermute(far_sum, "dp", swap_side)
    came_up = lax.ppermute(sent_up, "dp", swap_above)
    far_output = pair_sum(bf16(mm_tn(far_hidden, flat_down)))
    far_came = lax.ppermute(far_output, "dp", swap_side)
    sent_down = bf16(mm(near_hidden[pair_block:], near_grad) + mm(far_hidden[pair_block:], far_grad))
    came_down = lax.ppermute(sent_down, "dp", swap_above)
    term_up = weight_grad(column, far_up, far_normed, weight_grad(column, near_up, normed))
    term_down = mm(near_hidden[:pair_block], near_grad) + mm(far_hidden[:pair_block], far_grad)

    rider = jnp.arange(extra, dtype=jnp.int32)[:, None]
    lane = jnp.arange(128, dtype=jnp.int32)[None, :]
    collect = bf16(
        ((rider < 2 * slots) & (lane == 0))
        | ((rider >= 2 * slots) & (rider < 4 * slots) & (lane == 1 + rider % size))
    )
    probs = lax.dynamic_slice_in_dim(near_heads, me * rows, rows, 1).T
    probs = jnp.pad(probs, ((0, 0), (0, 128 - probs.shape[1])))
    part, aside_part, term_up, term_down, sent_down, far_output = lax.optimization_barrier(
        (part, aside_part, term_up, term_down, sent_down, far_output)
    )
    grad_middle, grad_branch, grad_heads, term_norm_two = remote_call(
        branch_kernel,
        chips,
        [
            part,
            aside_part.reshape(chips, rows, width + extra),
            middle,
            gain_two[None, :],
            grad_own,
            probs,
            collect,
            router_rows,
        ],
        [
            ((rows, width), jnp.float32, False),
            ((group, width), jnp.bfloat16, True),
            ((rows, 128), jnp.bfloat16, False),
            ((1, width), jnp.float32, False),
        ],
        [
            pltpu.VMEM((rows, width + extra), jnp.float32),
            pltpu.VMEM((rows, width), jnp.bfloat16),
        ]
        + scatter_scratch(chips, rows, width + extra)
        + gather_scratch(chips),
        2,
        80,
    )
    grad_branch, came_up, far_came = lax.optimization_barrier((grad_branch, came_up, far_came))
    term_router = mm_tn(rows_of(normed, me), grad_heads)[:, : 1 + experts]

    which = (jnp.arange(2) == core)[None, :, None, None]
    combined = near_output.reshape(chips, 2, rows, width).astype(jnp.float32)
    combined = combined + jnp.where(
        which, far_came.reshape(chips, 1, rows, width).astype(jnp.float32), 0.0
    )
    summed_part = bf16(combined).reshape(group, width)

    shape = (2, half, pair_block, width // 2)
    up = term_up.reshape(shape).astype(jnp.float32) + came_up.reshape(shape)[:, ::-1].astype(
        jnp.float32
    )
    up = bf16(up).reshape(2 * hidden_units, width // 2)
    quarter = width // 4
    side_kept = lax.dynamic_slice_in_dim(up, side_by * quarter, quarter, 1)
    side_given = lax.dynamic_slice_in_dim(up, (1 - side_by) * quarter, quarter, 1)
    grad_branch, side_given, summed_part = lax.optimization_barrier(
        (grad_branch, side_given, summed_part)
    )
    summed = lax.psum_scatter(summed_part, "expert", scatter_dimension=0, tiled=True)
    side_came = lax.ppermute(side_given, "dp", swap_side)

    grad_attended = bf16(mm_nt(grad_branch, weight_out)).reshape(group, own_heads, HD)
    weights_again = jnp.exp(score_rows() - log_total)
    grad_weights = jnp.einsum(
        "qhd,khd->hqk", grad_attended, value_low, preferred_element_type=jnp.float32
    )
    delta_rows = jnp.sum(weights_again * grad_weights, axis=-1, keepdims=True)
    grad_scores = bf16(weights_again * (grad_weights - delta_rows))
    grad_query_turned = (
        jnp.einsum("hqk,khd->qhd", grad_scores, key_low, preferred_element_type=jnp.float32)
        * score_scale
    )
    grad_key_turned = (
        jnp.einsum("hqk,qhd->khd", grad_scores, query_low, preferred_element_type=jnp.float32)
        * score_scale
    )
    grad_values = jnp.einsum(
        "hqk,qhd->khd", bf16(weights_again), grad_attended, preferred_element_type=jnp.float32
    )
    grad_projected = bf16(
        jnp.stack(
            [
                rotate_back(grad_query_turned, cosine, sine),
                rotate_back(grad_key_turned, cosine, sine),
                grad_values,
            ],
            axis=1,
        ).reshape(group, own_qkv)
    )
    part = bf16(mm_nt(grad_projected, weight_qkv))
    term_out = bf16(mm_tn(attended, grad_branch)).reshape(half, 2, block, width)
    kept = jnp.where(core == 0, term_out[:, 0], term_out[:, 1])
    given = jnp.where(core == 0, term_out[:, 1], term_out[:, 0])
    came = lax.ppermute(given, "expert", swap)
    out_blocks = jnp.concatenate(
        [jnp.where(core == 0, kept, came), jnp.where(core == 0, came, kept)], axis=0
    )
    back = jnp.concatenate(
        [bf16(mm_tn(normed_one, grad_projected)), out_blocks.reshape(width, out_cols)], axis=1
    )
    part, back, summed = lax.optimization_barrier((part, back, summed))
    back = lax.psum_scatter(back, "dp", scatter_dimension=0, tiled=True)
    grad_out_weight = back[:, own_qkv:].reshape(block, width).astype(jnp.float32)
    input_grad, term_norm_one = remote_call(
        input_kernel,
        chips,
        [part, hidden_in, gain_one[None, :], grad_middle],
        [((rows, width), jnp.bfloat16, False), ((1, width), jnp.float32, False)],
        [pltpu.VMEM((rows, width), jnp.float32)] + scatter_scratch(chips, rows, width),
        3,
        40,
    )
    grad_down = term_down + came_down.astype(jnp.float32)
    grad_shared_out = grad_down[expert_block:]
    grad_expert_out = grad_down[None, :expert_block]
    up = ordered(side_by, side_kept[None], side_came[None], 0)
    up = up.reshape(2, 2, half, pair_block, quarter)
    up = ordered(above, up[:, :, :1], up[:, :, 1:], 2)
    grad_expert_in = (
        up[:, :, :, :expert_block]
        .transpose(4, 1, 2, 0, 3)
        .reshape(1, quarter, 2 * parts * expert_block)
        .astype(jnp.float32)
    )
    cut = lax.all_to_all(
        up[:, :, :, expert_block:].transpose(4, 1, 2, 0, 3).reshape(size, block, 2 * own_shared),
        "expert",
        split_axis=0,
        concat_axis=0,
        tiled=True,
    )
    grad_shared_in = (
        cut.reshape(size, block, 2, parts, shared_block)
        .transpose(1, 2, 3, 0, 4)
        .reshape(block, 2 * parts * size * shared_block)
        .astype(jnp.float32)
    )
    back = lax.all_to_all(
        back[:, :own_qkv].reshape(size, block, own_qkv),
        "expert",
        split_axis=0,
        concat_axis=0,
        tiled=True,
    )
    grad_qkv = from_head(back).astype(jnp.float32)

    term_bias = jnp.sum(grad_projected.astype(jnp.float32), axis=0)
    bias_slots = jnp.where(jnp.arange(size)[:, None] == me, term_bias[None, :], 0.0)
    bias_rows = from_head(bias_slots[:, None, :]).reshape(width, bias_cols)
    small_terms = jnp.concatenate(
        [term_norm_one[0][:, None], term_norm_two[0][:, None], term_router, bias_rows], axis=1
    )
    count = small_terms.shape[1]
    small_terms = lax.all_to_all(
        small_terms.T.reshape(count, parts * size, block).transpose(1, 0, 2),
        ("dp", "expert"),
        split_axis=0,
        concat_axis=0,
        tiled=True,
    )
    small_sum = jnp.sum(small_terms, axis=0)
    output = bf16(valid_rows * (middle + summed.astype(jnp.float32)))
    grad_norm1 = small_sum[0]
    grad_norm2 = small_sum[1]
    grad_shared_gate = small_sum[2]
    grad_router = small_sum[3 : 3 + experts].T
    grad_bias = small_sum[3 + experts :].T.reshape(block * bias_cols)
    return (
        output,
        input_grad,
        grad_norm1,
        grad_qkv,
        grad_bias,
        grad_out_weight,
        grad_norm2,
        grad_router,
        grad_shared_gate,
        grad_shared_in,
        grad_shared_out,
        grad_expert_in,
        grad_expert_out,
    )


def solution(mesh):
    size, parts = mesh.shape["expert"], mesh.shape["dp"]

    def device(*arrays):
        block = arrays[5].shape[0]
        whole_heads = 2 * block == HD and parts == 4 and size % 2 == 0
        one_expert = arrays[13].shape[0] == 1
        if whole_heads and one_expert and arrays[5].shape[1] % (3 * size * HD) == 0:
            return group_device(*arrays)
        return per_device(*arrays)

    return jax.shard_map(
        device,
        mesh=mesh,
        in_specs=(
            P(("dp", "expert"), None),
            P(("dp", "expert"), None),
            P("dp", None),
            P(("dp", "expert"), None),
            P(("dp", "expert")),
            P(("dp", "expert"), None),
            P(("dp", "expert")),
            P(("dp", "expert"), None),
            P(("dp", "expert")),
            P(("dp", "expert"), None),
            P(("dp", "expert")),
            P(("dp", "expert"), None),
            P(("dp", "expert"), None),
            P("expert", "dp", None),
            P("expert", "dp", None),
        ),
        out_specs=(
            P(("dp", "expert"), None),
            P(("dp", "expert"), None),
            P(("dp", "expert")),
            P(("dp", "expert"), None),
            P(("dp", "expert")),
            P(("dp", "expert"), None),
            P(("dp", "expert")),
            P(("dp", "expert"), None),
            P(("dp", "expert")),
            P(("dp", "expert"), None),
            P(("dp", "expert"), None),
            P("expert", "dp", None),
            P("expert", "dp", None),
        ),
        check_vma=False,
    )
```
